256 devices in a mesh: band: 16 (over y, x), lev: 16 (over z, core).
Axes of the slice: x: 4, y: 4, z: 8, core: 2. Of those that a mesh axis runs over, the one named last changes fastest.
Arguments:
- adj_spec: bfloat16 [64, 1280, 2, 1280], P('lev', 'band'), may hold values from -6 to 6
- wave_of_slot: int32 [1280], replicated, may hold values from 0 to 1279, each once
- legendre: bfloat16 [1280, 32, 1280], P('band'), may hold values from -0.15625 to 0.15625
- lat_weight: float32 [32], replicated, may hold values from 0.5 to 1.5
- traj: bfloat16 [64, 64, 5136], P('lev', 'band'), may hold values from -3 to 3
- traj_exp: int32 [64, 64, 4], P('lev', 'band'), may hold values from -2 to 2
- traj_order: int32 [16, 4], P('lev'), may hold values from 0 to 3, each once within a row
- lev_coef: float32 [64], P('lev'), may hold values from 0.02 to 0.2
Outputs:
- adj_out: bfloat16 [64, 1280, 2, 1280], P('lev', 'band')
The draws below stay inside these ranges and needn't reach their ends.
Inputs may be any that keep to these rules, and one draw needn't show every extreme that they name: `wave_of_slot`: every wavenumber 0 to 1279 is held by exactly one slot. `traj_order`: each row is a permutation of 0 to 3.
All inputs are finite; a program needn't handle non-finite values.
Results may differ from the reference program's by a relative error of at most 0.0085.
Values may be sent and summed in bfloat16 or wider, within the bound.
No kernel may reach another device: no remote copies, remote signals or barrier semaphores. Data moves between devices by JAX's collectives and lax.ppermute only.
A program may use at most 128 MiB of HBM per device.

```python
import math
import jax
import jax.numpy as jnp
from jax import lax

M = 1280
NLON = 5136
NBLK = 4
LEV_DEV = 4
NLAT = 64
NH = 32
NLEV = 64
N_LEV = 16


def touch_ends(values, key, smallest, largest):
    longest = values.shape.index(max(values.shape))
    spots = []
    for shift in (0, 1):
        where = [jax.random.randint(jax.random.fold_in(key, axis), (), 0, length) for axis, length in enumerate(values.shape)]
        where[longest] = (where[longest] + shift) % values.shape[longest]
        spots.append(tuple(where))
    return values.at[spots[0]].set(smallest).at[spots[1]].set(largest)


def levels(stream_key, shape, shards, smallest, top_value):
    loudness = 1.0
    for position, blocks in shards:
        steps = jax.random.uniform(jax.random.fold_in(jax.random.fold_in(stream_key, 6), position), (blocks,), jnp.float32, smallest / len(shards), top_value / len(shards))
        loudness = loudness * jnp.repeat(jnp.exp(steps), shape[position] // blocks).reshape((-1,) + (1,) * (len(shape) - 1 - position))
    return loudness


def noise(own_key, extent, width, bound, cuts=(), held_as=jnp.bfloat16):
    values = jax.random.normal(own_key, extent, jnp.float32) * width
    if len(cuts) > 0:
        values = levels(own_key, extent, cuts, -0.22, 0.18) * values
    return jnp.clip(values, min=-bound, max=bound).astype(held_as)


def setup_inputs(seed: int = 0) -> dict:
    key_list = jax.random.split(jax.random.key(seed), 9)
    adj_spec = noise(key_list[0], (NLEV, M, 2, M), 1.0, 6.0, ((0, 16), (1, 16)))
    wave_of_slot = jax.random.permutation(key_list[1], M).astype(jnp.int32)
    legendre = noise(key_list[2], (M, NH, M), M ** -0.5, 0.15625, ((0, 16),))
    lat_weight = jnp.clip(jax.random.uniform(key_list[3], (NH,), jnp.float32, 0.5, 1.5), 0.5, 1.5)
    traj = noise(key_list[4], (NLEV, NLAT, NLON), 0.5, 3.0, ((0, 16), (1, 16)))
    traj_exp = touch_ends(jax.random.randint(key_list[5], (NLEV, NLAT, NBLK), -2, 3), jax.random.fold_in(key_list[5], 1), -2, 2).astype(jnp.int32)
    traj_order = jax.vmap(lambda own: jax.random.permutation(own, LEV_DEV))(jax.random.split(key_list[6], N_LEV)).reshape((N_LEV, LEV_DEV)).astype(jnp.int32)
    lev_coef = jnp.clip(jnp.exp(math.log(0.2) - 2.3025851 * jax.random.uniform(key_list[7], (NLEV,), jnp.float32) ** levels(key_list[7], (NLEV,), ((0, 16),), -0.2, 0.2)), 0.02, 0.2)
    return {"adj_spec": adj_spec, "wave_of_slot": wave_of_slot, "legendre": legendre, "lat_weight": lat_weight, "traj": traj, "traj_exp": traj_exp, "traj_order": traj_order, "lev_coef": lev_coef}


def trig_block(wave_ids, lon_start, block_width, lon_count):
    lon_ids = lon_start + jnp.arange(block_width, dtype=jnp.int32)
    phase_int = wave_ids.astype(jnp.int32)[:, None] * lon_ids[None, :] % lon_count
    angle_rad = phase_int.astype(jnp.float32) * (2.0 * math.pi / lon_count)
    return jnp.stack([jnp.cos(angle_rad), -jnp.sin(angle_rad)], axis=1).astype(jnp.bfloat16)

def reference(adj_spec, wave_of_slot, legendre, lat_weight, traj, traj_exp, traj_order, lev_coef):
    highest = lax.Precision.HIGHEST
    degree_ids = jnp.arange(M, dtype=jnp.int32)
    valid_mask = degree_ids[None, :] < (M - wave_of_slot.astype(jnp.int32))[:, None]
    masked = jnp.where(valid_mask[None, :, None, :], adj_spec, jnp.zeros_like(adj_spec))
    parity_sign = jnp.where(degree_ids % 2 == 0, 1.0, -1.0).astype(jnp.float32)
    table_full = legendre.astype(jnp.float32)
    weight_q = jnp.repeat(lat_weight, 2)

    def synthesis(level_data):
        values = level_data.astype(jnp.float32)
        stacked = jnp.stack([values, values * parity_sign], axis=2)
        side_values = jnp.einsum('scej,shj->sche', stacked, table_full, precision=highest)
        return (side_values.reshape(M, 2, NLAT) * weight_q).astype(jnp.bfloat16)
    fourier = lax.map(synthesis, masked).astype(jnp.float32)
    block_width = NLON // NBLK
    norm_scale = 1.0 / math.sqrt(M)
    stored = traj.astype(jnp.float32).reshape(N_LEV, LEV_DEV, NLAT, NLON)
    select = (traj_order[:, None, :] == jnp.arange(LEV_DEV, dtype=jnp.int32)[None, :, None]).astype(jnp.float32)
    level_coef = lev_coef[:, None, None]
    analysis = jnp.zeros((NLEV, M, 2, NLAT), jnp.float32)
    for block_id in range(NBLK):
        lon_start = block_id * block_width
        trig_table = trig_block(wave_of_slot, lon_start, block_width, NLON).astype(jnp.float32)
        grid_block = jnp.einsum('lscq,scw->lqw', fourier, trig_table, precision=highest) * norm_scale
        running = jnp.cumsum(grid_block, axis=0)
        above_sum = jnp.concatenate([jnp.zeros_like(grid_block[:1]), running[:-1]], axis=0)
        exponent = jnp.exp2(traj_exp[:, :, block_id].astype(jnp.float32)).reshape(N_LEV, LEV_DEV, NLAT)
        traj_piece = stored[..., lon_start:lon_start + block_width] * exponent[..., None]
        traj_value = jnp.einsum('gir,grqw->giqw', select, traj_piece, precision=highest).reshape(NLEV, NLAT, block_width)
        forcing = ((1.0 + jnp.tanh(traj_value)) * (grid_block + level_coef * above_sum)).astype(jnp.bfloat16).astype(jnp.float32)
        analysis = analysis + jnp.einsum('lqw,scw->lscq', forcing, trig_table, precision=highest) * norm_scale
    halves = analysis.reshape(NLEV, M, 2, NH, 2)
    sym_part = (halves[..., 0] + halves[..., 1]).astype(jnp.bfloat16)
    anti_part = (halves[..., 0] - halves[..., 1]).astype(jnp.bfloat16)

    def analysis_level(level_pair):
        from_sym = jnp.einsum('sch,shj->scj', level_pair[0].astype(jnp.float32), table_full, precision=highest)
        from_anti = jnp.einsum('sch,shj->scj', level_pair[1].astype(jnp.float32), table_full, precision=highest)
        return jnp.where(degree_ids % 2 == 0, from_sym, from_anti)
    result = lax.map(analysis_level, (sym_part, anti_part))
    return jnp.where(valid_mask[None, :, None, :], result, 0.0).astype(jnp.bfloat16)
```

```python
import math

import jax
import jax.numpy as jnp
from jax import lax
from jax.sharding import PartitionSpec as P

NBLK = 4
LO = 32


def angles(wave_ids, lon_ids, lon_count):
    phase = lon_ids[:, None] * wave_ids[None, :] % lon_count
    angle = phase.astype(jnp.float32) * (2.0 * math.pi / lon_count)
    return jnp.cos(angle), jnp.sin(angle)


def quarter_table(wave_ids, width, lon_count):
    steps = -(-width // LO)
    low = angles(wave_ids, jnp.arange(LO, dtype=jnp.int32), lon_count)
    high = angles(wave_ids, jnp.arange(steps, dtype=jnp.int32) * LO, lon_count)
    cos_low, sin_low, cos_high, sin_high = lax.optimization_barrier((*low, *high))
    cos_high, sin_high = cos_high[:, None], sin_high[:, None]
    cos_all = cos_high * cos_low - sin_high * sin_low
    sin_all = sin_high * cos_low + cos_high * sin_low
    flat = (steps * LO, wave_ids.shape[0])
    cos_all = cos_all.astype(jnp.bfloat16).reshape(flat)
    sin_all = (-sin_all).astype(jnp.bfloat16).reshape(flat)
    return lax.optimization_barrier((cos_all[:width], sin_all[:width]))


def scan_levels(total):
    size, axis = 16, "lev"
    running = total
    step = 1
    while step < size:
        moved = lax.ppermute(
            running.astype(jnp.bfloat16), axis, [(i, i + step) for i in range(size - step)]
        )
        running = running + moved.astype(jnp.float32)
        step *= 2
    return lax.ppermute(
        running.astype(jnp.bfloat16), axis, [(i, i + 1) for i in range(size - 1)]
    ).astype(jnp.float32)


def body(adj_spec, wave_of_slot, legendre, lat_weight, traj, traj_exp, traj_order, lev_coef):
    bf16, f32 = jnp.bfloat16, jnp.float32
    highest = lax.Precision.HIGHEST
    levels, slots, _, degrees = adj_spec.shape
    lat_rows, lon_count = traj.shape[1:]
    width = lon_count // NBLK
    norm_scale = 1.0 / math.sqrt(degrees)
    waves_here = lax.dynamic_slice_in_dim(wave_of_slot, lax.axis_index("band") * slots, slots)
    degree_ids = jnp.arange(degrees, dtype=jnp.int32)
    valid = degree_ids[None, :] < (degrees - waves_here)[:, None]
    masked = jnp.where(valid[None, :, None, :], adj_spec, jnp.zeros_like(adj_spec))
    sign = jnp.where(degree_ids % 2 == 0, 1.0, -1.0).astype(bf16)
    stacked = jnp.stack([masked, masked * sign], axis=3)
    side = jnp.einsum("lscej,shj->lsche", stacked, legendre, preferred_element_type=f32)
    weight_q = jnp.repeat(lat_weight, 2)
    fourier = (side.reshape(levels, slots, 2, -1) * weight_q).astype(bf16)
    fourier = lax.all_to_all(fourier, "band", split_axis=3, concat_axis=1, tiled=True)
    total = jnp.sum(fourier.astype(f32), axis=0)
    carry = scan_levels(total)

    cos_t, sin_t = quarter_table(wave_of_slot, width, lon_count)
    turn = jnp.arange(NBLK, dtype=jnp.int32)[:, None] * wave_of_slot[None, :] % 4
    cos_b = jnp.where(turn == 0, 1.0, jnp.where(turn == 2, -1.0, 0.0))
    sin_b = jnp.where(turn == 1, 1.0, jnp.where(turn == 3, -1.0, 0.0))

    def to_grid(rows):
        first, second = rows[:, None, :, 0], rows[:, None, :, 1]
        first, second = jnp.moveaxis(first, 2, 3), jnp.moveaxis(second, 2, 3)
        cb, sb = cos_b[None, :, None, :], sin_b[None, :, None, :]
        with_cos = (first * cb - second * sb).astype(bf16)
        with_sin = (first * sb + second * cb).astype(bf16)
        out = jnp.einsum("lbqs,ks->lbqk", with_cos, cos_t, preferred_element_type=f32)
        out = out + jnp.einsum("lbqs,ks->lbqk", with_sin, sin_t, preferred_element_type=f32)
        return out * norm_scale

    grid = to_grid(fourier.astype(f32))
    group = to_grid(carry[None])
    running = jnp.cumsum(grid, axis=0)
    above = jnp.concatenate([jnp.zeros_like(grid[:1]), running[:-1]], axis=0) + group

    order = jnp.arange(levels, dtype=jnp.int32)
    select = (traj_order[0][None, :] == order[:, None]).astype(f32)
    scaled = traj.astype(f32).reshape(levels, lat_rows, NBLK, width)
    scaled = scaled * jnp.exp2(traj_exp.astype(f32))[..., None]
    ordered = jnp.einsum("ir,rqbk->ibqk", select, scaled, precision=highest)
    forcing = (1.0 + jnp.tanh(ordered)) * (grid + lev_coef[:, None, None, None] * above)
    forcing = forcing.astype(bf16)

    by_cos = jnp.einsum("lbqk,ks->lbqs", forcing, cos_t, preferred_element_type=f32)
    by_sin = jnp.einsum("lbqk,ks->lbqs", forcing, sin_t, preferred_element_type=f32)
    cb, sb = cos_b[None, :, None, :], sin_b[None, :, None, :]
    first = jnp.sum(by_cos * cb + by_sin * sb, axis=1) * norm_scale
    second = jnp.sum(by_sin * cb - by_cos * sb, axis=1) * norm_scale
    analysis = jnp.stack([first, second], axis=1)
    halves = analysis.reshape(levels, 2, lat_rows // 2, 2, -1)
    sym = halves[:, :, :, 0] + halves[:, :, :, 1]
    anti = halves[:, :, :, 0] - halves[:, :, :, 1]
    sides = jnp.stack([sym, anti], axis=2).astype(bf16)
    sides = lax.all_to_all(sides, "band", split_axis=4, concat_axis=3, tiled=True)
    both = jnp.einsum("lcehs,shj->lsecj", sides, legendre, preferred_element_type=f32)
    result = jnp.where(degree_ids % 2 == 0, both[:, :, 0], both[:, :, 1])
    return jnp.where(valid[None, :, None, :], result, 0.0).astype(bf16)


def solution(mesh):
    return jax.shard_map(
        body,
        mesh=mesh,
        in_specs=(
            P("lev", "band", None, None),
            P(),
            P("band", None, None),
            P(),
            P("lev", "band", None),
            P("lev", "band", None),
            P("lev", None),
            P("lev"),
        ),
        out_specs=P("lev", "band", None, None),
        check_vma=False,
    )
```

```python
import functools
import math

import jax
import jax.numpy as jnp
from jax import lax
from jax.experimental import pallas as pl
from jax.experimental.pallas import tpu as pltpu
from jax.sharding import PartitionSpec as P

F32, BF16, I32 = jnp.float32, jnp.bfloat16, jnp.int32
GROUP = 8


def iota(shape, dim):
    return lax.broadcasted_iota(I32, shape, dim)


def matmul(a, b, ca, cb):
    return lax.dot_general(a, b, (((ca,), (cb,)), ((), ())), preferred_element_type=F32)


def one_hot(rows, cols):
    return jnp.where(rows == cols, 1.0, 0.0).astype(BF16)


def synthesis_kernel(limit_ref, weight_ref, adj_ref, leg_ref, out_ref, acc_ref):
    step = pl.program_id(0)
    levels, groups_slots, comps, degrees = adj_ref.shape
    rows = GROUP * comps
    heights = leg_ref.shape[1]
    for part in range(groups_slots // GROUP):
        here = pl.ds(part * GROUP, GROUP)
        limit = limit_ref[pl.ds(part * rows, rows), :]
        degree = iota((rows, degrees), 1)
        inside = degree < limit
        even = jnp.where(inside & (degree % 2 == 0), 1.0, 0.0).astype(BF16)
        odd = jnp.where(inside & (degree % 2 == 1), 1.0, 0.0).astype(BF16)
        values = [adj_ref[l, here].reshape(rows, degrees) for l in range(levels)]
        left = jnp.concatenate([v * even for v in values] + [v * odd for v in values], axis=0)
        table = leg_ref[here].reshape(GROUP * heights, degrees)
        both = matmul(left, table, 1, 1)
        shape = both.shape
        own = (iota(shape, 0) % rows) // comps == iota(shape, 1) // heights
        both = jnp.where(own, both, 0.0)
        both = both[:, :128] + both[:, 128:]
        both = both + pltpu.roll(both, 64, 1)
        both = both + pltpu.roll(both, 32, 1)
        half = levels * rows
        from_even, from_odd = both[:half], both[half:]
        north = (from_even + from_odd) * weight_ref[...]
        south = (from_even - from_odd) * weight_ref[...]
        at = step * (groups_slots // GROUP) + part
        for l in range(levels):
            acc_ref[l, pl.ds(at * rows, rows), :] = north[l * rows : (l + 1) * rows]
            acc_ref[levels + l, pl.ds(at * rows, rows), :] = south[l * rows : (l + 1) * rows]

    @pl.when(step == pl.num_programs(0) - 1)
    def _():
        total = acc_ref.shape[1]
        slots = total // comps
        sides = 2 * levels
        lane = iota((total, 128), 1) // heights
        blocks = []
        for k in range(sides // 4):
            mix = acc_ref[4 * k]
            for r in range(1, 4):
                mix = jnp.where(lane == r, acc_ref[4 * k + r], mix)
            blocks.append(mix.astype(BF16))
        wide = jnp.concatenate(blocks, axis=1)
        col = iota((total, 2 * 128), 1)
        source = iota((total, 2 * 128), 0)
        comp, slot = col // 128, col % 128
        spread = jnp.where((source == slot * comps + comp) & (slot < slots), 1.0, 0.0).astype(BF16)
        turned = matmul(wide, spread, 0, 0).astype(BF16)
        size = sides * heights
        dest = iota((size, size), 0)
        origin = iota((size, size), 1)
        band, e, hh, l = dest // 16, dest // 8 % 2, dest // 4 % 2, dest % 4
        wanted = (e * levels + l) * heights + band * 2 + hh
        moved = matmul(one_hot(wanted, origin), turned, 1, 0).astype(BF16)
        for d in range(size // 16):
            for c in range(comps):
                out_ref[d, c] = moved[16 * d : 16 * d + 16, 128 * c : 128 * c + slots]


def synthesis(adj, leg, limit, weight):
    levels, slots, comps, degrees = adj.shape
    heights = leg.shape[1]
    wide = 16
    steps = slots // wide
    limit = jnp.repeat(limit, comps)[:, None]
    weight = jnp.tile(weight, 128 // heights)[None, :]
    return pl.pallas_call(
        synthesis_kernel,
        grid=(steps,),
        in_specs=[
            pl.BlockSpec((wide * comps, 1), lambda i: (i, 0)),
            pl.BlockSpec((1, 128), lambda i: (0, 0)),
            pl.BlockSpec((levels, wide, comps, degrees), lambda i: (0, i, 0, 0)),
            pl.BlockSpec((wide, heights, degrees), lambda i: (i, 0, 0)),
        ],
        out_specs=pl.BlockSpec((16, comps, 16, slots), lambda i: (0, 0, 0, 0)),
        out_shape=jax.ShapeDtypeStruct((16, comps, 16, slots), BF16),
        scratch_shapes=[pltpu.VMEM((2 * levels, slots * comps, 128), F32)],
        compiler_params=pltpu.CompilerParams(vmem_limit_bytes=40 * 2**20),
        name="synthesis",
    )(limit, weight, adj, leg)


def analysis_kernel(limit_ref, in_ref, leg_ref, out_ref, left_ref):
    step = pl.program_id(0)
    levels, wide, comps, degrees = out_ref.shape
    heights = leg_ref.shape[1]
    sources, _, sub, slots = in_ref.shape
    rows = GROUP * comps
    kinds = 2 * levels

    @pl.when(step == 0)
    def _():
        size = sources * sub
        row = iota((size, kinds * 128), 0)
        col = iota((size, kinds * 128), 1)
        row_key = (row // 8 % 2 * levels + row % 4) * heights + row // 16 * 2 + row // 4 % 2
        pick = one_hot(row_key, col // 128 * heights + col % heights)
        parts = []
        for c in range(comps):
            flat = jnp.concatenate([in_ref[d, c] for d in range(sources)], axis=0)
            parts.append(matmul(flat, pick, 0, 0).astype(BF16))
        apart = jnp.concatenate(parts, axis=0)
        total = slots * comps
        row = iota((total, total), 0)
        col = iota((total, total), 1)
        weave = one_hot(row % comps * slots + row // comps, col)
        left_ref[...] = matmul(weave, apart, 1, 0).astype(BF16)

    for part in range(wide // GROUP):
        at = step * (wide // GROUP) + part
        here = left_ref[pl.ds(pl.multiple_of(at * rows, rows), rows), :]
        stack = jnp.concatenate([here[:, 128 * k : 128 * k + 128] for k in range(kinds)], axis=0)
        left = jnp.concatenate([stack, stack], axis=1)
        shape = left.shape
        own = (iota(shape, 0) % rows) // comps == iota(shape, 1) // heights
        left = left * jnp.where(own, 1.0, 0.0).astype(BF16)
        table = leg_ref[pl.ds(part * GROUP, GROUP)].reshape(GROUP * heights, degrees)
        both = matmul(left, table, 1, 0)
        limit = limit_ref[pl.ds(part * rows, rows), :]
        degree = iota((rows, degrees), 1)
        inside = degree < limit
        even = degree % 2 == 0
        half = levels * rows
        for l in range(levels):
            sym = both[l * rows : (l + 1) * rows]
            anti = both[half + l * rows : half + (l + 1) * rows]
            value = jnp.where(inside, jnp.where(even, sym, anti), 0.0).astype(BF16)
            out_ref[l, pl.ds(part * GROUP, GROUP)] = value.reshape(GROUP, comps, degrees)


def analysis(sides, leg, limit, levels):
    sources, comps, sub, slots = sides.shape
    heights, degrees = leg.shape[1:]
    wide = 16
    limit = jnp.repeat(limit, comps)[:, None]
    return pl.pallas_call(
        analysis_kernel,
        grid=(slots // wide,),
        in_specs=[
            pl.BlockSpec((wide * comps, 1), lambda i: (i, 0)),
            pl.BlockSpec(sides.shape, lambda i: (0, 0, 0, 0)),
            pl.BlockSpec((wide, heights, degrees), lambda i: (i, 0, 0)),
        ],
        out_specs=pl.BlockSpec((levels, wide, comps, degrees), lambda i: (0, i, 0, 0)),
        out_shape=jax.ShapeDtypeStruct((levels, slots, comps, degrees), BF16),
        scratch_shapes=[pltpu.VMEM((slots * comps, 2 * levels * 128), BF16)],
        compiler_params=pltpu.CompilerParams(vmem_limit_bytes=40 * 2**20),
        name="analysis",
    )(limit, sides, leg)

NBLK = 4


def turns(wave, b):
    turn = (wave * b) & 3
    cos_b = jnp.where(turn == 0, 1.0, jnp.where(turn == 2, -1.0, 0.0))
    sin_b = jnp.where(turn == 1, 1.0, jnp.where(turn == 3, -1.0, 0.0))
    return cos_b, sin_b


def table_kernel(cos_low_ref, sin_low_ref, cos_high_ref, sin_high_ref, cos_ref, sin_ref):
    low = cos_low_ref.shape[0]

    @pl.loop(0, cos_high_ref.shape[0])
    def _(i):
        cos_high = cos_high_ref[pl.ds(i, 1), :]
        sin_high = sin_high_ref[pl.ds(i, 1), :]
        cos_low, sin_low = cos_low_ref[...], sin_low_ref[...]
        at = pl.ds(pl.multiple_of(i * low, low), low)
        cos_ref[at, :] = (cos_high * cos_low - sin_high * sin_low).astype(BF16)
        sin_ref[at, :] = (-(sin_high * cos_low + cos_high * sin_low)).astype(BF16)


def angles(wave_ids, lon_ids, lon_count):
    phase = lon_ids[:, None] * wave_ids[None, :] % lon_count
    angle = phase.astype(F32) * (2.0 * math.pi / lon_count)
    return jnp.cos(angle), jnp.sin(angle)


def quarter_table(wave_ids, width, lon_count):
    low_count = 16
    steps = -(-width // low_count)
    low = angles(wave_ids, jnp.arange(low_count, dtype=I32), lon_count)
    high = angles(wave_ids, jnp.arange(steps, dtype=I32) * low_count, lon_count)
    shape = jax.ShapeDtypeStruct((steps * low_count, wave_ids.shape[0]), BF16)
    return pl.pallas_call(
        table_kernel,
        out_shape=(shape, shape),
        compiler_params=pltpu.CompilerParams(vmem_limit_bytes=24 * 2**20),
        cost_estimate=pl.CostEstimate(flops=12_000_000, bytes_accessed=8_000_000, transcendentals=0),
        name="trig_table",
    )(*low, *high)


def gather_kernel(in_ref, out_ref, total_ref):
    sources, comps, sub, slots = in_ref.shape
    rows = iota((8, comps * sub), 0)
    cols = iota((8, comps * sub), 1)
    pick = one_hot(cols // 4, rows)
    flat = []
    for c in range(comps):
        flat.append(jnp.concatenate([in_ref[d, c] for d in range(sources)], axis=1))
        out_ref[c] = flat[-1]
    total_ref[...] = matmul(pick, jnp.concatenate(flat, axis=0), 1, 0).astype(BF16)


def gather_rows(blocks):
    sources, comps, sub, slots = blocks.shape
    return pl.pallas_call(
        gather_kernel,
        out_shape=(
            jax.ShapeDtypeStruct((comps, sub, sources * slots), BF16),
            jax.ShapeDtypeStruct((comps * sub // 4, sources * slots), BF16),
        ),
        name="gather_rows",
    )(blocks)


def to_longitudes(first, second, wave, cos_ref, sin_ref):
    with_cos, with_sin = [], []
    for b in range(NBLK):
        cos_b, sin_b = (v.astype(BF16) for v in turns(wave, b))
        with_cos.append(first * cos_b - second * sin_b)
        with_sin.append(first * sin_b + second * cos_b)
    with_cos = jnp.concatenate(with_cos, axis=0)
    with_sin = jnp.concatenate(with_sin, axis=0)
    return matmul(with_cos, cos_ref[...], 1, 1) + matmul(with_sin, sin_ref[...], 1, 1)


def grid_kernel(four_ref, wave_ref, coef_ref, scale_ref, pick_ref, traj_ref, cos_ref, sin_ref, sum_ref, gain_ref, *, width, norm):
    grid = to_longitudes(four_ref[0], four_ref[1], wave_ref[...], cos_ref, sin_ref)
    level = iota(grid.shape, 0) % 4
    prior = jnp.where(level >= 1, pltpu.roll(grid, 1, 0), 0.0)
    prior = prior + jnp.where(level >= 2, pltpu.roll(grid, 2, 0), 0.0)
    prior = prior + jnp.where(level >= 3, pltpu.roll(grid, 3, 0), 0.0)
    sum_ref[...] = grid + coef_ref[...] * prior
    levels, lats, lons = traj_ref.shape
    stored = jnp.concatenate([traj_ref[r] for r in range(levels)], axis=0)
    ordered = matmul(pick_ref[...], stored, 1, 0)
    sub = levels * lats
    full = cos_ref.shape[0]
    for b in range(NBLK):
        piece = ordered[:, b * width : (b + 1) * width] * scale_ref[b * sub : (b + 1) * sub, :]
        gain = norm * (1.0 + jnp.tanh(piece))
        gain_ref[b * sub : (b + 1) * sub, :] = jnp.concatenate(
            [gain, jnp.zeros((sub, full - width), F32)], axis=1
        )


def grid_part(four, wave, coef, scale, pick, traj, cos_t, sin_t, width, norm):
    shape = jax.ShapeDtypeStruct((NBLK * four.shape[1], cos_t.shape[0]), F32)
    return pl.pallas_call(
        functools.partial(grid_kernel, width=width, norm=norm),
        out_shape=(shape, shape),
        compiler_params=pltpu.CompilerParams(vmem_limit_bytes=40 * 2**20),
        cost_estimate=pl.CostEstimate(flops=450_000_000, bytes_accessed=8_000_000, transcendentals=100_000),
        name="grid_part",
    )(four, wave, coef, scale, pick, traj, cos_t, sin_t)


def forcing_kernel(index_ref, total_ref, wave_ref, coef_ref, sum_ref, gain_ref, cos_ref, sin_ref, out_ref, *, norm):
    me = index_ref[0]
    groups, rows, waves = total_ref.shape
    carry = jnp.zeros((rows, waves), F32)
    for g in range(groups):
        carry = carry + jnp.where(g < me, total_ref[g].astype(F32), 0.0)
    sub = 16
    copies = one_hot(iota((2 * sub, rows), 0) // 4, iota((2 * sub, rows), 1))
    spread = matmul(copies, carry.astype(BF16), 1, 0).astype(BF16)
    wave = wave_ref[...]
    group = to_longitudes(spread[:sub], spread[sub:], wave, cos_ref, sin_ref)
    forcing = (gain_ref[...] * (sum_ref[...] + coef_ref[...] * group)).astype(BF16)
    by_cos = matmul(forcing, cos_ref[...], 1, 0)
    by_sin = matmul(forcing, sin_ref[...], 1, 0)
    first = jnp.zeros((sub, waves), F32)
    second = jnp.zeros((sub, waves), F32)
    for b in range(NBLK):
        cos_b, sin_b = turns(wave, b)
        part_cos, part_sin = by_cos[b * sub : (b + 1) * sub], by_sin[b * sub : (b + 1) * sub]
        first = first + part_cos * cos_b + part_sin * sin_b
        second = second + part_sin * cos_b - part_cos * sin_b
    bands, comps, _, slots = out_ref.shape
    half = sub // 2
    for c, value in enumerate((first, second)):
        value = value * norm
        sym, anti = value[:half] + value[half:], value[:half] - value[half:]
        sides = jnp.concatenate([sym, anti], axis=0).astype(BF16)
        for d in range(bands):
            out_ref[d, c] = sides[:, slots * d : slots * (d + 1)]


def forcing_part(index, totals, wave, coef, sums, gain, cos_t, sin_t, shape, norm):
    vmem = pl.BlockSpec(memory_space=pltpu.VMEM)
    return pl.pallas_call(
        functools.partial(forcing_kernel, norm=norm),
        in_specs=[pl.BlockSpec(memory_space=pltpu.SMEM)] + [vmem] * 7,
        out_specs=vmem,
        out_shape=jax.ShapeDtypeStruct(shape, BF16),
        compiler_params=pltpu.CompilerParams(vmem_limit_bytes=40 * 2**20),
        cost_estimate=pl.CostEstimate(flops=900_000_000, bytes_accessed=8_000_000, transcendentals=0),
        name="forcing_part",
    )(index, totals, wave, coef, sums, gain, cos_t, sin_t)


def body(adj_spec, wave_of_slot, legendre, lat_weight, traj, traj_exp, traj_order, lev_coef):
    levels, slots, _, degrees = adj_spec.shape
    lats, lon_count = traj.shape[1:]
    width = lon_count // NBLK
    norm = 1.0 / math.sqrt(degrees)
    waves_here = lax.dynamic_slice_in_dim(wave_of_slot, lax.axis_index("band") * slots, slots)
    limit = degrees - waves_here
    blocks = synthesis(adj_spec, legendre, limit, lat_weight)
    blocks = lax.all_to_all(blocks, "band", split_axis=0, concat_axis=0, tiled=True)
    cos_t, sin_t = quarter_table(wave_of_slot, width, lon_count)
    four, total = gather_rows(blocks)
    totals = lax.all_gather(total, "lev")

    wave = wave_of_slot[None, :]
    row = jnp.arange(NBLK * lats * levels, dtype=I32)
    blk, side, pair, level = row // 16, row // 8 % 2, row // 4 % 2, row % 4
    stored = jnp.argmax(traj_order[0][None, :] == jnp.arange(levels, dtype=I32)[:, None], axis=1)
    stored_row = stored[level]
    lat = 2 * pair + side
    scale = jnp.exp2(traj_exp[stored_row, lat, blk].astype(F32))[:, None]
    coef = lev_coef[level][:, None]
    source = (stored_row * lats + lat)[:16]
    pick = (source[:, None] == jnp.arange(16, dtype=I32)[None, :]).astype(BF16)
    sums, gain = grid_part(four, wave, coef, scale, pick, traj, cos_t, sin_t, width, norm)
    index = lax.axis_index("lev").astype(I32)[None]
    sides = forcing_part(index, totals, wave, coef, sums, gain, cos_t, sin_t, blocks.shape, norm)
    sides = lax.all_to_all(sides, "band", split_axis=0, concat_axis=0, tiled=True)
    return analysis(sides, legendre, limit, levels)


def solution(mesh):
    return jax.shard_map(
        body,
        mesh=mesh,
        in_specs=(
            P("lev", "band", None, None),
            P(),
            P("band", None, None),
            P(),
            P("lev", "band", None),
            P("lev", "band", None),
            P("lev", None),
            P("lev"),
        ),
        out_specs=P("lev", "band", None, None),
        check_vma=False,
    )
```

```python
import functools
import math

import jax
import jax.numpy as jnp
from jax import lax
from jax.experimental import pallas as pl
from jax.experimental.pallas import tpu as pltpu
from jax.sharding import PartitionSpec as P

F32, BF16, I32 = jnp.float32, jnp.bfloat16, jnp.int32
GROUP = 8


def iota(shape, dim):
    return lax.broadcasted_iota(I32, shape, dim)


def matmul(a, b, ca, cb):
    return lax.dot_general(a, b, (((ca,), (cb,)), ((), ())), preferred_element_type=F32)


def one_hot(rows, cols):
    return jnp.where(rows == cols, 1.0, 0.0).astype(BF16)


def limits(band_ref, wave_ref, at, slots, comps, degrees):
    rows = GROUP * comps
    slot = iota((rows, 1), 0) // comps
    first = band_ref[0] * slots + at * GROUP
    limit = jnp.zeros((rows, 1), I32)
    for s in range(GROUP):
        limit = jnp.where(slot == s, degrees - wave_ref[first + s], limit)
    return limit


def synthesis_kernel(band_ref, wave_ref, weight_ref, adj_ref, leg_ref, out_ref, acc_ref):
    step = pl.program_id(0)
    levels, groups_slots, comps, degrees = adj_ref.shape
    rows = GROUP * comps
    heights = leg_ref.shape[1]
    weight = jnp.concatenate([weight_ref[...]] * (128 // heights), axis=1)
    for part in range(groups_slots // GROUP):
        here = pl.ds(part * GROUP, GROUP)
        at = step * (groups_slots // GROUP) + part
        limit = limits(band_ref, wave_ref, at, acc_ref.shape[1] // comps, comps, degrees)
        degree = iota((rows, degrees), 1)
        inside = degree < limit
        even = jnp.where(inside & (degree % 2 == 0), 1.0, 0.0).astype(BF16)
        odd = jnp.where(inside & (degree % 2 == 1), 1.0, 0.0).astype(BF16)
        values = [adj_ref[l, here].reshape(rows, degrees) for l in range(levels)]
        left = jnp.concatenate([v * even for v in values] + [v * odd for v in values], axis=0)
        table = leg_ref[here].reshape(GROUP * heights, degrees)
        both = matmul(left, table, 1, 1)
        shape = both.shape
        own = (iota(shape, 0) % rows) // comps == iota(shape, 1) // heights
        both = jnp.where(own, both, 0.0)
        both = both[:, :128] + both[:, 128:]
        both = both + pltpu.roll(both, 64, 1)
        both = both + pltpu.roll(both, 32, 1)
        half = levels * rows
        from_even, from_odd = both[:half], both[half:]
        north = (from_even + from_odd) * weight
        south = (from_even - from_odd) * weight
        for l in range(levels):
            acc_ref[l, pl.ds(at * rows, rows), :] = north[l * rows : (l + 1) * rows]
            acc_ref[levels + l, pl.ds(at * rows, rows), :] = south[l * rows : (l + 1) * rows]

    @pl.when(step == pl.num_programs(0) - 1)
    def _():
        total = acc_ref.shape[1]
        slots = total // comps
        sides = 2 * levels
        lane = iota((total, 128), 1) // heights
        blocks = []
        for k in range(sides // 4):
            mix = acc_ref[4 * k]
            for r in range(1, 4):
                mix = jnp.where(lane == r, acc_ref[4 * k + r], mix)
            blocks.append(mix.astype(BF16))
        wide = jnp.concatenate(blocks, axis=1)
        col = iota((total, 2 * 128), 1)
        source = iota((total, 2 * 128), 0)
        comp, slot = col // 128, col % 128
        spread = jnp.where((source == slot * comps + comp) & (slot < slots), 1.0, 0.0).astype(BF16)
        turned = matmul(wide, spread, 0, 0).astype(BF16)
        size = sides * heights
        dest = iota((size, size), 0)
        origin = iota((size, size), 1)
        band, e, hh, l = dest // 16, dest // 8 % 2, dest // 4 % 2, dest % 4
        wanted = (e * levels + l) * heights + band * 2 + hh
        moved = matmul(one_hot(wanted, origin), turned, 1, 0).astype(BF16)
        for d in range(size // 16):
            for c in range(comps):
                out_ref[d, c] = moved[16 * d : 16 * d + 16, 128 * c : 128 * c + slots]


def synthesis(adj, leg, band, waves, weight):
    levels, slots, comps, degrees = adj.shape
    heights = leg.shape[1]
    wide = 16
    steps = slots // wide
    return pl.pallas_call(
        synthesis_kernel,
        grid=(steps,),
        in_specs=[
            pl.BlockSpec(memory_space=pltpu.SMEM),
            pl.BlockSpec(memory_space=pltpu.SMEM),
            pl.BlockSpec((1, heights), lambda i: (0, 0)),
            pl.BlockSpec((levels, wide, comps, degrees), lambda i: (0, i, 0, 0)),
            pl.BlockSpec((wide, heights, degrees), lambda i: (i, 0, 0)),
        ],
        out_specs=pl.BlockSpec((16, comps, 16, slots), lambda i: (0, 0, 0, 0)),
        out_shape=jax.ShapeDtypeStruct((16, comps, 16, slots), BF16),
        scratch_shapes=[pltpu.VMEM((2 * levels, slots * comps, 128), F32)],
        compiler_params=pltpu.CompilerParams(vmem_limit_bytes=60 * 2**20),
        name="synthesis",
    )(band, waves, weight[None, :], adj, leg)


def analysis_kernel(band_ref, wave_ref, in_ref, leg_ref, out_ref, left_ref):
    step = pl.program_id(0)
    levels, wide, comps, degrees = out_ref.shape
    heights = leg_ref.shape[1]
    sources, _, sub, slots = in_ref.shape
    rows = GROUP * comps
    kinds = 2 * levels

    @pl.when(step == 0)
    def _():
        size = sources * sub
        row = iota((size, kinds * 128), 0)
        col = iota((size, kinds * 128), 1)
        row_key = (row // 8 % 2 * levels + row % 4) * heights + row // 16 * 2 + row // 4 % 2
        pick = one_hot(row_key, col // 128 * heights + col % heights)
        parts = []
        for c in range(comps):
            flat = jnp.concatenate([in_ref[d, c] for d in range(sources)], axis=0)
            parts.append(matmul(flat, pick, 0, 0).astype(BF16))
        apart = jnp.concatenate(parts, axis=0)
        total = slots * comps
        row = iota((total, total), 0)
        col = iota((total, total), 1)
        weave = one_hot(row % comps * slots + row // comps, col)
        left_ref[...] = matmul(weave, apart, 1, 0).astype(BF16)

    for part in range(wide // GROUP):
        at = step * (wide // GROUP) + part
        here = left_ref[pl.ds(pl.multiple_of(at * rows, rows), rows), :]
        stack = jnp.concatenate([here[:, 128 * k : 128 * k + 128] for k in range(kinds)], axis=0)
        left = jnp.concatenate([stack, stack], axis=1)
        shape = left.shape
        own = (iota(shape, 0) % rows) // comps == iota(shape, 1) // heights
        left = left * jnp.where(own, 1.0, 0.0).astype(BF16)
        table = leg_ref[pl.ds(part * GROUP, GROUP)].reshape(GROUP * heights, degrees)
        both = matmul(left, table, 1, 0)
        limit = limits(band_ref, wave_ref, at, slots, comps, degrees)
        degree = iota((rows, degrees), 1)
        inside = degree < limit
        even = degree % 2 == 0
        half = levels * rows
        for l in range(levels):
            sym = both[l * rows : (l + 1) * rows]
            anti = both[half + l * rows : half + (l + 1) * rows]
            value = jnp.where(inside, jnp.where(even, sym, anti), 0.0).astype(BF16)
            out_ref[l, pl.ds(part * GROUP, GROUP)] = value.reshape(GROUP, comps, degrees)


def analysis(sides, leg, band, waves, levels):
    sources, comps, sub, slots = sides.shape
    heights, degrees = leg.shape[1:]
    wide = 16
    return pl.pallas_call(
        analysis_kernel,
        grid=(slots // wide,),
        in_specs=[
            pl.BlockSpec(memory_space=pltpu.SMEM),
            pl.BlockSpec(memory_space=pltpu.SMEM),
            pl.BlockSpec(sides.shape, lambda i: (0, 0, 0, 0)),
            pl.BlockSpec((wide, heights, degrees), lambda i: (i, 0, 0)),
        ],
        out_specs=pl.BlockSpec((levels, wide, comps, degrees), lambda i: (0, i, 0, 0)),
        out_shape=jax.ShapeDtypeStruct((levels, slots, comps, degrees), BF16),
        scratch_shapes=[pltpu.VMEM((slots * comps, 2 * levels * 128), BF16)],
        compiler_params=pltpu.CompilerParams(vmem_limit_bytes=60 * 2**20),
        name="analysis",
    )(band, waves, sides, leg)

NBLK = 4
LOW = 16


def turns(wave, b):
    turn = (wave * b) & 3
    cos_b = jnp.where(turn == 0, 1.0, jnp.where(turn == 2, -1.0, 0.0))
    sin_b = jnp.where(turn == 1, 1.0, jnp.where(turn == 3, -1.0, 0.0))
    return cos_b, sin_b


def circle(product, lon_count):
    quarter = lon_count // 4
    count = jnp.floor(product * (1.0 / quarter) + 0.5)
    angle = (product - count * quarter) * (2.0 * math.pi / lon_count)
    turn = count.astype(I32) & 3
    square = angle * angle
    cos = 1.0 + square * (-1 / 2 + square * (1 / 24 + square * (-1 / 720 + square * (1 / 40320))))
    sin = angle * (
        1.0 + square * (-1 / 6 + square * (1 / 120 + square * (-1 / 5040 + square * (1 / 362880))))
    )
    swap = (turn & 1) == 1
    near, far = jnp.where(swap, sin, cos), jnp.where(swap, cos, sin)
    near = jnp.where((turn == 1) | (turn == 2), -near, near)
    far = jnp.where(turn >= 2, -far, far)
    return near, far


def prepare_kernel(
    order_ref, wave_ref, exp_ref, traj_ref, cos_ref, sin_ref, gain_ref, cos_high_ref, sin_high_ref, *, norm
):
    levels, lats, lons = traj_ref.shape
    width = lons // NBLK
    wave = wave_ref[...].astype(F32)
    shape = (LOW, wave.shape[1])
    cos_low, sin_low = circle(iota(shape, 0).astype(F32) * wave, lons)
    shape = cos_high_ref.shape
    cos_high_ref[...], sin_high_ref[...] = circle((iota(shape, 0) * LOW).astype(F32) * wave, lons)

    @pl.loop(0, cos_ref.shape[0] // LOW)
    def _(i):
        cos_high = cos_high_ref[pl.ds(i, 1), :]
        sin_high = sin_high_ref[pl.ds(i, 1), :]
        at = pl.ds(pl.multiple_of(i * LOW, LOW), LOW)
        cos_ref[at, :] = (cos_high * cos_low - sin_high * sin_low).astype(BF16)
        sin_ref[at, :] = (-(sin_high * cos_low + cos_high * sin_low)).astype(BF16)

    sub = levels * lats
    row, col = iota((sub, sub), 0), iota((sub, sub), 1)
    held = jnp.zeros((sub, sub), I32)
    for r in range(levels):
        held = jnp.where(col // lats == r, order_ref[0, r], held)
    lat = row // 4 % 2 * 2 + row // 8
    pick = jnp.where((held == row % 4) & (col % lats == lat), 1.0, 0.0).astype(BF16)
    power = jnp.concatenate([exp_ref[r] for r in range(levels)], axis=0).astype(F32)
    scale = matmul(pick, jnp.exp2(power).astype(BF16), 1, 0)
    stored = jnp.concatenate([traj_ref[r] for r in range(levels)], axis=0)
    ordered = matmul(pick, stored, 1, 0)
    full = cos_ref.shape[0]
    ahead = iota((sub, full), 1)
    reverse = jnp.where(iota((full, full), 0) + iota((full, full), 1) == full, 1.0, 0.0).astype(BF16)
    for b in range(NBLK):
        start = b * width
        piece = ordered[:, start : start + full] * scale[:, b : b + 1]
        gain = jnp.where(ahead <= width // 2, norm * (1.0 + jnp.tanh(piece)), 0.0)
        gain_ref[b * sub : (b + 1) * sub, :] = gain
        back = ordered[:, start + width - full : start + width].astype(BF16)
        piece = matmul(back, reverse, 1, 0) * scale[:, b : b + 1]
        gain = norm * (1.0 + jnp.tanh(piece))
        gain = jnp.where((ahead >= 1) & (2 * ahead < width), gain, 0.0)
        at = (NBLK + (b + 1) % NBLK) * sub
        gain_ref[at : at + sub, :] = gain


def prepare(order, wave, exps, traj, norm):
    levels, lats, lons = traj.shape
    waves = wave.shape[1]
    high = -(-(lons // NBLK // 2 + 1) // LOW)
    table = jax.ShapeDtypeStruct((high * LOW, waves), BF16)
    vmem = pl.BlockSpec(memory_space=pltpu.VMEM)
    return pl.pallas_call(
        functools.partial(prepare_kernel, norm=norm),
        in_specs=[pl.BlockSpec(memory_space=pltpu.SMEM)] + [vmem] * 3,
        out_specs=[vmem] * 3,
        out_shape=(table, table, jax.ShapeDtypeStruct((2 * NBLK * levels * lats, high * LOW), F32)),
        scratch_shapes=[pltpu.VMEM((-(-high // 8) * 8, waves), F32)] * 2,
        compiler_params=pltpu.CompilerParams(vmem_limit_bytes=16 * 2**20),
        cost_estimate=pl.CostEstimate(flops=12_000_000, bytes_accessed=20_000_000, transcendentals=0),
        name="prepare",
    )(order, wave, exps, traj)


def gather_kernel(in_ref, out_ref, total_ref):
    sources, comps, sub, slots = in_ref.shape
    pick = one_hot(iota((8, comps * sub), 1) // 4, iota((8, comps * sub), 0))
    flat = [jnp.concatenate([in_ref[d, c] for d in range(sources)], axis=1) for c in range(comps)]
    flat = jnp.concatenate(flat, axis=0)
    out_ref[...] = flat
    total_ref[...] = matmul(pick, flat, 1, 0).astype(BF16)


def gather_rows(blocks):
    sources, comps, sub, slots = blocks.shape
    return pl.pallas_call(
        gather_kernel,
        out_shape=(
            jax.ShapeDtypeStruct((comps * sub, sources * slots), BF16),
            jax.ShapeDtypeStruct((comps * sub // 4, sources * slots), BF16),
        ),
        compiler_params=pltpu.CompilerParams(vmem_limit_bytes=8 * 2**20),
        name="gather_rows",
    )(blocks)


def forcing_kernel(index_ref, coef_ref, total_ref, four_ref, wave_ref, gain_ref, cos_ref, sin_ref, out_ref, held_ref, held_sem, *, norm):
    fetch = pltpu.make_async_copy(gain_ref, held_ref, held_sem)
    fetch.start()
    me = index_ref[0]
    groups, rows, waves = total_ref.shape
    both = four_ref.shape[0]
    sub = both // 2
    wave = wave_ref[...]
    carry = jnp.zeros((rows, waves), F32)
    for g in range(groups):
        carry = carry + jnp.where(g < me, total_ref[g].astype(F32), 0.0)
    four = four_ref[...]
    row, col = iota((both, both), 0), iota((both, both), 1)
    earlier = jnp.where((row // 4 == col // 4) & (col < row), 1.0, 0.0).astype(BF16)
    copies = one_hot(iota((both, rows), 0) // 4, iota((both, rows), 1))
    above = matmul(earlier, four, 1, 0) + matmul(copies, carry.astype(BF16), 1, 0)
    level = iota((both, 1), 0) % 4
    coef = jnp.zeros((both, 1), F32)
    for l in range(4):
        coef = jnp.where(level == l, coef_ref[l], coef)
    mixed = (four.astype(F32) + coef * above).astype(BF16)
    first, second = mixed[:sub], mixed[sub:]
    with_cos, with_sin = [], []
    for b in range(NBLK):
        cos_b, sin_b = (v.astype(BF16) for v in turns(wave, b))
        with_cos.append(first * cos_b - second * sin_b)
        with_sin.append(first * sin_b + second * cos_b)
    with_cos = jnp.concatenate(with_cos, axis=0)
    with_sin = jnp.concatenate(with_sin, axis=0)
    even = matmul(with_cos, cos_ref[...], 1, 1)
    odd = matmul(with_sin, sin_ref[...], 1, 1)
    half = NBLK * sub
    fetch.wait()
    ahead = held_ref[:half, :] * (even + odd)
    behind = held_ref[half:, :] * (even - odd)
    forcing = jnp.concatenate([ahead, behind], axis=0).astype(BF16)
    by_cos = matmul(forcing, cos_ref[...], 1, 0)
    by_sin = matmul(forcing, sin_ref[...], 1, 0)
    by_cos = by_cos[:half] + by_cos[half:]
    by_sin = by_sin[:half] - by_sin[half:]
    first = jnp.zeros((sub, waves), F32)
    second = jnp.zeros((sub, waves), F32)
    for b in range(NBLK):
        cos_b, sin_b = turns(wave, b)
        part_cos, part_sin = by_cos[b * sub : (b + 1) * sub], by_sin[b * sub : (b + 1) * sub]
        first = first + part_cos * cos_b + part_sin * sin_b
        second = second + part_sin * cos_b - part_cos * sin_b
    bands, comps, _, slots = out_ref.shape
    half = sub // 2
    for c, value in enumerate((first, second)):
        value = value * norm
        sym, anti = value[:half] + value[half:], value[:half] - value[half:]
        sides = jnp.concatenate([sym, anti], axis=0).astype(BF16)
        for d in range(bands):
            out_ref[d, c] = sides[:, slots * d : slots * (d + 1)]


def forcing_part(index, coef, totals, four, wave, gain, cos_t, sin_t, shape, norm):
    vmem = pl.BlockSpec(memory_space=pltpu.VMEM)
    smem = pl.BlockSpec(memory_space=pltpu.SMEM)
    return pl.pallas_call(
        functools.partial(forcing_kernel, norm=norm),
        in_specs=[smem] * 2 + [vmem] * 3 + [pl.BlockSpec(memory_space=pltpu.HBM)] + [vmem] * 2,
        out_specs=vmem,
        scratch_shapes=[pltpu.VMEM(gain.shape, F32), pltpu.SemaphoreType.DMA],
        out_shape=jax.ShapeDtypeStruct(shape, BF16),
        compiler_params=pltpu.CompilerParams(vmem_limit_bytes=16 * 2**20),
        cost_estimate=pl.CostEstimate(flops=900_000_000, bytes_accessed=8_000_000, transcendentals=0),
        name="forcing_part",
    )(index, coef, totals, four, wave, gain, cos_t, sin_t)


def body(adj_spec, wave_of_slot, legendre, lat_weight, traj, traj_exp, traj_order, lev_coef):
    levels, degrees = adj_spec.shape[0], adj_spec.shape[3]
    norm = 1.0 / math.sqrt(degrees)
    band = lax.axis_index("band").astype(I32)[None]
    index = lax.axis_index("lev").astype(I32)[None]
    wave = wave_of_slot[None, :]
    blocks = synthesis(adj_spec, legendre, band, wave_of_slot, lat_weight)
    blocks = lax.all_to_all(blocks, "band", split_axis=0, concat_axis=0, tiled=True)
    cos_t, sin_t, gain = prepare(traj_order, wave, traj_exp, traj, norm)
    four, total = gather_rows(blocks)
    totals = lax.all_gather(total, "lev")
    sides = forcing_part(
        index, lev_coef, totals, four, wave, gain, cos_t, sin_t, blocks.shape, norm
    )
    sides = lax.all_to_all(sides, "band", split_axis=0, concat_axis=0, tiled=True)
    return analysis(sides, legendre, band, wave_of_slot, levels)


def solution(mesh):
    return jax.shard_map(
        body,
        mesh=mesh,
        in_specs=(
            P("lev", "band", None, None),
            P(),
            P("band", None, None),
            P(),
            P("lev", "band", None),
            P("lev", "band", None),
            P("lev", None),
            P("lev"),
        ),
        out_specs=P("lev", "band", None, None),
        check_vma=False,
    )
```

```python
import functools
import math

import jax
import jax.numpy as jnp
from jax import lax
from jax.experimental import pallas as pl
from jax.experimental.pallas import tpu as pltpu
from jax.sharding import Mesh
from jax.sharding import PartitionSpec as P

F32, BF16, I32 = jnp.float32, jnp.bfloat16, jnp.int32
GROUP = 8


def iota(shape, dim):
    return lax.broadcasted_iota(I32, shape, dim)


def matmul(a, b, ca, cb):
    return lax.dot_general(a, b, (((ca,), (cb,)), ((), ())), preferred_element_type=F32)


def one_hot(rows, cols):
    return jnp.where(rows == cols, 1.0, 0.0).astype(BF16)


def limits(band_ref, wave_ref, at, slots, comps, degrees):
    rows = GROUP * comps
    slot = iota((rows, 1), 0) // comps
    first = band_ref[0] * slots + at * GROUP
    limit = jnp.zeros((rows, 1), I32)
    for s in range(GROUP):
        limit = jnp.where(slot == s, degrees - wave_ref[first + s], limit)
    return limit


def synthesis_kernel(
    band_ref, wave_ref, weight_ref, adj_hbm, leg_hbm, out_ref, adj_ref, leg_ref, acc_ref, adj_sem, leg_sem
):
    levels, slots, comps, degrees = adj_ref.shape
    rows = GROUP * comps
    heights = leg_ref.shape[1]
    steps = slots // GROUP
    fetches = []
    for g in range(steps):
        here = pl.ds(g * GROUP, GROUP)
        fetches.append((
            pltpu.make_async_copy(adj_hbm.at[:, here], adj_ref.at[:, here], adj_sem.at[g]),
            pltpu.make_async_copy(leg_hbm.at[here], leg_ref.at[here], leg_sem.at[g]),
        ))
        for fetch in fetches[-1]:
            fetch.start()
    weight = jnp.concatenate([weight_ref[...]] * (128 // heights), axis=1)
    half = levels * rows
    for g in range(steps):
        for fetch in fetches[g]:
            fetch.wait()
        here = pl.ds(g * GROUP, GROUP)
        limit = limits(band_ref, wave_ref, g, slots, comps, degrees)
        degree = iota((rows, degrees), 1)
        inside = degree < limit
        even = jnp.where(inside & (degree % 2 == 0), 1.0, 0.0).astype(BF16)
        odd = jnp.where(inside & (degree % 2 == 1), 1.0, 0.0).astype(BF16)
        values = [adj_ref[l, here].reshape(rows, degrees) for l in range(levels)]
        left = jnp.concatenate([v * even for v in values] + [v * odd for v in values], axis=0)
        table = leg_ref[here].reshape(GROUP * heights, degrees)
        both = matmul(left, table, 1, 1)
        shape = both.shape
        own = (iota(shape, 0) % rows) // comps == iota(shape, 1) // heights
        both = jnp.where(own, both, 0.0)
        both = both[:, :128] + both[:, 128:]
        both = both + pltpu.roll(both, 64, 1)
        both = both + pltpu.roll(both, 32, 1)
        from_even, from_odd = both[:half], both[half:]
        north = (from_even + from_odd) * weight
        south = (from_even - from_odd) * weight
        for l in range(levels):
            acc_ref[l, g * rows : (g + 1) * rows, :] = north[l * rows : (l + 1) * rows]
            acc_ref[levels + l, g * rows : (g + 1) * rows, :] = south[l * rows : (l + 1) * rows]
    total = acc_ref.shape[1]
    sides = 2 * levels
    lane = iota((total, 128), 1) // heights
    blocks = []
    for k in range(sides // 4):
        mix = acc_ref[4 * k]
        for r in range(1, 4):
            mix = jnp.where(lane == r, acc_ref[4 * k + r], mix)
        blocks.append(mix.astype(BF16))
    wide = jnp.concatenate(blocks, axis=1)
    col = iota((total, 2 * 128), 1)
    source = iota((total, 2 * 128), 0)
    comp, slot = col // 128, col % 128
    spread = jnp.where((source == slot * comps + comp) & (slot < slots), 1.0, 0.0).astype(BF16)
    turned = matmul(wide, spread, 0, 0).astype(BF16)
    size = sides * heights
    dest = iota((size, size), 0)
    origin = iota((size, size), 1)
    band, e, hh, l = dest // 16, dest // 8 % 2, dest // 4 % 2, dest % 4
    wanted = (e * levels + l) * heights + band * 2 + hh
    moved = matmul(one_hot(wanted, origin), turned, 1, 0).astype(BF16)
    for d in range(size // 16):
        for c in range(comps):
            tile = moved[16 * d : 16 * d + 16, 128 * c : 128 * c + slots]
            for core in range(2):
                out_ref[2 * d + core, c] = tile


def synthesis(adj, leg, band, waves, weight):
    levels, slots, comps, degrees = adj.shape
    heights = leg.shape[1]
    smem = pl.BlockSpec(memory_space=pltpu.SMEM)
    vmem = pl.BlockSpec(memory_space=pltpu.VMEM)
    hbm = pl.BlockSpec(memory_space=pltpu.HBM)
    return pl.pallas_call(
        synthesis_kernel,
        in_specs=[smem, smem, vmem, hbm, hbm],
        out_specs=vmem,
        out_shape=jax.ShapeDtypeStruct((32, comps, 16, slots), BF16),
        scratch_shapes=[
            pltpu.VMEM(adj.shape, BF16),
            pltpu.VMEM(leg.shape, BF16),
            pltpu.VMEM((2 * levels, slots * comps, 128), F32),
            pltpu.SemaphoreType.DMA((slots // GROUP,)),
            pltpu.SemaphoreType.DMA((slots // GROUP,)),
        ],
        compiler_params=pltpu.CompilerParams(vmem_limit_bytes=60 * 2**20),
        name="synthesis",
    )(band, waves, weight[None, :], adj, leg)


def analysis_kernel(band_ref, wave_ref, in_ref, leg_hbm, out_hbm, leg_ref, left_ref, out_ref, leg_sem, out_sem):
    slots, heights, degrees = leg_ref.shape
    levels, _, comps, _ = out_ref.shape
    sources, _, sub, _ = in_ref.shape
    rows = GROUP * comps
    kinds = 2 * levels
    steps = slots // GROUP
    fetches = []
    for g in range(steps):
        here = pl.ds(g * GROUP, GROUP)
        fetches.append(pltpu.make_async_copy(leg_hbm.at[here], leg_ref.at[here], leg_sem.at[g]))
        fetches[-1].start()
    size = sources * sub
    row = iota((size, kinds * 128), 0)
    col = iota((size, kinds * 128), 1)
    row_key = (row // 8 % 2 * levels + row % 4) * heights + row // 16 * 2 + row // 4 % 2
    pick = one_hot(row_key, col // 128 * heights + col % heights)
    parts = []
    for c in range(comps):
        flat = jnp.concatenate([in_ref[d, c] for d in range(sources)], axis=0)
        parts.append(matmul(flat, pick, 0, 0).astype(BF16))
    apart = jnp.concatenate(parts, axis=0)
    total = slots * comps
    weave = one_hot(
        iota((total, total), 0) % comps * slots + iota((total, total), 0) // comps,
        iota((total, total), 1),
    )
    left_ref[...] = matmul(weave, apart, 1, 0).astype(BF16)
    half = levels * rows
    sends = []
    for g in range(steps):
        here = pl.ds(g * GROUP, GROUP)
        own_rows = left_ref[g * rows : (g + 1) * rows, :]
        stack = jnp.concatenate([own_rows[:, 128 * k : 128 * k + 128] for k in range(kinds)], axis=0)
        left = jnp.concatenate([stack, stack], axis=1)
        shape = left.shape
        own = (iota(shape, 0) % rows) // comps == iota(shape, 1) // heights
        left = left * jnp.where(own, 1.0, 0.0).astype(BF16)
        fetches[g].wait()
        both = matmul(left, leg_ref[here].reshape(GROUP * heights, degrees), 1, 0)
        limit = limits(band_ref, wave_ref, g, slots, comps, degrees)
        degree = iota((rows, degrees), 1)
        inside = degree < limit
        even = degree % 2 == 0
        for l in range(levels):
            sym = both[l * rows : (l + 1) * rows]
            anti = both[half + l * rows : half + (l + 1) * rows]
            value = jnp.where(inside, jnp.where(even, sym, anti), 0.0).astype(BF16)
            out_ref[l, here] = value.reshape(GROUP, comps, degrees)
        sends.append(pltpu.make_async_copy(out_ref.at[:, here], out_hbm.at[:, here], out_sem.at[g]))
        sends[-1].start()
    for send in sends:
        send.wait()


def analysis(sides, leg, band, waves, levels):
    sources, comps, sub, slots = sides.shape
    heights, degrees = leg.shape[1:]
    smem = pl.BlockSpec(memory_space=pltpu.SMEM)
    vmem = pl.BlockSpec(memory_space=pltpu.VMEM)
    hbm = pl.BlockSpec(memory_space=pltpu.HBM)
    shape = (levels, slots, comps, degrees)
    return pl.pallas_call(
        analysis_kernel,
        in_specs=[smem, smem, vmem, hbm],
        out_specs=hbm,
        out_shape=jax.ShapeDtypeStruct(shape, BF16),
        scratch_shapes=[
            pltpu.VMEM(leg.shape, BF16),
            pltpu.VMEM((slots * comps, 2 * levels * 128), BF16),
            pltpu.VMEM(shape, BF16),
            pltpu.SemaphoreType.DMA((slots // GROUP,)),
            pltpu.SemaphoreType.DMA((slots // GROUP,)),
        ],
        compiler_params=pltpu.CompilerParams(vmem_limit_bytes=60 * 2**20),
        name="analysis",
    )(band, waves, sides, leg)

NBLK = 4
LOW = 16


def turns(wave, b):
    turn = (wave * b) & 3
    cos_b = jnp.where(turn == 0, 1.0, jnp.where(turn == 2, -1.0, 0.0))
    sin_b = jnp.where(turn == 1, 1.0, jnp.where(turn == 3, -1.0, 0.0))
    return cos_b, sin_b


def circle(product, lon_count):
    quarter = lon_count // 4
    count = jnp.floor(product * (1.0 / quarter) + 0.5)
    angle = (product - count * quarter) * (2.0 * math.pi / lon_count)
    turn = count.astype(I32) & 3
    square = angle * angle
    cos = 1.0 + square * (-1 / 2 + square * (1 / 24 + square * (-1 / 720 + square * (1 / 40320))))
    sin = angle * (
        1.0 + square * (-1 / 6 + square * (1 / 120 + square * (-1 / 5040 + square * (1 / 362880))))
    )
    swap = (turn & 1) == 1
    near, far = jnp.where(swap, sin, cos), jnp.where(swap, cos, sin)
    near = jnp.where((turn == 1) | (turn == 2), -near, near)
    far = jnp.where(turn >= 2, -far, far)
    return near, far


def prepare_kernel(
    order_ref, wave_ref, exp_ref, traj_ref, cos_ref, sin_ref, gain_hbm, token_ref,
    cos_high_ref, sin_high_ref, gain_ref, gain_sem, *, norm
):
    levels, lats, lons = traj_ref.shape
    width = lons // NBLK
    wave = wave_ref[...].astype(F32)
    shape = (LOW, wave.shape[1])
    cos_low, sin_low = circle(iota(shape, 0).astype(F32) * wave, lons)
    shape = cos_high_ref.shape
    cos_high_ref[...], sin_high_ref[...] = circle((iota(shape, 0) * LOW).astype(F32) * wave, lons)

    @pl.loop(0, cos_ref.shape[0] // LOW)
    def _(i):
        cos_high = cos_high_ref[pl.ds(i, 1), :]
        sin_high = sin_high_ref[pl.ds(i, 1), :]
        at = pl.ds(pl.multiple_of(i * LOW, LOW), LOW)
        cos_ref[at, :] = (cos_high * cos_low - sin_high * sin_low).astype(BF16)
        sin_ref[at, :] = (-(sin_high * cos_low + cos_high * sin_low)).astype(BF16)

    sub = levels * lats
    row, col = iota((sub, sub), 0), iota((sub, sub), 1)
    held = jnp.zeros((sub, sub), I32)
    for r in range(levels):
        held = jnp.where(col // lats == r, order_ref[0, r], held)
    lat = row // 4 % 2 * 2 + row // 8
    pick = jnp.where((held == row % 4) & (col % lats == lat), 1.0, 0.0).astype(BF16)
    power = jnp.concatenate([exp_ref[r] for r in range(levels)], axis=0).astype(F32)
    scale = matmul(pick, jnp.exp2(power).astype(BF16), 1, 0)
    stored = jnp.concatenate([traj_ref[r] for r in range(levels)], axis=0)
    ordered = matmul(pick, stored, 1, 0)
    full = cos_ref.shape[0]
    ahead = iota((sub, full), 1)
    reverse = jnp.where(iota((full, full), 0) + iota((full, full), 1) == full, 1.0, 0.0).astype(BF16)
    for b in range(NBLK):
        start = b * width
        piece = ordered[:, start : start + full] * scale[:, b : b + 1]
        gain = jnp.where(ahead <= width // 2, norm * (1.0 + jnp.tanh(piece)), 0.0)
        gain_ref[b * sub : (b + 1) * sub, :] = gain
        back = ordered[:, start + width - full : start + width].astype(BF16)
        piece = matmul(back, reverse, 1, 0) * scale[:, b : b + 1]
        gain = norm * (1.0 + jnp.tanh(piece))
        gain = jnp.where((ahead >= 1) & (2 * ahead < width), gain, 0.0)
        at = (NBLK + (b + 1) % NBLK) * sub
        gain_ref[at : at + sub, :] = gain
    send = pltpu.make_async_copy(gain_ref, gain_hbm, gain_sem)
    send.start()
    token_ref[...] = jnp.zeros(token_ref.shape, F32)
    send.wait()


def prepare(order, wave, exps, traj, norm):
    levels, lats, lons = traj.shape
    waves = wave.shape[1]
    high = -(-(lons // NBLK // 2 + 1) // LOW)
    table = jax.ShapeDtypeStruct((high * LOW, waves), BF16)
    gain = jax.ShapeDtypeStruct((2 * NBLK * levels * lats, high * LOW), F32)
    vmem = pl.BlockSpec(memory_space=pltpu.VMEM)
    return pl.pallas_call(
        functools.partial(prepare_kernel, norm=norm),
        in_specs=[pl.BlockSpec(memory_space=pltpu.SMEM)] + [vmem] * 3,
        out_specs=[vmem, vmem, pl.BlockSpec(memory_space=pltpu.HBM), vmem],
        out_shape=(table, table, gain, jax.ShapeDtypeStruct((8, 128), F32)),
        scratch_shapes=[pltpu.VMEM((-(-high // 8) * 8, waves), F32)] * 2
        + [pltpu.VMEM(gain.shape, F32), pltpu.SemaphoreType.DMA],
        compiler_params=pltpu.CompilerParams(vmem_limit_bytes=16 * 2**20),
        cost_estimate=pl.CostEstimate(flops=12_000_000, bytes_accessed=20_000_000, transcendentals=0),
        name="prepare",
    )(order, wave, exps, traj)


def gather_kernel(index_ref, token_ref, in_ref, out_ref, below_ref, share_ref):
    core = index_ref[0] % 2
    sources, comps, sub, slots = in_ref.shape
    bands = sources // 2
    pick = one_hot(iota((sub // 4, sub), 1) // 4, iota((sub // 4, sub), 0))
    totals = []
    for side in range(2):
        at = core if side == 0 else 1 - core
        flat = [
            jnp.concatenate([in_ref[2 * d + at, c] for d in range(bands)], axis=1)
            for c in range(comps)
        ]
        if side == 0:
            out_ref[...] = jnp.concatenate(flat, axis=0)
        totals.append([matmul(pick, value, 1, 0) for value in flat])
    below_ref[...] = jnp.concatenate(totals[1], axis=0)
    chip = [mine + other for mine, other in zip(*totals)]
    chip = jnp.where(core == 0, chip[0], chip[1])
    half = chip.shape[1] // 2
    share = jnp.concatenate([chip[:, :half], chip[:, half:]], axis=0).astype(BF16)
    for d in range(share_ref.shape[0]):
        share_ref[d] = share


def gather_rows(index, token, blocks, groups):
    sources, comps, sub, slots = blocks.shape
    waves = sources // 2 * slots
    smem = pl.BlockSpec(memory_space=pltpu.SMEM)
    vmem = pl.BlockSpec(memory_space=pltpu.VMEM)
    return pl.pallas_call(
        gather_kernel,
        in_specs=[smem, vmem, vmem],
        out_specs=[vmem] * 3,
        out_shape=(
            jax.ShapeDtypeStruct((comps * sub, waves), BF16),
            jax.ShapeDtypeStruct((comps * sub // 4, waves), F32),
            jax.ShapeDtypeStruct((groups, sub // 2, waves // 2), BF16),
        ),
        compiler_params=pltpu.CompilerParams(vmem_limit_bytes=8 * 2**20),
        name="gather_rows",
    )(index, token, blocks)


def forcing_kernel(
    index_ref, coef_ref, total_ref, below_ref, four_ref, wave_ref, gain_ref, cos_ref, sin_ref,
    out_ref, held_ref, held_sem, *, norm
):
    fetch = pltpu.make_async_copy(gain_ref, held_ref, held_sem)
    fetch.start()
    me = index_ref[0]
    groups = total_ref.shape[0]
    rows, waves = below_ref.shape
    both = four_ref.shape[0]
    sub = both // 2
    wave = wave_ref[...]
    parts = []
    for c in range(2):
        part = jnp.zeros(total_ref.shape[1:], F32)
        for z in range(groups // 2):
            part = part + jnp.where(z < me // 2, total_ref[2 * z + c].astype(F32), 0.0)
        parts.append(jnp.concatenate([part[: rows // 2], part[rows // 2 :]], axis=1))
    carry = jnp.concatenate(parts, axis=0) + jnp.where(me % 2 == 1, below_ref[...], 0.0)
    four = four_ref[...]
    row, col = iota((both, both), 0), iota((both, both), 1)
    earlier = jnp.where((row // 4 == col // 4) & (col < row), 1.0, 0.0).astype(BF16)
    copies = one_hot(iota((both, rows), 0) // 4, iota((both, rows), 1))
    above = matmul(earlier, four, 1, 0) + matmul(copies, carry.astype(BF16), 1, 0)
    level = iota((both, 1), 0) % 4
    coef = jnp.zeros((both, 1), F32)
    for l in range(4):
        coef = jnp.where(level == l, coef_ref[l], coef)
    mixed = (four.astype(F32) + coef * above).astype(BF16)
    first, second = mixed[:sub], mixed[sub:]
    with_cos, with_sin = [], []
    for b in range(NBLK):
        cos_b, sin_b = (v.astype(BF16) for v in turns(wave, b))
        with_cos.append(first * cos_b - second * sin_b)
        with_sin.append(first * sin_b + second * cos_b)
    with_cos = jnp.concatenate(with_cos, axis=0)
    with_sin = jnp.concatenate(with_sin, axis=0)
    even = matmul(with_cos, cos_ref[...], 1, 1)
    odd = matmul(with_sin, sin_ref[...], 1, 1)
    half = NBLK * sub
    fetch.wait()
    ahead = held_ref[:half, :] * (even + odd)
    behind = held_ref[half:, :] * (even - odd)
    forcing = jnp.concatenate([ahead, behind], axis=0).astype(BF16)
    by_cos = matmul(forcing, cos_ref[...], 1, 0)
    by_sin = matmul(forcing, sin_ref[...], 1, 0)
    by_cos = by_cos[:half] + by_cos[half:]
    by_sin = by_sin[:half] - by_sin[half:]
    first = jnp.zeros((sub, waves), F32)
    second = jnp.zeros((sub, waves), F32)
    for b in range(NBLK):
        cos_b, sin_b = turns(wave, b)
        part_cos, part_sin = by_cos[b * sub : (b + 1) * sub], by_sin[b * sub : (b + 1) * sub]
        first = first + part_cos * cos_b + part_sin * sin_b
        second = second + part_sin * cos_b - part_cos * sin_b
    bands, comps, _, slots = out_ref.shape
    half = sub // 2
    for c, value in enumerate((first, second)):
        value = value * norm
        sym, anti = value[:half] + value[half:], value[:half] - value[half:]
        sides = jnp.concatenate([sym, anti], axis=0).astype(BF16)
        for d in range(bands):
            out_ref[d, c] = sides[:, slots * d : slots * (d + 1)]


def forcing_part(index, coef, totals, below, four, wave, gain, cos_t, sin_t, shape, norm):
    vmem = pl.BlockSpec(memory_space=pltpu.VMEM)
    smem = pl.BlockSpec(memory_space=pltpu.SMEM)
    return pl.pallas_call(
        functools.partial(forcing_kernel, norm=norm),
        in_specs=[smem] * 2 + [vmem] * 4 + [pl.BlockSpec(memory_space=pltpu.HBM)] + [vmem] * 2,
        out_specs=vmem,
        scratch_shapes=[pltpu.VMEM(gain.shape, F32), pltpu.SemaphoreType.DMA],
        out_shape=jax.ShapeDtypeStruct(shape, BF16),
        compiler_params=pltpu.CompilerParams(vmem_limit_bytes=40 * 2**20),
        cost_estimate=pl.CostEstimate(flops=900_000_000, bytes_accessed=8_000_000, transcendentals=0),
        name="forcing_part",
    )(index, coef, totals, below, four, wave, gain, cos_t, sin_t)


def body(adj_spec, wave_of_slot, legendre, lat_weight, traj, traj_exp, traj_order, lev_coef):
    levels, degrees = adj_spec.shape[0], adj_spec.shape[3]
    groups = lax.axis_size(("z", "core"))
    norm = 1.0 / math.sqrt(degrees)
    band = lax.axis_index("band").astype(I32)[None]
    index = lax.axis_index(("z", "core")).astype(I32)[None]
    wave = wave_of_slot[None, :]
    blocks = synthesis(adj_spec, legendre, band, wave_of_slot, lat_weight)
    blocks = lax.all_to_all(blocks, ("band", "core"), split_axis=0, concat_axis=0, tiled=True)
    cos_t, sin_t, gain, token = prepare(traj_order, wave, traj_exp, traj, norm)
    four, below, shares = gather_rows(index, token, blocks, groups)
    totals = lax.all_to_all(shares, ("z", "core"), split_axis=0, concat_axis=0, tiled=True)
    shape = (blocks.shape[0] // 2, *blocks.shape[1:])
    sides = forcing_part(
        index, lev_coef, totals, below, four, wave, gain, cos_t, sin_t, shape, norm
    )
    sides = lax.all_to_all(sides, "band", split_axis=0, concat_axis=0, tiled=True)
    return analysis(sides, legendre, band, wave_of_slot, levels)


def solution(mesh):
    chips = Mesh(mesh.devices.reshape(mesh.shape["band"], -1, 2), ("band", "z", "core"))
    lev = ("z", "core")
    return jax.shard_map(
        body,
        mesh=chips,
        in_specs=(
            P(lev, "band", None, None),
            P(),
            P("band", None, None),
            P(),
            P(lev, "band", None),
            P(lev, "band", None),
            P(lev, None),
            P(lev),
        ),
        out_specs=P(lev, "band", None, None),
        check_vma=False,
    )
```

```python
import functools
import math

import jax
import jax.numpy as jnp
from jax import lax
from jax.experimental import pallas as pl
from jax.experimental.pallas import tpu as pltpu
from jax.sharding import Mesh
from jax.sharding import PartitionSpec as P

F32, BF16, I32 = jnp.float32, jnp.bfloat16, jnp.int32
GROUP = 8
CHUNK = 2


def iota(shape, dim):
    return lax.broadcasted_iota(I32, shape, dim)


def matmul(a, b, ca, cb):
    return lax.dot_general(a, b, (((ca,), (cb,)), ((), ())), preferred_element_type=F32)


def one_hot(rows, cols):
    return jnp.where(rows == cols, 1.0, 0.0).astype(BF16)


def limits(band_ref, wave_ref, at, slots, comps, degrees):
    rows = GROUP * comps
    slot = iota((rows, 1), 0) // comps
    first = band_ref[0] * slots + at * GROUP
    limit = jnp.zeros((rows, 1), I32)
    for s in range(GROUP):
        limit = jnp.where(slot == s, degrees - wave_ref[first + s], limit)
    return limit


def synthesis_kernel(
    band_ref, wave_ref, weight_ref, adj_hbm, leg_hbm, out_ref,
    adj_ref, leg_ref, acc_ref, spread_ref, order_ref, adj_sem, leg_sem
):
    levels, slots, comps, degrees = adj_ref.shape
    rows = GROUP * comps
    heights = leg_ref.shape[1]
    steps = slots // GROUP
    fetches = []
    for g in range(steps):
        here = pl.ds(g * GROUP, GROUP)
        fetches.append((
            pltpu.make_async_copy(adj_hbm.at[:, here], adj_ref.at[:, here], adj_sem.at[g]),
            pltpu.make_async_copy(leg_hbm.at[here], leg_ref.at[here], leg_sem.at[g]),
        ))
        for fetch in fetches[-1]:
            fetch.start()
    weight = jnp.concatenate([weight_ref[...]] * (128 // heights), axis=1)
    total = slots * comps
    col, source = iota((total, comps * 128), 1), iota((total, comps * 128), 0)
    slot = col % 128
    own = (source == slot * comps + col // 128) & (slot < slots)
    spread_ref[...] = jnp.where(own, 1.0, 0.0).astype(BF16)
    size = 2 * levels * heights
    dest, origin = iota((size, size), 1), iota((size, size), 0)
    band, e, hh, l = dest // 16, dest // 8 % 2, dest // 4 % 2, dest % 4
    order_ref[...] = one_hot((e * levels + l) * heights + band * 2 + hh, origin)
    shape = (2 * levels * rows, GROUP * heights)
    own = (iota(shape, 0) % rows) // comps == iota(shape, 1) // heights
    degree = iota((rows, degrees), 1)
    sign = jnp.where(degree % 2 == 0, 1.0, -1.0).astype(BF16)
    lane = iota((rows, 128), 1) // heights
    for first in range(0, steps, CHUNK):
        group = range(first, first + CHUNK)
        for g in group:
            for fetch in fetches[g]:
                fetch.wait()
        wide = []
        for g in group:
            here = pl.ds(g * GROUP, GROUP)
            limit = limits(band_ref, wave_ref, g, slots, comps, degrees)
            inside = jnp.where(degree < limit, 1.0, 0.0).astype(BF16)
            flipped = inside * sign
            values = [adj_ref[l, here].reshape(rows, degrees) for l in range(levels)]
            left = jnp.concatenate(
                [v * inside for v in values] + [v * flipped for v in values], axis=0
            )
            both = matmul(left, leg_ref[here].reshape(GROUP * heights, degrees), 1, 1)
            both = jnp.where(own, both, 0.0)
            both = both[:, :128] + both[:, 128:]
            both = both + pltpu.roll(both, 64, 1)
            both = (both + pltpu.roll(both, 32, 1)) * weight
            blocks = []
            for k in range(2 * levels // 4):
                mix = both[4 * k * rows : (4 * k + 1) * rows]
                for r in range(1, 4):
                    part = both[(4 * k + r) * rows : (4 * k + r + 1) * rows]
                    mix = jnp.where(lane == r, part, mix)
                blocks.append(mix.astype(BF16))
            wide.append(jnp.concatenate(blocks, axis=1))
        acc_ref[first * rows : (first + CHUNK) * rows, :] = jnp.concatenate(wide, axis=0)
    wide = matmul(acc_ref[...], order_ref[...], 1, 0).astype(BF16)
    moved = matmul(wide, spread_ref[...], 0, 0).astype(BF16)
    for d in range(size // 16):
        for c in range(comps):
            out_ref[d, c] = moved[16 * d : 16 * d + 16, 128 * c : 128 * c + slots]


def synthesis(adj, leg, band, waves, weight):
    levels, slots, comps, degrees = adj.shape
    heights = leg.shape[1]
    size = 2 * levels * heights
    smem = pl.BlockSpec(memory_space=pltpu.SMEM)
    vmem = pl.BlockSpec(memory_space=pltpu.VMEM)
    hbm = pl.BlockSpec(memory_space=pltpu.HBM)
    return pl.pallas_call(
        synthesis_kernel,
        in_specs=[smem, smem, vmem, hbm, hbm],
        out_specs=vmem,
        out_shape=jax.ShapeDtypeStruct((16, comps, 16, slots), BF16),
        scratch_shapes=[
            pltpu.VMEM(adj.shape, BF16),
            pltpu.VMEM(leg.shape, BF16),
            pltpu.VMEM((slots * comps, size), BF16),
            pltpu.VMEM((slots * comps, comps * 128), BF16),
            pltpu.VMEM((size, size), BF16),
            pltpu.SemaphoreType.DMA((slots // GROUP,)),
            pltpu.SemaphoreType.DMA((slots // GROUP,)),
        ],
        compiler_params=pltpu.CompilerParams(vmem_limit_bytes=60 * 2**20),
        name="synthesis",
    )(band, waves, weight[None, :], adj, leg)


def analysis_kernel(band_ref, wave_ref, in_ref, leg_hbm, out_hbm, leg_ref, left_ref, out_ref, leg_sem, out_sem):
    slots, heights, degrees = leg_ref.shape
    levels, _, comps, _ = out_ref.shape
    sources, _, sub, _ = in_ref.shape
    rows = GROUP * comps
    kinds = 2 * levels
    steps = slots // GROUP
    fetches = []
    for g in range(steps):
        here = pl.ds(g * GROUP, GROUP)
        fetches.append(pltpu.make_async_copy(leg_hbm.at[here], leg_ref.at[here], leg_sem.at[g]))
        fetches[-1].start()
    size = sources * sub
    row = iota((size, kinds * 128), 0)
    col = iota((size, kinds * 128), 1)
    row_key = (row // 8 % 2 * levels + row % 4) * heights + row // 16 * 2 + row // 4 % 2
    pick = one_hot(row_key, col // 128 * heights + col % heights)
    parts = []
    for c in range(comps):
        flat = jnp.concatenate([in_ref[d, c] for d in range(sources)], axis=0)
        parts.append(matmul(flat, pick, 0, 0).astype(BF16))
    apart = jnp.concatenate(parts, axis=0)
    total = slots * comps
    weave = one_hot(
        iota((total, total), 0) % comps * slots + iota((total, total), 0) // comps,
        iota((total, total), 1),
    )
    left_ref[...] = matmul(weave, apart, 1, 0).astype(BF16)
    half = levels * rows
    sends = []
    for g in range(steps):
        here = pl.ds(g * GROUP, GROUP)
        own_rows = left_ref[g * rows : (g + 1) * rows, :]
        stack = jnp.concatenate([own_rows[:, 128 * k : 128 * k + 128] for k in range(kinds)], axis=0)
        left = jnp.concatenate([stack, stack], axis=1)
        shape = left.shape
        own = (iota(shape, 0) % rows) // comps == iota(shape, 1) // heights
        left = left * jnp.where(own, 1.0, 0.0).astype(BF16)
        fetches[g].wait()
        both = matmul(left, leg_ref[here].reshape(GROUP * heights, degrees), 1, 0)
        limit = limits(band_ref, wave_ref, g, slots, comps, degrees)
        degree = iota((rows, degrees), 1)
        inside = degree < limit
        even = degree % 2 == 0
        for l in range(levels):
            sym = both[l * rows : (l + 1) * rows]
            anti = both[half + l * rows : half + (l + 1) * rows]
            value = jnp.where(inside, jnp.where(even, sym, anti), 0.0).astype(BF16)
            out_ref[l, here] = value.reshape(GROUP, comps, degrees)
        sends.append(pltpu.make_async_copy(out_ref.at[:, here], out_hbm.at[:, here], out_sem.at[g]))
        sends[-1].start()
    for send in sends:
        send.wait()


def analysis(sides, leg, band, waves, levels):
    sources, comps, sub, slots = sides.shape
    heights, degrees = leg.shape[1:]
    smem = pl.BlockSpec(memory_space=pltpu.SMEM)
    vmem = pl.BlockSpec(memory_space=pltpu.VMEM)
    hbm = pl.BlockSpec(memory_space=pltpu.HBM)
    shape = (levels, slots, comps, degrees)
    return pl.pallas_call(
        analysis_kernel,
        in_specs=[smem, smem, vmem, hbm],
        out_specs=hbm,
        out_shape=jax.ShapeDtypeStruct(shape, BF16),
        scratch_shapes=[
            pltpu.VMEM(leg.shape, BF16),
            pltpu.VMEM((slots * comps, 2 * levels * 128), BF16),
            pltpu.VMEM(shape, BF16),
            pltpu.SemaphoreType.DMA((slots // GROUP,)),
            pltpu.SemaphoreType.DMA((slots // GROUP,)),
        ],
        compiler_params=pltpu.CompilerParams(vmem_limit_bytes=60 * 2**20),
        name="analysis",
    )(band, waves, sides, leg)

NBLK = 4
LOW = 16


def turns(wave, b):
    turn = (wave * b) & 3
    cos_b = jnp.where(turn == 0, 1.0, jnp.where(turn == 2, -1.0, 0.0))
    sin_b = jnp.where(turn == 1, 1.0, jnp.where(turn == 3, -1.0, 0.0))
    return cos_b, sin_b


def circle(product, lon_count):
    quarter = lon_count // 4
    count = jnp.floor(product * (1.0 / quarter) + 0.5)
    angle = (product - count * quarter) * (2.0 * math.pi / lon_count)
    turn = count.astype(I32) & 3
    square = angle * angle
    cos = 1.0 + square * (-1 / 2 + square * (1 / 24 + square * (-1 / 720 + square * (1 / 40320))))
    sin = angle * (
        1.0 + square * (-1 / 6 + square * (1 / 120 + square * (-1 / 5040 + square * (1 / 362880))))
    )
    swap = (turn & 1) == 1
    near, far = jnp.where(swap, sin, cos), jnp.where(swap, cos, sin)
    near = jnp.where((turn == 1) | (turn == 2), -near, near)
    far = jnp.where(turn >= 2, -far, far)
    return near, far


def prepare_kernel(
    order_ref, wave_ref, exp_ref, traj_ref, cos_ref, sin_ref, gain_hbm, token_ref,
    cos_high_ref, sin_high_ref, gain_ref, gain_sem, *, norm
):
    levels, lats, lons = traj_ref.shape
    width = lons // NBLK
    wave = wave_ref[...].astype(F32)
    shape = (LOW, wave.shape[1])
    cos_low, sin_low = circle(iota(shape, 0).astype(F32) * wave, lons)
    shape = cos_high_ref.shape
    cos_high_ref[...], sin_high_ref[...] = circle((iota(shape, 0) * LOW).astype(F32) * wave, lons)

    @pl.loop(0, cos_ref.shape[0] // LOW)
    def _(i):
        cos_high = cos_high_ref[pl.ds(i, 1), :]
        sin_high = sin_high_ref[pl.ds(i, 1), :]
        at = pl.ds(pl.multiple_of(i * LOW, LOW), LOW)
        cos_ref[at, :] = (cos_high * cos_low - sin_high * sin_low).astype(BF16)
        sin_ref[at, :] = (-(sin_high * cos_low + cos_high * sin_low)).astype(BF16)

    sub = levels * lats
    row, col = iota((sub, sub), 0), iota((sub, sub), 1)
    held = jnp.zeros((sub, sub), I32)
    for r in range(levels):
        held = jnp.where(col // lats == r, order_ref[0, r], held)
    lat = row // 4 % 2 * 2 + row // 8
    pick = jnp.where((held == row % 4) & (col % lats == lat), 1.0, 0.0).astype(BF16)
    power = jnp.concatenate([exp_ref[r] for r in range(levels)], axis=0).astype(F32)
    scale = matmul(pick, jnp.exp2(power).astype(BF16), 1, 0)
    stored = jnp.concatenate([traj_ref[r] for r in range(levels)], axis=0)
    ordered = matmul(pick, stored, 1, 0)
    full = cos_ref.shape[0]
    ahead = iota((sub, full), 1)
    reverse = jnp.where(iota((full, full), 0) + iota((full, full), 1) == full, 1.0, 0.0).astype(BF16)
    for b in range(NBLK):
        start = b * width
        piece = ordered[:, start : start + full] * scale[:, b : b + 1]
        gain = jnp.where(ahead <= width // 2, norm * (1.0 + jnp.tanh(piece)), 0.0)
        gain_ref[b * sub : (b + 1) * sub, :] = gain
        back = ordered[:, start + width - full : start + width].astype(BF16)
        piece = matmul(back, reverse, 1, 0) * scale[:, b : b + 1]
        gain = norm * (1.0 + jnp.tanh(piece))
        gain = jnp.where((ahead >= 1) & (2 * ahead < width), gain, 0.0)
        at = (NBLK + (b + 1) % NBLK) * sub
        gain_ref[at : at + sub, :] = gain
    send = pltpu.make_async_copy(gain_ref, gain_hbm, gain_sem)
    send.start()
    token_ref[...] = jnp.zeros(token_ref.shape, F32)
    send.wait()


def prepare(order, wave, exps, traj, norm):
    levels, lats, lons = traj.shape
    waves = wave.shape[1]
    high = -(-(lons // NBLK // 2 + 1) // LOW)
    table = jax.ShapeDtypeStruct((high * LOW, waves), BF16)
    gain = jax.ShapeDtypeStruct((2 * NBLK * levels * lats, high * LOW), F32)
    vmem = pl.BlockSpec(memory_space=pltpu.VMEM)
    return pl.pallas_call(
        functools.partial(prepare_kernel, norm=norm),
        in_specs=[pl.BlockSpec(memory_space=pltpu.SMEM)] + [vmem] * 3,
        out_specs=[vmem, vmem, pl.BlockSpec(memory_space=pltpu.HBM), vmem],
        out_shape=(table, table, gain, jax.ShapeDtypeStruct((8, 128), F32)),
        scratch_shapes=[pltpu.VMEM((-(-high // 8) * 8, waves), F32)] * 2
        + [pltpu.VMEM(gain.shape, F32), pltpu.SemaphoreType.DMA],
        compiler_params=pltpu.CompilerParams(vmem_limit_bytes=16 * 2**20),
        cost_estimate=pl.CostEstimate(flops=12_000_000, bytes_accessed=20_000_000, transcendentals=0),
        name="prepare",
    )(order, wave, exps, traj)


def gather_kernel(token_ref, in_ref, out_ref, total_ref):
    sources, comps, sub, slots = in_ref.shape
    pick = one_hot(iota((8, comps * sub), 1) // 4, iota((8, comps * sub), 0))
    flat = [jnp.concatenate([in_ref[d, c] for d in range(sources)], axis=1) for c in range(comps)]
    flat = jnp.concatenate(flat, axis=0)
    out_ref[...] = flat
    total_ref[...] = matmul(pick, flat, 1, 0)


def gather_rows(token, blocks):
    sources, comps, sub, slots = blocks.shape
    vmem = pl.BlockSpec(memory_space=pltpu.VMEM)
    return pl.pallas_call(
        gather_kernel,
        in_specs=[vmem] * 2,
        out_specs=[vmem] * 2,
        out_shape=(
            jax.ShapeDtypeStruct((comps * sub, sources * slots), BF16),
            jax.ShapeDtypeStruct((comps * sub // 4, sources * slots), F32),
        ),
        compiler_params=pltpu.CompilerParams(vmem_limit_bytes=8 * 2**20),
        name="gather_rows",
    )(token, blocks)


def share_kernel(index_ref, pair_ref, share_ref, below_ref):
    core = index_ref[0] % 2
    chip = pair_ref[0] + pair_ref[1]
    below_ref[...] = pair_ref[1 - core]
    rows, waves = chip.shape
    half = waves // 2
    chip = jnp.where(core == 0, chip[: rows // 2], chip[rows // 2 :])
    share = jnp.concatenate([chip[:, :half], chip[:, half:]], axis=0).astype(BF16)
    for d in range(share_ref.shape[0]):
        share_ref[d] = share


def share_rows(index, pair, groups):
    _, rows, waves = pair.shape
    vmem = pl.BlockSpec(memory_space=pltpu.VMEM)
    return pl.pallas_call(
        share_kernel,
        in_specs=[pl.BlockSpec(memory_space=pltpu.SMEM), vmem],
        out_specs=[vmem] * 2,
        out_shape=(
            jax.ShapeDtypeStruct((groups, rows, waves // 2), BF16),
            jax.ShapeDtypeStruct((rows, waves), F32),
        ),
        compiler_params=pltpu.CompilerParams(vmem_limit_bytes=8 * 2**20),
        name="share_rows",
    )(index, pair)


def forcing_kernel(
    index_ref, coef_ref, total_ref, below_ref, four_ref, wave_ref, gain_ref, cos_ref, sin_ref,
    out_ref, held_ref, held_sem, *, norm
):
    fetch = pltpu.make_async_copy(gain_ref, held_ref, held_sem)
    fetch.start()
    me = index_ref[0]
    groups = total_ref.shape[0]
    rows, waves = below_ref.shape
    both = four_ref.shape[0]
    sub = both // 2
    wave = wave_ref[...]
    parts = []
    for c in range(2):
        part = jnp.zeros(total_ref.shape[1:], F32)
        for z in range(groups // 2):
            part = part + jnp.where(z < me // 2, total_ref[2 * z + c].astype(F32), 0.0)
        parts.append(jnp.concatenate([part[: rows // 2], part[rows // 2 :]], axis=1))
    carry = jnp.concatenate(parts, axis=0) + jnp.where(me % 2 == 1, below_ref[...], 0.0)
    four = four_ref[...]
    row, col = iota((both, both), 0), iota((both, both), 1)
    earlier = jnp.where((row // 4 == col // 4) & (col < row), 1.0, 0.0).astype(BF16)
    copies = one_hot(iota((both, rows), 0) // 4, iota((both, rows), 1))
    above = matmul(earlier, four, 1, 0) + matmul(copies, carry.astype(BF16), 1, 0)
    level = iota((both, 1), 0) % 4
    coef = jnp.zeros((both, 1), F32)
    for l in range(4):
        coef = jnp.where(level == l, coef_ref[l], coef)
    mixed = (four.astype(F32) + coef * above).astype(BF16)
    first, second = mixed[:sub], mixed[sub:]
    with_cos, with_sin = [], []
    for b in range(NBLK):
        cos_b, sin_b = (v.astype(BF16) for v in turns(wave, b))
        with_cos.append(first * cos_b - second * sin_b)
        with_sin.append(first * sin_b + second * cos_b)
    with_cos = jnp.concatenate(with_cos, axis=0)
    with_sin = jnp.concatenate(with_sin, axis=0)
    even = matmul(with_cos, cos_ref[...], 1, 1)
    odd = matmul(with_sin, sin_ref[...], 1, 1)
    half = NBLK * sub
    fetch.wait()
    ahead = held_ref[:half, :] * (even + odd)
    behind = held_ref[half:, :] * (even - odd)
    forcing = jnp.concatenate([ahead, behind], axis=0).astype(BF16)
    by_cos = matmul(forcing, cos_ref[...], 1, 0)
    by_sin = matmul(forcing, sin_ref[...], 1, 0)
    by_cos = by_cos[:half] + by_cos[half:]
    by_sin = by_sin[:half] - by_sin[half:]
    first = jnp.zeros((sub, waves), F32)
    second = jnp.zeros((sub, waves), F32)
    for b in range(NBLK):
        cos_b, sin_b = turns(wave, b)
        part_cos, part_sin = by_cos[b * sub : (b + 1) * sub], by_sin[b * sub : (b + 1) * sub]
        first = first + part_cos * cos_b + part_sin * sin_b
        second = second + part_sin * cos_b - part_cos * sin_b
    bands, comps, _, slots = out_ref.shape
    half = sub // 2
    for c, value in enumerate((first, second)):
        value = value * norm
        sym, anti = value[:half] + value[half:], value[:half] - value[half:]
        sides = jnp.concatenate([sym, anti], axis=0).astype(BF16)
        for d in range(bands):
            out_ref[d, c] = sides[:, slots * d : slots * (d + 1)]


def forcing_part(index, coef, totals, below, four, wave, gain, cos_t, sin_t, shape, norm):
    vmem = pl.BlockSpec(memory_space=pltpu.VMEM)
    smem = pl.BlockSpec(memory_space=pltpu.SMEM)
    return pl.pallas_call(
        functools.partial(forcing_kernel, norm=norm),
        in_specs=[smem] * 2 + [vmem] * 4 + [pl.BlockSpec(memory_space=pltpu.HBM)] + [vmem] * 2,
        out_specs=vmem,
        scratch_shapes=[pltpu.VMEM(gain.shape, F32), pltpu.SemaphoreType.DMA],
        out_shape=jax.ShapeDtypeStruct(shape, BF16),
        compiler_params=pltpu.CompilerParams(vmem_limit_bytes=41_943_040),
        cost_estimate=pl.CostEstimate(flops=900_000_000, bytes_accessed=8_000_000, transcendentals=0),
        name="forcing_part",
    )(index, coef, totals, below, four, wave, gain, cos_t, sin_t)


def body(adj_spec, wave_of_slot, legendre, lat_weight, traj, traj_exp, traj_order, lev_coef):
    levels, degrees = adj_spec.shape[0], adj_spec.shape[3]
    groups = lax.axis_size(("z", "core"))
    norm = 1.0 / math.sqrt(degrees)
    band = lax.axis_index("band").astype(I32)[None]
    index = lax.axis_index(("z", "core")).astype(I32)[None]
    wave = wave_of_slot[None, :]
    blocks = synthesis(adj_spec, legendre, band, wave_of_slot, lat_weight)
    blocks = lax.all_to_all(blocks, "band", split_axis=0, concat_axis=0, tiled=True)
    cos_t, sin_t, gain, token = prepare(traj_order, wave, traj_exp, traj, norm)
    four, total = gather_rows(token, blocks)
    pair = lax.all_gather(total, "core")
    shares, below = share_rows(index, pair, groups)
    totals = lax.all_to_all(shares, ("z", "core"), split_axis=0, concat_axis=0, tiled=True)
    sides = forcing_part(
        index, lev_coef, totals, below, four, wave, gain, cos_t, sin_t, blocks.shape, norm
    )
    sides = lax.all_to_all(sides, "band", split_axis=0, concat_axis=0, tiled=True)
    return analysis(sides, legendre, band, wave_of_slot, levels)


def solution(mesh):
    chips = Mesh(mesh.devices.reshape(mesh.shape["band"], -1, 2), ("band", "z", "core"))
    lev = ("z", "core")
    return jax.shard_map(
        body,
        mesh=chips,
        in_specs=(
            P(lev, "band", None, None),
            P(),
            P("band", None, None),
            P(),
            P(lev, "band", None),
            P(lev, "band", None),
            P(lev, None),
            P(lev),
        ),
        out_specs=P(lev, "band", None, None),
        check_vma=False,
    )
```

```python
import functools
import math

import jax
import jax.numpy as jnp
from jax import lax
from jax.experimental import pallas as pl
from jax.experimental.pallas import tpu as pltpu
from jax.sharding import Mesh
from jax.sharding import PartitionSpec as P

F32, BF16, I32 = jnp.float32, jnp.bfloat16, jnp.int32
GROUP = 8
CHUNK = 2
NBLK = 4
LOW = 16


def iota(shape, dim):
    return lax.broadcasted_iota(I32, shape, dim)


def matmul(a, b, ca, cb):
    return lax.dot_general(a, b, (((ca,), (cb,)), ((), ())), preferred_element_type=F32)


def one_hot(rows, cols):
    return jnp.where(rows == cols, 1.0, 0.0).astype(BF16)


def limits(band_ref, wave_ref, at, slots, comps, degrees):
    rows = GROUP * comps
    slot = iota((rows, 1), 0) // comps
    first = band_ref[0] * slots + at * GROUP
    limit = jnp.zeros((rows, 1), I32)
    for s in range(GROUP):
        limit = jnp.where(slot == s, degrees - wave_ref[first + s], limit)
    return limit


def turns(wave, b):
    turn = (wave * b) & 3
    cos_b = jnp.where(turn == 0, 1.0, jnp.where(turn == 2, -1.0, 0.0))
    sin_b = jnp.where(turn == 1, 1.0, jnp.where(turn == 3, -1.0, 0.0))
    return cos_b, sin_b


def circle(product, lon_count):
    quarter = lon_count // 4
    count = jnp.floor(product * (1.0 / quarter) + 0.5)
    angle = (product - count * quarter) * (2.0 * math.pi / lon_count)
    turn = count.astype(I32) & 3
    square = angle * angle
    cos = 1.0 + square * (-1 / 2 + square * (1 / 24 + square * (-1 / 720 + square * (1 / 40320))))
    sin = angle * (
        1.0 + square * (-1 / 6 + square * (1 / 120 + square * (-1 / 5040 + square * (1 / 362880))))
    )
    swap = (turn & 1) == 1
    near, far = jnp.where(swap, sin, cos), jnp.where(swap, cos, sin)
    near = jnp.where((turn == 1) | (turn == 2), -near, near)
    far = jnp.where(turn >= 2, -far, far)
    return near, far


def fill_tables(wave_ref, cos_ref, sin_ref, cos_high_ref, sin_high_ref, lons):
    wave = wave_ref[...].astype(F32)
    shape = (LOW, wave.shape[1])
    cos_low, sin_low = circle(iota(shape, 0).astype(F32) * wave, lons)
    shape = cos_high_ref.shape
    cos_high_ref[...], sin_high_ref[...] = circle((iota(shape, 0) * LOW).astype(F32) * wave, lons)

    @pl.loop(0, cos_ref.shape[0] // LOW)
    def _(i):
        cos_high = cos_high_ref[pl.ds(i, 1), :]
        sin_high = sin_high_ref[pl.ds(i, 1), :]
        at = pl.ds(pl.multiple_of(i * LOW, LOW), LOW)
        cos_ref[at, :] = (cos_high * cos_low - sin_high * sin_low).astype(BF16)
        sin_ref[at, :] = (-(sin_high * cos_low + cos_high * sin_low)).astype(BF16)


def fill_gain(order_ref, exp_ref, traj_ref, gain_ref, norm):
    levels, lats, lons = traj_ref.shape
    width = lons // NBLK
    sub = levels * lats
    row, col = iota((sub, sub), 0), iota((sub, sub), 1)
    held = jnp.zeros((sub, sub), I32)
    for r in range(levels):
        held = jnp.where(col // lats == r, order_ref[0, r], held)
    lat = row // 4 % 2 * 2 + row // 8
    pick = jnp.where((held == row % 4) & (col % lats == lat), 1.0, 0.0).astype(BF16)
    power = jnp.concatenate([exp_ref[r] for r in range(levels)], axis=0).astype(F32)
    scale = matmul(pick, jnp.exp2(power).astype(BF16), 1, 0)
    stored = jnp.concatenate([traj_ref[r] for r in range(levels)], axis=0)
    ordered = matmul(pick, stored, 1, 0)
    full = gain_ref.shape[1]
    ahead = iota((sub, full), 1)
    reverse = jnp.where(iota((full, full), 0) + iota((full, full), 1) == full, 1.0, 0.0).astype(BF16)
    for b in range(NBLK):
        start = b * width
        piece = ordered[:, start : start + full] * scale[:, b : b + 1]
        gain = jnp.where(ahead <= width // 2, norm * (1.0 + jnp.tanh(piece)), 0.0)
        gain_ref[b * sub : (b + 1) * sub, :] = gain
        back = ordered[:, start + width - full : start + width].astype(BF16)
        piece = matmul(back, reverse, 1, 0) * scale[:, b : b + 1]
        gain = norm * (1.0 + jnp.tanh(piece))
        gain = jnp.where((ahead >= 1) & (2 * ahead < width), gain, 0.0)
        at = (NBLK + (b + 1) % NBLK) * sub
        gain_ref[at : at + sub, :] = gain


def synthesis_kernel(
    band_ref, index_ref, wave_ref, held_ref, weight_ref, row_ref, exp_ref, traj_hbm, adj_hbm, leg_hbm,
    out_ref, leg_ref, cos_ref, sin_ref, gain_ref,
    adj_ref, traj_ref, acc_ref, spread_ref, order_ref, cos_high_ref, sin_high_ref,
    adj_sem, leg_sem, traj_sem, *, norm
):
    traj_fetch = pltpu.make_async_copy(traj_hbm, traj_ref, traj_sem)
    traj_fetch.start()
    levels, slots, comps, degrees = adj_ref.shape
    rows = GROUP * comps
    heights = leg_ref.shape[1]
    steps = slots // GROUP
    fetches = []
    for g in range(steps):
        here = pl.ds(g * GROUP, GROUP)
        fetches.append((
            pltpu.make_async_copy(adj_hbm.at[:, here], adj_ref.at[:, here], adj_sem.at[g]),
            pltpu.make_async_copy(leg_hbm.at[here], leg_ref.at[here], leg_sem.at[g]),
        ))
        for fetch in fetches[-1]:
            fetch.start()
    weight = jnp.concatenate([weight_ref[...]] * (128 // heights), axis=1)
    total = slots * comps
    col, source = iota((total, comps * 128), 1), iota((total, comps * 128), 0)
    slot = col % 128
    own = (source == slot * comps + col // 128) & (slot < slots)
    spread_ref[...] = jnp.where(own, 1.0, 0.0).astype(BF16)
    size = 2 * levels * heights
    dest, origin = iota((size, size), 1), iota((size, size), 0)
    band, e, hh, l = dest // 16, dest // 8 % 2, dest // 4 % 2, dest % 4
    order_ref[...] = one_hot((e * levels + l) * heights + band * 2 + hh, origin)
    shape = (2 * levels * rows, GROUP * heights)
    own = (iota(shape, 0) % rows) // comps == iota(shape, 1) // heights
    degree = iota((rows, degrees), 1)
    sign = jnp.where(degree % 2 == 0, 1.0, -1.0).astype(BF16)
    lane = iota((rows, 128), 1) // heights
    fill_tables(row_ref, cos_ref, sin_ref, cos_high_ref, sin_high_ref, traj_ref.shape[2])
    traj_fetch.wait()
    fill_gain(held_ref, exp_ref, traj_ref, gain_ref, norm)
    for first in range(0, steps, CHUNK):
        group = range(first, first + CHUNK)
        for g in group:
            for fetch in fetches[g]:
                fetch.wait()
        wide = []
        for g in group:
            here = pl.ds(g * GROUP, GROUP)
            limit = limits(band_ref, wave_ref, g, slots, comps, degrees)
            inside = jnp.where(degree < limit, 1.0, 0.0).astype(BF16)
            flipped = inside * sign
            values = [adj_ref[l, here].reshape(rows, degrees) for l in range(levels)]
            left = jnp.concatenate(
                [v * inside for v in values] + [v * flipped for v in values], axis=0
            )
            both = matmul(left, leg_ref[here].reshape(GROUP * heights, degrees), 1, 1)
            both = jnp.where(own, both, 0.0)
            both = both[:, :128] + both[:, 128:]
            both = both + pltpu.roll(both, 64, 1)
            both = (both + pltpu.roll(both, 32, 1)) * weight
            blocks = []
            for k in range(2 * levels // 4):
                mix = both[4 * k * rows : (4 * k + 1) * rows]
                for r in range(1, 4):
                    part = both[(4 * k + r) * rows : (4 * k + r + 1) * rows]
                    mix = jnp.where(lane == r, part, mix)
                blocks.append(mix.astype(BF16))
            wide.append(jnp.concatenate(blocks, axis=1))
        acc_ref[first * rows : (first + CHUNK) * rows, :] = jnp.concatenate(wide, axis=0)
    wide = matmul(acc_ref[...], order_ref[...], 1, 0).astype(BF16)
    moved = matmul(wide, spread_ref[...], 0, 0).astype(BF16)
    for d in range(size // 16):
        for c in range(comps):
            out_ref[d, c] = moved[16 * d : 16 * d + 16, 128 * c : 128 * c + slots]


def synthesis(adj, leg, band, index, waves, row, weight, order, exps, traj, norm):
    levels, slots, comps, degrees = adj.shape
    heights = leg.shape[1]
    lats, lons = traj.shape[1:]
    size = 2 * levels * heights
    count = waves.shape[0]
    high = -(-(lons // NBLK // 2 + 1) // LOW)
    table = jax.ShapeDtypeStruct((high * LOW, count), BF16)
    smem = pl.BlockSpec(memory_space=pltpu.SMEM)
    vmem = pl.BlockSpec(memory_space=pltpu.VMEM)
    hbm = pl.BlockSpec(memory_space=pltpu.HBM)
    return pl.pallas_call(
        functools.partial(synthesis_kernel, norm=norm),
        in_specs=[smem] * 4 + [vmem] * 3 + [hbm] * 3,
        out_specs=[vmem] * 5,
        out_shape=(
            jax.ShapeDtypeStruct((16, comps, 16, slots), BF16),
            jax.ShapeDtypeStruct(leg.shape, BF16),
            table,
            table,
            jax.ShapeDtypeStruct((2 * NBLK * levels * lats, high * LOW), F32),
        ),
        scratch_shapes=[
            pltpu.VMEM(adj.shape, BF16),
            pltpu.VMEM(traj.shape, BF16),
            pltpu.VMEM((slots * comps, size), BF16),
            pltpu.VMEM((slots * comps, comps * 128), BF16),
            pltpu.VMEM((size, size), BF16),
            pltpu.VMEM((-(-high // 8) * 8, count), F32),
            pltpu.VMEM((-(-high // 8) * 8, count), F32),
            pltpu.SemaphoreType.DMA((slots // GROUP,)),
            pltpu.SemaphoreType.DMA((slots // GROUP,)),
            pltpu.SemaphoreType.DMA,
        ],
        compiler_params=pltpu.CompilerParams(vmem_limit_bytes=40_000_000),
        name="synthesis",
    )(band, index, waves, order, weight, row, exps, traj, adj, leg)


def analysis_kernel(band_ref, wave_ref, in_ref, leg_ref, out_hbm, left_ref, out_ref, out_sem):
    slots, heights, degrees = leg_ref.shape
    levels, _, comps, _ = out_ref.shape
    sources, _, sub, _ = in_ref.shape
    rows = GROUP * comps
    kinds = 2 * levels
    steps = slots // GROUP
    size = sources * sub
    row = iota((size, kinds * 128), 0)
    col = iota((size, kinds * 128), 1)
    row_key = (row // 8 % 2 * levels + row % 4) * heights + row // 16 * 2 + row // 4 % 2
    pick = one_hot(row_key, col // 128 * heights + col % heights)
    parts = []
    for c in range(comps):
        flat = jnp.concatenate([in_ref[d, c] for d in range(sources)], axis=0)
        parts.append(matmul(flat, pick, 0, 0).astype(BF16))
    apart = jnp.concatenate(parts, axis=0)
    total = slots * comps
    weave = one_hot(
        iota((total, total), 0) % comps * slots + iota((total, total), 0) // comps,
        iota((total, total), 1),
    )
    left_ref[...] = matmul(weave, apart, 1, 0).astype(BF16)
    half = levels * rows
    sends = []
    for g in range(steps):
        here = pl.ds(g * GROUP, GROUP)
        own_rows = left_ref[g * rows : (g + 1) * rows, :]
        stack = jnp.concatenate([own_rows[:, 128 * k : 128 * k + 128] for k in range(kinds)], axis=0)
        left = jnp.concatenate([stack, stack], axis=1)
        shape = left.shape
        own = (iota(shape, 0) % rows) // comps == iota(shape, 1) // heights
        left = left * jnp.where(own, 1.0, 0.0).astype(BF16)
        both = matmul(left, leg_ref[here].reshape(GROUP * heights, degrees), 1, 0)
        limit = limits(band_ref, wave_ref, g, slots, comps, degrees)
        degree = iota((rows, degrees), 1)
        inside = degree < limit
        even = degree % 2 == 0
        for l in range(levels):
            sym = both[l * rows : (l + 1) * rows]
            anti = both[half + l * rows : half + (l + 1) * rows]
            value = jnp.where(inside, jnp.where(even, sym, anti), 0.0).astype(BF16)
            out_ref[l, here] = value.reshape(GROUP, comps, degrees)
        sends.append(pltpu.make_async_copy(out_ref.at[:, here], out_hbm.at[:, here], out_sem.at[g]))
        sends[-1].start()
    for send in sends:
        send.wait()


def analysis(sides, leg, band, waves, levels):
    sources, comps, sub, slots = sides.shape
    heights, degrees = leg.shape[1:]
    smem = pl.BlockSpec(memory_space=pltpu.SMEM)
    vmem = pl.BlockSpec(memory_space=pltpu.VMEM)
    hbm = pl.BlockSpec(memory_space=pltpu.HBM)
    shape = (levels, slots, comps, degrees)
    return pl.pallas_call(
        analysis_kernel,
        in_specs=[smem, smem, vmem, vmem],
        out_specs=hbm,
        out_shape=jax.ShapeDtypeStruct(shape, BF16),
        scratch_shapes=[
            pltpu.VMEM((slots * comps, 2 * levels * 128), BF16),
            pltpu.VMEM(shape, BF16),
            pltpu.SemaphoreType.DMA((slots // GROUP,)),
        ],
        compiler_params=pltpu.CompilerParams(vmem_limit_bytes=16 * 2**20),
        name="analysis",
    )(band, waves, sides, leg)


def gather_kernel(in_ref, out_ref, total_ref):
    sources, comps, sub, slots = in_ref.shape
    pick = one_hot(iota((8, comps * sub), 1) // 4, iota((8, comps * sub), 0))
    flat = [jnp.concatenate([in_ref[d, c] for d in range(sources)], axis=1) for c in range(comps)]
    flat = jnp.concatenate(flat, axis=0)
    out_ref[...] = flat
    total_ref[...] = matmul(pick, flat, 1, 0)


def gather_rows(blocks):
    sources, comps, sub, slots = blocks.shape
    vmem = pl.BlockSpec(memory_space=pltpu.VMEM)
    return pl.pallas_call(
        gather_kernel,
        in_specs=[vmem],
        out_specs=[vmem] * 2,
        out_shape=(
            jax.ShapeDtypeStruct((comps * sub, sources * slots), BF16),
            jax.ShapeDtypeStruct((comps * sub // 4, sources * slots), F32),
        ),
        compiler_params=pltpu.CompilerParams(vmem_limit_bytes=8 * 2**20),
        name="gather_rows",
    )(blocks)


def share_kernel(index_ref, pair_ref, share_ref, below_ref):
    core = index_ref[0] % 2
    chip = pair_ref[0] + pair_ref[1]
    below_ref[...] = pair_ref[1 - core]
    rows, waves = chip.shape
    half = waves // 2
    chip = jnp.where(core == 0, chip[: rows // 2], chip[rows // 2 :])
    share = jnp.concatenate([chip[:, :half], chip[:, half:]], axis=0).astype(BF16)
    for d in range(share_ref.shape[0]):
        share_ref[d] = share


def share_rows(index, pair, groups):
    _, rows, waves = pair.shape
    vmem = pl.BlockSpec(memory_space=pltpu.VMEM)
    return pl.pallas_call(
        share_kernel,
        in_specs=[pl.BlockSpec(memory_space=pltpu.SMEM), vmem],
        out_specs=[vmem] * 2,
        out_shape=(
            jax.ShapeDtypeStruct((groups, rows, waves // 2), BF16),
            jax.ShapeDtypeStruct((rows, waves), F32),
        ),
        compiler_params=pltpu.CompilerParams(vmem_limit_bytes=8 * 2**20),
        name="share_rows",
    )(index, pair)


def forcing_kernel(
    index_ref, coef_ref, total_ref, below_ref, four_ref, wave_ref, gain_ref, cos_ref, sin_ref,
    out_ref, *, norm
):
    me = index_ref[0]
    groups = total_ref.shape[0]
    rows, waves = below_ref.shape
    both = four_ref.shape[0]
    sub = both // 2
    wave = wave_ref[...]
    parts = []
    for c in range(2):
        part = jnp.zeros(total_ref.shape[1:], F32)
        for z in range(groups // 2):
            part = part + jnp.where(z < me // 2, total_ref[2 * z + c].astype(F32), 0.0)
        parts.append(jnp.concatenate([part[: rows // 2], part[rows // 2 :]], axis=1))
    carry = jnp.concatenate(parts, axis=0) + jnp.where(me % 2 == 1, below_ref[...], 0.0)
    four = four_ref[...]
    row, col = iota((both, both), 0), iota((both, both), 1)
    earlier = jnp.where((row // 4 == col // 4) & (col < row), 1.0, 0.0).astype(BF16)
    copies = one_hot(iota((both, rows), 0) // 4, iota((both, rows), 1))
    above = matmul(earlier, four, 1, 0) + matmul(copies, carry.astype(BF16), 1, 0)
    level = iota((both, 1), 0) % 4
    coef = jnp.zeros((both, 1), F32)
    for l in range(4):
        coef = jnp.where(level == l, coef_ref[l], coef)
    mixed = (four.astype(F32) + coef * above).astype(BF16)
    first, second = mixed[:sub], mixed[sub:]
    with_cos, with_sin = [], []
    for b in range(NBLK):
        cos_b, sin_b = (v.astype(BF16) for v in turns(wave, b))
        with_cos.append(first * cos_b - second * sin_b)
        with_sin.append(first * sin_b + second * cos_b)
    with_cos = jnp.concatenate(with_cos, axis=0)
    with_sin = jnp.concatenate(with_sin, axis=0)
    even = matmul(with_cos, cos_ref[...], 1, 1)
    odd = matmul(with_sin, sin_ref[...], 1, 1)
    half = NBLK * sub
    ahead = gain_ref[:half, :] * (even + odd)
    behind = gain_ref[half:, :] * (even - odd)
    forcing = jnp.concatenate([ahead, behind], axis=0).astype(BF16)
    by_cos = matmul(forcing, cos_ref[...], 1, 0)
    by_sin = matmul(forcing, sin_ref[...], 1, 0)
    by_cos = by_cos[:half] + by_cos[half:]
    by_sin = by_sin[:half] - by_sin[half:]
    first = jnp.zeros((sub, waves), F32)
    second = jnp.zeros((sub, waves), F32)
    for b in range(NBLK):
        cos_b, sin_b = turns(wave, b)
        part_cos, part_sin = by_cos[b * sub : (b + 1) * sub], by_sin[b * sub : (b + 1) * sub]
        first = first + part_cos * cos_b + part_sin * sin_b
        second = second + part_sin * cos_b - part_cos * sin_b
    bands, comps, _, slots = out_ref.shape
    half = sub // 2
    for c, value in enumerate((first, second)):
        value = value * norm
        sym, anti = value[:half] + value[half:], value[:half] - value[half:]
        sides = jnp.concatenate([sym, anti], axis=0).astype(BF16)
        for d in range(bands):
            out_ref[d, c] = sides[:, slots * d : slots * (d + 1)]


def forcing_part(index, coef, totals, below, four, wave, gain, cos_t, sin_t, shape, norm):
    vmem = pl.BlockSpec(memory_space=pltpu.VMEM)
    smem = pl.BlockSpec(memory_space=pltpu.SMEM)
    return pl.pallas_call(
        functools.partial(forcing_kernel, norm=norm),
        in_specs=[smem] * 2 + [vmem] * 7,
        out_specs=vmem,
        out_shape=jax.ShapeDtypeStruct(shape, BF16),
        compiler_params=pltpu.CompilerParams(vmem_limit_bytes=32 * 2**20),
        cost_estimate=pl.CostEstimate(flops=900_000_000, bytes_accessed=8_000_000, transcendentals=0),
        name="forcing_part",
    )(index, coef, totals, below, four, wave, gain, cos_t, sin_t)


def body(adj_spec, wave_of_slot, legendre, lat_weight, traj, traj_exp, traj_order, lev_coef):
    levels, degrees = adj_spec.shape[0], adj_spec.shape[3]
    groups = lax.axis_size(("z", "core"))
    norm = 1.0 / math.sqrt(degrees)
    band = lax.axis_index("band").astype(I32)[None]
    index = lax.axis_index(("z", "core")).astype(I32)[None]
    wave = wave_of_slot[None, :]
    adj_spec, table, traj, traj_exp, traj_order, lev_coef, wave_of_slot, weight = (
        pltpu.with_memory_space_constraint(v, pltpu.HBM)
        for v in (
            adj_spec, legendre, traj, traj_exp, traj_order, lev_coef, wave_of_slot, lat_weight[None, :]
        )
    )
    blocks, table, cos_t, sin_t, gain = synthesis(
        adj_spec, table, band, index, wave_of_slot, wave, weight, traj_order, traj_exp, traj, norm
    )
    blocks = lax.all_to_all(blocks, "band", split_axis=0, concat_axis=0, tiled=True)
    four, total = gather_rows(blocks)
    pair = lax.all_gather(total, "core")
    shares, below = share_rows(index, pair, groups)
    totals = lax.all_to_all(shares, ("z", "core"), split_axis=0, concat_axis=0, tiled=True)
    sides = forcing_part(
        index, lev_coef, totals, below, four, wave, gain, cos_t, sin_t, blocks.shape, norm
    )
    sides = lax.all_to_all(sides, "band", split_axis=0, concat_axis=0, tiled=True)
    return analysis(sides, table, band, wave_of_slot, levels)


def solution(mesh):
    chips = Mesh(mesh.devices.reshape(mesh.shape["band"], -1, 2), ("band", "z", "core"))
    lev = ("z", "core")
    return jax.shard_map(
        body,
        mesh=chips,
        in_specs=(
            P(lev, "band", None, None),
            P(),
            P("band", None, None),
            P(),
            P(lev, "band", None),
            P(lev, "band", None),
            P(lev, None),
            P(lev),
        ),
        out_specs=P(lev, "band", None, None),
        check_vma=False,
    )
```

```python
import functools
import math

import jax
import jax.numpy as jnp
from jax import lax
from jax.experimental import pallas as pl
from jax.experimental.pallas import tpu as pltpu
from jax.sharding import Mesh
from jax.sharding import PartitionSpec as P

F32, BF16, I32 = jnp.float32, jnp.bfloat16, jnp.int32
GROUP = 8
CHUNK = 10
NBLK = 4
LOW = 16


def iota(shape, dim):
    return lax.broadcasted_iota(I32, shape, dim)


def matmul(a, b, ca, cb):
    return lax.dot_general(a, b, (((ca,), (cb,)), ((), ())), preferred_element_type=F32)


def one_hot(rows, cols):
    return jnp.where(rows == cols, 1.0, 0.0).astype(BF16)


def limits(band_ref, wave_ref, at, slots, comps, degrees):
    rows = GROUP * comps
    slot = iota((rows, 1), 0) // comps
    first = band_ref[0] * slots + at * GROUP
    limit = jnp.zeros((rows, 1), I32)
    for s in range(GROUP):
        limit = jnp.where(slot == s, degrees - wave_ref[first + s], limit)
    return limit


def turns(wave, b):
    turn = (wave * b) & 3
    cos_b = jnp.where(turn == 0, 1.0, jnp.where(turn == 2, -1.0, 0.0))
    sin_b = jnp.where(turn == 1, 1.0, jnp.where(turn == 3, -1.0, 0.0))
    return cos_b, sin_b


def circle(product, lon_count):
    quarter = lon_count // 4
    count = jnp.floor(product * (1.0 / quarter) + 0.5)
    angle = (product - count * quarter) * (2.0 * math.pi / lon_count)
    turn = count.astype(I32) & 3
    square = angle * angle
    cos = 1.0 + square * (-1 / 2 + square * (1 / 24 + square * (-1 / 720 + square * (1 / 40320))))
    sin = angle * (
        1.0 + square * (-1 / 6 + square * (1 / 120 + square * (-1 / 5040 + square * (1 / 362880))))
    )
    swap = (turn & 1) == 1
    near, far = jnp.where(swap, sin, cos), jnp.where(swap, cos, sin)
    near = jnp.where((turn == 1) | (turn == 2), -near, near)
    far = jnp.where(turn >= 2, -far, far)
    return near, far


def fill_tables(wave_ref, cos_ref, sin_ref, cos_high_ref, sin_high_ref, lons):
    wave = wave_ref[...][None, :].astype(F32)
    shape = (LOW, wave.shape[1])
    cos_low, sin_low = circle(iota(shape, 0).astype(F32) * wave, lons)
    shape = cos_high_ref.shape
    cos_high_ref[...], sin_high_ref[...] = circle((iota(shape, 0) * LOW).astype(F32) * wave, lons)

    @pl.loop(0, cos_ref.shape[0] // LOW)
    def _(i):
        cos_high = cos_high_ref[pl.ds(i, 1), :]
        sin_high = sin_high_ref[pl.ds(i, 1), :]
        at = pl.ds(pl.multiple_of(i * LOW, LOW), LOW)
        cos_ref[at, :] = (cos_high * cos_low - sin_high * sin_low).astype(BF16)
        sin_ref[at, :] = (-(sin_high * cos_low + cos_high * sin_low)).astype(BF16)


def fill_gain(order_ref, exp_ref, traj_ref, gain_ref, norm):
    levels, lats, lons = traj_ref.shape
    width = lons // NBLK
    sub = levels * lats
    row, col = iota((sub, sub), 0), iota((sub, sub), 1)
    held = jnp.zeros((sub, sub), I32)
    for r in range(levels):
        held = jnp.where(col // lats == r, order_ref[0, r], held)
    lat = row // 4 % 2 * 2 + row // 8
    pick = jnp.where((held == row % 4) & (col % lats == lat), 1.0, 0.0).astype(BF16)
    power = jnp.concatenate([exp_ref[r] for r in range(levels)], axis=0).astype(F32)
    scale = matmul(pick, jnp.exp2(power).astype(BF16), 1, 0)
    stored = jnp.concatenate([traj_ref[r] for r in range(levels)], axis=0)
    ordered = matmul(pick, stored, 1, 0)
    full = gain_ref.shape[1]
    ahead = iota((sub, full), 1)
    reverse = jnp.where(iota((full, full), 0) + iota((full, full), 1) == full, 1.0, 0.0).astype(BF16)
    back = [ordered[:, (b + 1) * width - full : (b + 1) * width] for b in range(NBLK)]
    back = matmul(jnp.concatenate(back, axis=0).astype(BF16), reverse, 1, 0)
    for b in range(NBLK):
        start = b * width
        piece = ordered[:, start : start + full] * scale[:, b : b + 1]
        gain = jnp.where(ahead <= width // 2, norm * (1.0 + jnp.tanh(piece)), 0.0)
        gain_ref[b * sub : (b + 1) * sub, :] = gain
        piece = back[b * sub : (b + 1) * sub] * scale[:, b : b + 1]
        gain = norm * (1.0 + jnp.tanh(piece))
        gain = jnp.where((ahead >= 1) & (2 * ahead < width), gain, 0.0)
        at = (NBLK + (b + 1) % NBLK) * sub
        gain_ref[at : at + sub, :] = gain


def synthesis_kernel(
    band_ref, index_ref, wave_ref, held_ref, weight_ref, row_ref, exp_ref, traj_hbm, adj_hbm, leg_hbm,
    out_ref, leg_ref, cos_ref, sin_ref, gain_ref,
    adj_ref, traj_ref, acc_ref, spread_ref, order_ref, cos_high_ref, sin_high_ref,
    adj_sem, leg_sem, traj_sem, *, norm
):
    traj_fetch = pltpu.make_async_copy(traj_hbm, traj_ref, traj_sem)
    traj_fetch.start()
    levels, slots, comps, degrees = adj_ref.shape
    rows = GROUP * comps
    heights = leg_ref.shape[1]
    steps = slots // GROUP
    fetches = []
    for g in range(steps):
        here = pl.ds(g * GROUP, GROUP)
        fetches.append((
            pltpu.make_async_copy(adj_hbm.at[:, here], adj_ref.at[:, here], adj_sem.at[g]),
            pltpu.make_async_copy(leg_hbm.at[here], leg_ref.at[here], leg_sem.at[g]),
        ))
        for fetch in fetches[-1]:
            fetch.start()
    weight = jnp.concatenate([weight_ref[...]] * (128 // heights), axis=1)
    total = slots * comps
    col, source = iota((total, comps * 128), 1), iota((total, comps * 128), 0)
    slot = col % 128
    own = (source == slot * comps + col // 128) & (slot < slots)
    spread_ref[...] = jnp.where(own, 1.0, 0.0).astype(BF16)
    size = 2 * levels * heights
    dest, origin = iota((size, size), 1), iota((size, size), 0)
    band, e, hh, l = dest // 16, dest // 8 % 2, dest // 4 % 2, dest % 4
    order_ref[...] = one_hot((e * levels + l) * heights + band * 2 + hh, origin)
    shape = (2 * levels * rows, GROUP * heights)
    own = (iota(shape, 0) % rows) // comps == iota(shape, 1) // heights
    degree = iota((rows, degrees), 1)
    sign = jnp.where(degree % 2 == 0, 1.0, -1.0).astype(BF16)
    lane = iota((rows, 128), 1) // heights
    fill_tables(row_ref, cos_ref, sin_ref, cos_high_ref, sin_high_ref, traj_ref.shape[2])
    traj_fetch.wait()
    fill_gain(held_ref, exp_ref, traj_ref, gain_ref, norm)
    for first in range(0, steps, CHUNK):
        group = range(first, first + CHUNK)
        for g in group:
            for fetch in fetches[g]:
                fetch.wait()
        wide = []
        for g in group:
            here = pl.ds(g * GROUP, GROUP)
            limit = limits(band_ref, wave_ref, g, slots, comps, degrees)
            inside = jnp.where(degree < limit, 1.0, 0.0).astype(BF16)
            flipped = inside * sign
            values = [adj_ref[l, here].reshape(rows, degrees) for l in range(levels)]
            left = jnp.concatenate(
                [v * inside for v in values] + [v * flipped for v in values], axis=0
            )
            both = matmul(left, leg_ref[here].reshape(GROUP * heights, degrees), 1, 1)
            both = jnp.where(own, both, 0.0)
            both = both[:, :128] + both[:, 128:]
            both = both + pltpu.roll(both, 64, 1)
            both = (both + pltpu.roll(both, 32, 1)) * weight
            blocks = []
            for k in range(2 * levels // 4):
                mix = both[4 * k * rows : (4 * k + 1) * rows]
                for r in range(1, 4):
                    part = both[(4 * k + r) * rows : (4 * k + r + 1) * rows]
                    mix = jnp.where(lane == r, part, mix)
                blocks.append(mix.astype(BF16))
            wide.append(jnp.concatenate(blocks, axis=1))
        acc_ref[first * rows : (first + CHUNK) * rows, :] = jnp.concatenate(wide, axis=0)
    wide = matmul(acc_ref[...], order_ref[...], 1, 0).astype(BF16)
    moved = matmul(wide, spread_ref[...], 0, 0).astype(BF16)
    for d in range(size // 16):
        for c in range(comps):
            out_ref[d, c] = moved[16 * d : 16 * d + 16, 128 * c : 128 * c + slots]


def synthesis(adj, leg, band, index, waves, weight, order, exps, traj, norm):
    levels, slots, comps, degrees = adj.shape
    heights = leg.shape[1]
    lats, lons = traj.shape[1:]
    size = 2 * levels * heights
    count = waves.shape[0]
    high = -(-(lons // NBLK // 2 + 1) // LOW)
    table = jax.ShapeDtypeStruct((high * LOW, count), BF16)
    smem = pl.BlockSpec(memory_space=pltpu.SMEM)
    vmem = pl.BlockSpec(memory_space=pltpu.VMEM)
    hbm = pl.BlockSpec(memory_space=pltpu.HBM)
    return pl.pallas_call(
        functools.partial(synthesis_kernel, norm=norm),
        in_specs=[smem] * 4 + [vmem] * 3 + [hbm] * 3,
        out_specs=[vmem] * 5,
        out_shape=(
            jax.ShapeDtypeStruct((16, comps, 16, slots), BF16),
            jax.ShapeDtypeStruct(leg.shape, BF16),
            table,
            table,
            jax.ShapeDtypeStruct((2 * NBLK * levels * lats, high * LOW), F32),
        ),
        scratch_shapes=[
            pltpu.VMEM(adj.shape, BF16),
            pltpu.VMEM(traj.shape, BF16),
            pltpu.VMEM((slots * comps, size), BF16),
            pltpu.VMEM((slots * comps, comps * 128), BF16),
            pltpu.VMEM((size, size), BF16),
            pltpu.VMEM((-(-high // 8) * 8, count), F32),
            pltpu.VMEM((-(-high // 8) * 8, count), F32),
            pltpu.SemaphoreType.DMA((slots // GROUP,)),
            pltpu.SemaphoreType.DMA((slots // GROUP,)),
            pltpu.SemaphoreType.DMA,
        ],
        compiler_params=pltpu.CompilerParams(vmem_limit_bytes=40_000_000),
        name="synthesis",
    )(band, index, waves, order, weight, waves, exps, traj, adj, leg)


def analysis_kernel(band_ref, wave_ref, in_ref, leg_ref, out_hbm, left_ref, out_ref, out_sem):
    slots, heights, degrees = leg_ref.shape
    levels, _, comps, _ = out_ref.shape
    sources, _, sub, _ = in_ref.shape
    rows = GROUP * comps
    kinds = 2 * levels
    steps = slots // GROUP
    size = sources * sub
    row = iota((size, kinds * 128), 0)
    col = iota((size, kinds * 128), 1)
    row_key = (row // 8 % 2 * levels + row % 4) * heights + row // 16 * 2 + row // 4 % 2
    pick = one_hot(row_key, col // 128 * heights + col % heights)
    parts = []
    for c in range(comps):
        flat = jnp.concatenate([in_ref[d, c] for d in range(sources)], axis=0)
        parts.append(matmul(flat, pick, 0, 0).astype(BF16))
    apart = jnp.concatenate(parts, axis=0)
    total = slots * comps
    weave = one_hot(
        iota((total, total), 0) % comps * slots + iota((total, total), 0) // comps,
        iota((total, total), 1),
    )
    left_ref[...] = matmul(weave, apart, 1, 0).astype(BF16)
    half = levels * rows
    sends = []
    for g in range(steps):
        here = pl.ds(g * GROUP, GROUP)
        own_rows = left_ref[g * rows : (g + 1) * rows, :]
        stack = jnp.concatenate([own_rows[:, 128 * k : 128 * k + 128] for k in range(kinds)], axis=0)
        left = jnp.concatenate([stack, stack], axis=1)
        shape = left.shape
        own = (iota(shape, 0) % rows) // comps == iota(shape, 1) // heights
        left = left * jnp.where(own, 1.0, 0.0).astype(BF16)
        both = matmul(left, leg_ref[here].reshape(GROUP * heights, degrees), 1, 0)
        limit = limits(band_ref, wave_ref, g, slots, comps, degrees)
        degree = iota((rows, degrees), 1)
        inside = degree < limit
        even = degree % 2 == 0
        for l in range(levels):
            sym = both[l * rows : (l + 1) * rows]
            anti = both[half + l * rows : half + (l + 1) * rows]
            value = jnp.where(inside, jnp.where(even, sym, anti), 0.0).astype(BF16)
            out_ref[l, here] = value.reshape(GROUP, comps, degrees)
        sends.append(pltpu.make_async_copy(out_ref.at[:, here], out_hbm.at[:, here], out_sem.at[g]))
        sends[-1].start()
    for send in sends:
        send.wait()


def analysis(sides, leg, band, waves, levels):
    sources, comps, sub, slots = sides.shape
    heights, degrees = leg.shape[1:]
    smem = pl.BlockSpec(memory_space=pltpu.SMEM)
    vmem = pl.BlockSpec(memory_space=pltpu.VMEM)
    hbm = pl.BlockSpec(memory_space=pltpu.HBM)
    shape = (levels, slots, comps, degrees)
    return pl.pallas_call(
        analysis_kernel,
        in_specs=[smem, smem, vmem, vmem],
        out_specs=hbm,
        out_shape=jax.ShapeDtypeStruct(shape, BF16),
        scratch_shapes=[
            pltpu.VMEM((slots * comps, 2 * levels * 128), BF16),
            pltpu.VMEM(shape, BF16),
            pltpu.SemaphoreType.DMA((slots // GROUP,)),
        ],
        compiler_params=pltpu.CompilerParams(vmem_limit_bytes=16 * 2**20),
        name="analysis",
    )(band, waves, sides, leg)


def gather_kernel(in_ref, out_ref, total_ref):
    sources, comps, sub, slots = in_ref.shape
    pick = one_hot(iota((8, comps * sub), 1) // 4, iota((8, comps * sub), 0))
    flat = [jnp.concatenate([in_ref[d, c] for d in range(sources)], axis=1) for c in range(comps)]
    flat = jnp.concatenate(flat, axis=0)
    out_ref[...] = flat
    total_ref[...] = matmul(pick, flat, 1, 0)


def gather_rows(blocks):
    sources, comps, sub, slots = blocks.shape
    vmem = pl.BlockSpec(memory_space=pltpu.VMEM)
    return pl.pallas_call(
        gather_kernel,
        in_specs=[vmem],
        out_specs=[vmem] * 2,
        out_shape=(
            jax.ShapeDtypeStruct((comps * sub, sources * slots), BF16),
            jax.ShapeDtypeStruct((comps * sub // 4, sources * slots), F32),
        ),
        compiler_params=pltpu.CompilerParams(vmem_limit_bytes=8 * 2**20),
        name="gather_rows",
    )(blocks)


def share_kernel(index_ref, pair_ref, share_ref, below_ref):
    core = index_ref[0] % 2
    chip = pair_ref[0] + pair_ref[1]
    below_ref[...] = pair_ref[1 - core]
    rows, waves = chip.shape
    half = waves // 2
    chip = jnp.where(core == 0, chip[: rows // 2], chip[rows // 2 :])
    share = jnp.concatenate([chip[:, :half], chip[:, half:]], axis=0).astype(BF16)
    for d in range(share_ref.shape[0]):
        share_ref[d] = share


def share_rows(index, pair, groups):
    _, rows, waves = pair.shape
    vmem = pl.BlockSpec(memory_space=pltpu.VMEM)
    return pl.pallas_call(
        share_kernel,
        in_specs=[pl.BlockSpec(memory_space=pltpu.SMEM), vmem],
        out_specs=[vmem] * 2,
        out_shape=(
            jax.ShapeDtypeStruct((groups, rows, waves // 2), BF16),
            jax.ShapeDtypeStruct((rows, waves), F32),
        ),
        compiler_params=pltpu.CompilerParams(vmem_limit_bytes=8 * 2**20),
        name="share_rows",
    )(index, pair)


def forcing_kernel(
    index_ref, coef_ref, total_ref, below_ref, four_ref, wave_ref, gain_ref, cos_ref, sin_ref,
    out_ref, *, norm
):
    me = index_ref[0]
    groups = total_ref.shape[0]
    rows, waves = below_ref.shape
    both = four_ref.shape[0]
    sub = both // 2
    wave = wave_ref[...][None, :]
    parts = []
    for c in range(2):
        part = jnp.zeros(total_ref.shape[1:], F32)
        for z in range(groups // 2):
            part = part + jnp.where(z < me // 2, total_ref[2 * z + c].astype(F32), 0.0)
        parts.append(jnp.concatenate([part[: rows // 2], part[rows // 2 :]], axis=1))
    carry = jnp.concatenate(parts, axis=0) + jnp.where(me % 2 == 1, below_ref[...], 0.0)
    four = four_ref[...]
    row, col = iota((both, both), 0), iota((both, both), 1)
    earlier = jnp.where((row // 4 == col // 4) & (col < row), 1.0, 0.0).astype(BF16)
    copies = one_hot(iota((both, rows), 0) // 4, iota((both, rows), 1))
    above = matmul(earlier, four, 1, 0) + matmul(copies, carry.astype(BF16), 1, 0)
    level = iota((both, 1), 0) % 4
    coef = jnp.zeros((both, 1), F32)
    for l in range(4):
        coef = jnp.where(level == l, coef_ref[l], coef)
    mixed = (four.astype(F32) + coef * above).astype(BF16)
    first, second = mixed[:sub], mixed[sub:]
    with_cos, with_sin = [], []
    for b in range(NBLK):
        cos_b, sin_b = (v.astype(BF16) for v in turns(wave, b))
        with_cos.append(first * cos_b - second * sin_b)
        with_sin.append(first * sin_b + second * cos_b)
    with_cos = jnp.concatenate(with_cos, axis=0)
    with_sin = jnp.concatenate(with_sin, axis=0)
    even = matmul(with_cos, cos_ref[...], 1, 1)
    odd = matmul(with_sin, sin_ref[...], 1, 1)
    half = NBLK * sub
    ahead = gain_ref[:half, :] * (even + odd)
    behind = gain_ref[half:, :] * (even - odd)
    forcing = jnp.concatenate([ahead, behind], axis=0).astype(BF16)
    by_cos = matmul(forcing, cos_ref[...], 1, 0)
    by_sin = matmul(forcing, sin_ref[...], 1, 0)
    by_cos = by_cos[:half] + by_cos[half:]
    by_sin = by_sin[:half] - by_sin[half:]
    first = jnp.zeros((sub, waves), F32)
    second = jnp.zeros((sub, waves), F32)
    for b in range(NBLK):
        cos_b, sin_b = turns(wave, b)
        part_cos, part_sin = by_cos[b * sub : (b + 1) * sub], by_sin[b * sub : (b + 1) * sub]
        first = first + part_cos * cos_b + part_sin * sin_b
        second = second + part_sin * cos_b - part_cos * sin_b
    bands, comps, _, slots = out_ref.shape
    half = sub // 2
    for c, value in enumerate((first, second)):
        value = value * norm
        sym, anti = value[:half] + value[half:], value[:half] - value[half:]
        sides = jnp.concatenate([sym, anti], axis=0).astype(BF16)
        for d in range(bands):
            out_ref[d, c] = sides[:, slots * d : slots * (d + 1)]


def forcing_part(index, coef, totals, below, four, wave, gain, cos_t, sin_t, shape, norm):
    vmem = pl.BlockSpec(memory_space=pltpu.VMEM)
    smem = pl.BlockSpec(memory_space=pltpu.SMEM)
    return pl.pallas_call(
        functools.partial(forcing_kernel, norm=norm),
        in_specs=[smem] * 2 + [vmem] * 7,
        out_specs=vmem,
        out_shape=jax.ShapeDtypeStruct(shape, BF16),
        compiler_params=pltpu.CompilerParams(vmem_limit_bytes=32 * 2**20),
        cost_estimate=pl.CostEstimate(flops=900_000_000, bytes_accessed=8_000_000, transcendentals=0),
        name="forcing_part",
    )(index, coef, totals, below, four, wave, gain, cos_t, sin_t)


def body(adj_spec, wave_of_slot, legendre, lat_weight, traj, traj_exp, traj_order, lev_coef):
    levels, degrees = adj_spec.shape[0], adj_spec.shape[3]
    groups = lax.axis_size(("z", "core"))
    norm = 1.0 / math.sqrt(degrees)
    band = lax.axis_index("band").astype(I32)[None]
    index = lax.axis_index(("z", "core")).astype(I32)[None]
    adj_spec, table, traj, traj_exp, traj_order, lev_coef, wave_of_slot, weight = (
        pltpu.with_memory_space_constraint(v, pltpu.HBM)
        for v in (
            adj_spec, legendre, traj, traj_exp, traj_order, lev_coef, wave_of_slot, lat_weight[None, :]
        )
    )
    blocks, table, cos_t, sin_t, gain = synthesis(
        adj_spec, table, band, index, wave_of_slot, weight, traj_order, traj_exp, traj, norm
    )
    blocks = lax.all_to_all(blocks, "band", split_axis=0, concat_axis=0, tiled=True)
    four, total = gather_rows(blocks)
    pair = lax.all_gather(total, "core")
    shares, below = share_rows(index, pair, groups)
    totals = lax.all_to_all(shares, ("z", "core"), split_axis=0, concat_axis=0, tiled=True)
    sides = forcing_part(
        index, lev_coef, totals, below, four, wave_of_slot, gain, cos_t, sin_t, blocks.shape, norm
    )
    sides = lax.all_to_all(sides, "band", split_axis=0, concat_axis=0, tiled=True)
    return analysis(sides, table, band, wave_of_slot, levels)


def solution(mesh):
    chips = Mesh(mesh.devices.reshape(mesh.shape["band"], -1, 2), ("band", "z", "core"))
    lev = ("z", "core")
    return jax.shard_map(
        body,
        mesh=chips,
        in_specs=(
            P(lev, "band", None, None),
            P(),
            P("band", None, None),
            P(),
            P(lev, "band", None),
            P(lev, "band", None),
            P(lev, None),
            P(lev),
        ),
        out_specs=P(lev, "band", None, None),
        check_vma=False,
    )
```

```python
import functools
import math

import jax
import jax.numpy as jnp
from jax import lax
from jax.experimental import pallas as pl
from jax.experimental.pallas import tpu as pltpu
from jax.sharding import Mesh
from jax.sharding import PartitionSpec as P

F32, BF16, I32 = jnp.float32, jnp.bfloat16, jnp.int32
GROUP = 8
CUTS = (0, 10)
NBLK = 4
LOW = 16


def iota(shape, dim):
    return lax.broadcasted_iota(I32, shape, dim)


def matmul(a, b, ca, cb):
    return lax.dot_general(a, b, (((ca,), (cb,)), ((), ())), preferred_element_type=F32)


def one_hot(rows, cols):
    return jnp.where(rows == cols, 1.0, 0.0).astype(BF16)


def limits(band_ref, wave_ref, at, slots, comps, degrees):
    rows = GROUP * comps
    slot = iota((rows, 1), 0) // comps
    first = band_ref[0] * slots + at * GROUP
    limit = jnp.zeros((rows, 1), I32)
    for s in range(GROUP):
        limit = jnp.where(slot == s, degrees - wave_ref[first + s], limit)
    return limit


def turns(wave, b):
    turn = (wave * b) & 3
    cos_b = jnp.where(turn == 0, 1.0, jnp.where(turn == 2, -1.0, 0.0))
    sin_b = jnp.where(turn == 1, 1.0, jnp.where(turn == 3, -1.0, 0.0))
    return cos_b, sin_b


def circle(product, lon_count):
    quarter = lon_count // 4
    count = jnp.floor(product * (1.0 / quarter) + 0.5)
    angle = (product - count * quarter) * (2.0 * math.pi / lon_count)
    turn = count.astype(I32) & 3
    square = angle * angle
    cos = 1.0 + square * (-1 / 2 + square * (1 / 24 + square * (-1 / 720 + square * (1 / 40320))))
    sin = angle * (
        1.0 + square * (-1 / 6 + square * (1 / 120 + square * (-1 / 5040 + square * (1 / 362880))))
    )
    swap = (turn & 1) == 1
    near, far = jnp.where(swap, sin, cos), jnp.where(swap, cos, sin)
    near = jnp.where((turn == 1) | (turn == 2), -near, near)
    far = jnp.where(turn >= 2, -far, far)
    return near, far


def fill_tables(wave_ref, cos_ref, sin_ref, cos_high_ref, sin_high_ref, lons):
    wave = wave_ref[...][None, :].astype(F32)
    shape = (LOW, wave.shape[1])
    cos_low, sin_low = circle(iota(shape, 0).astype(F32) * wave, lons)
    shape = cos_high_ref.shape
    cos_high_ref[...], sin_high_ref[...] = circle((iota(shape, 0) * LOW).astype(F32) * wave, lons)

    @pl.loop(0, cos_ref.shape[0] // LOW)
    def _(i):
        cos_high = cos_high_ref[pl.ds(i, 1), :]
        sin_high = sin_high_ref[pl.ds(i, 1), :]
        at = pl.ds(pl.multiple_of(i * LOW, LOW), LOW)
        cos_ref[at, :] = (cos_high * cos_low - sin_high * sin_low).astype(BF16)
        sin_ref[at, :] = (-(sin_high * cos_low + cos_high * sin_low)).astype(BF16)


def fill_gain(order_ref, exp_ref, traj_ref, gain_ref, norm):
    levels, lats, lons = traj_ref.shape
    width = lons // NBLK
    sub = levels * lats
    row, col = iota((sub, sub), 0), iota((sub, sub), 1)
    held = jnp.zeros((sub, sub), I32)
    for r in range(levels):
        held = jnp.where(col // lats == r, order_ref[0, r], held)
    lat = row // 4 % 2 * 2 + row // 8
    pick = jnp.where((held == row % 4) & (col % lats == lat), 1.0, 0.0).astype(BF16)
    power = jnp.concatenate([exp_ref[r] for r in range(levels)], axis=0).astype(F32)
    scale = matmul(pick, jnp.exp2(power).astype(BF16), 1, 0)
    stored = jnp.concatenate([traj_ref[r] for r in range(levels)], axis=0)
    ordered = matmul(pick, stored, 1, 0)
    full = gain_ref.shape[1]
    ahead = iota((sub, full), 1)
    reverse = jnp.where(iota((full, full), 0) + iota((full, full), 1) == full, 1.0, 0.0).astype(BF16)
    back = [ordered[:, (b + 1) * width - full : (b + 1) * width] for b in range(NBLK)]
    back = matmul(jnp.concatenate(back, axis=0).astype(BF16), reverse, 1, 0)
    for b in range(NBLK):
        start = b * width
        piece = ordered[:, start : start + full] * scale[:, b : b + 1]
        gain = jnp.where(ahead <= width // 2, norm * (1.0 + jnp.tanh(piece)), 0.0)
        gain_ref[b * sub : (b + 1) * sub, :] = gain
        piece = back[b * sub : (b + 1) * sub] * scale[:, b : b + 1]
        gain = norm * (1.0 + jnp.tanh(piece))
        gain = jnp.where((ahead >= 1) & (2 * ahead < width), gain, 0.0)
        at = (NBLK + (b + 1) % NBLK) * sub
        gain_ref[at : at + sub, :] = gain


def synthesis_kernel(
    band_ref, index_ref, wave_ref, held_ref, weight_ref, row_ref, exp_ref, traj_hbm, adj_hbm, leg_hbm,
    out_ref, leg_ref, cos_ref, sin_ref, gain_ref, pick_ref, weave_ref,
    adj_ref, traj_ref, acc_ref, spread_ref, order_ref, cos_high_ref, sin_high_ref,
    adj_sem, leg_sem, traj_sem, *, norm
):
    traj_fetch = pltpu.make_async_copy(traj_hbm, traj_ref, traj_sem)
    traj_fetch.start()
    levels, slots, comps, degrees = adj_ref.shape
    rows = GROUP * comps
    heights = leg_ref.shape[1]
    steps = slots // GROUP
    fetches = []
    for g in range(steps):
        here = pl.ds(g * GROUP, GROUP)
        fetches.append((
            pltpu.make_async_copy(adj_hbm.at[:, here], adj_ref.at[:, here], adj_sem.at[g]),
            pltpu.make_async_copy(leg_hbm.at[here], leg_ref.at[here], leg_sem.at[g]),
        ))
        for fetch in fetches[-1]:
            fetch.start()
    weight = jnp.concatenate([weight_ref[...]] * (128 // heights), axis=1)
    total = slots * comps
    col, source = iota((total, comps * 128), 1), iota((total, comps * 128), 0)
    slot = col % 128
    own = (source == slot * comps + col // 128) & (slot < slots)
    spread_ref[...] = jnp.where(own, 1.0, 0.0).astype(BF16)
    row, col = iota(pick_ref.shape, 0), iota(pick_ref.shape, 1)
    row = (row // 8 % 2 * levels + row % 4) * heights + row // 16 * 2 + row // 4 % 2
    pick_ref[...] = one_hot(row, col // 128 * heights + col % heights)
    row, col = iota(weave_ref.shape, 0), iota(weave_ref.shape, 1)
    weave_ref[...] = one_hot(row % comps * slots + row // comps, col)
    size = 2 * levels * heights
    dest, origin = iota((size, size), 1), iota((size, size), 0)
    band, e, hh, l = dest // 16, dest // 8 % 2, dest // 4 % 2, dest % 4
    order_ref[...] = one_hot((e * levels + l) * heights + band * 2 + hh, origin)
    shape = (2 * levels * rows, GROUP * heights)
    own = (iota(shape, 0) % rows) // comps == iota(shape, 1) // heights
    degree = iota((rows, degrees), 1)
    sign = jnp.where(degree % 2 == 0, 1.0, -1.0).astype(BF16)
    lane = iota((rows, 128), 1) // heights
    fill_tables(row_ref, cos_ref, sin_ref, cos_high_ref, sin_high_ref, traj_ref.shape[2])
    traj_fetch.wait()
    fill_gain(held_ref, exp_ref, traj_ref, gain_ref, norm)
    for first, last in zip(CUTS, CUTS[1:]):
        group = range(first, last)
        for g in group:
            for fetch in fetches[g]:
                fetch.wait()
        wide = []
        for g in group:
            here = pl.ds(g * GROUP, GROUP)
            limit = limits(band_ref, wave_ref, g, slots, comps, degrees)
            inside = jnp.where(degree < limit, 1.0, 0.0).astype(BF16)
            flipped = inside * sign
            values = [adj_ref[l, here].reshape(rows, degrees) for l in range(levels)]
            left = jnp.concatenate(
                [v * inside for v in values] + [v * flipped for v in values], axis=0
            )
            both = matmul(left, leg_ref[here].reshape(GROUP * heights, degrees), 1, 1)
            both = jnp.where(own, both, 0.0)
            both = both[:, :128] + both[:, 128:]
            both = both + pltpu.roll(both, 64, 1)
            both = (both + pltpu.roll(both, 32, 1)) * weight
            blocks = []
            for k in range(2 * levels // 4):
                mix = both[4 * k * rows : (4 * k + 1) * rows]
                for r in range(1, 4):
                    part = both[(4 * k + r) * rows : (4 * k + r + 1) * rows]
                    mix = jnp.where(lane == r, part, mix)
                blocks.append(mix.astype(BF16))
            wide.append(jnp.concatenate(blocks, axis=1))
        acc_ref[first * rows : last * rows, :] = jnp.concatenate(wide, axis=0)
    wide = matmul(acc_ref[...], order_ref[...], 1, 0).astype(BF16)
    moved = matmul(wide, spread_ref[...], 0, 0).astype(BF16)
    for d in range(size // 16):
        for c in range(comps):
            out_ref[d, c] = moved[16 * d : 16 * d + 16, 128 * c : 128 * c + slots]


def synthesis(adj, leg, band, index, waves, weight, order, exps, traj, norm):
    levels, slots, comps, degrees = adj.shape
    heights = leg.shape[1]
    lats, lons = traj.shape[1:]
    size = 2 * levels * heights
    count = waves.shape[0]
    high = -(-(lons // NBLK // 2 + 1) // LOW)
    table = jax.ShapeDtypeStruct((high * LOW, count), BF16)
    smem = pl.BlockSpec(memory_space=pltpu.SMEM)
    vmem = pl.BlockSpec(memory_space=pltpu.VMEM)
    hbm = pl.BlockSpec(memory_space=pltpu.HBM)
    return pl.pallas_call(
        functools.partial(synthesis_kernel, norm=norm),
        in_specs=[smem] * 4 + [vmem] * 3 + [hbm] * 3,
        out_specs=[vmem] * 7,
        out_shape=(
            jax.ShapeDtypeStruct((16, comps, 16, slots), BF16),
            jax.ShapeDtypeStruct(leg.shape, BF16),
            table,
            table,
            jax.ShapeDtypeStruct((2 * NBLK * levels * lats, high * LOW), F32),
            jax.ShapeDtypeStruct((16 * 16, 2 * levels * 128), BF16),
            jax.ShapeDtypeStruct((slots * comps, slots * comps), BF16),
        ),
        scratch_shapes=[
            pltpu.VMEM(adj.shape, BF16),
            pltpu.VMEM(traj.shape, BF16),
            pltpu.VMEM((slots * comps, size), BF16),
            pltpu.VMEM((slots * comps, comps * 128), BF16),
            pltpu.VMEM((size, size), BF16),
            pltpu.VMEM((-(-high // 8) * 8, count), F32),
            pltpu.VMEM((-(-high // 8) * 8, count), F32),
            pltpu.SemaphoreType.DMA((slots // GROUP,)),
            pltpu.SemaphoreType.DMA((slots // GROUP,)),
            pltpu.SemaphoreType.DMA,
        ],
        compiler_params=pltpu.CompilerParams(vmem_limit_bytes=40_000_000),
        name="synthesis",
    )(band, index, waves, order, weight, waves, exps, traj, adj, leg)


def analysis_kernel(
    band_ref, wave_ref, in_ref, pick_ref, weave_ref, leg_ref, out_hbm, left_ref, out_ref, out_sem
):
    slots, heights, degrees = leg_ref.shape
    levels, _, comps, _ = out_ref.shape
    sources, _, sub, _ = in_ref.shape
    rows = GROUP * comps
    kinds = 2 * levels
    steps = slots // GROUP
    parts = []
    for c in range(comps):
        flat = jnp.concatenate([in_ref[d, c] for d in range(sources)], axis=0)
        parts.append(matmul(flat, pick_ref[...], 0, 0).astype(BF16))
    apart = jnp.concatenate(parts, axis=0)
    left_ref[...] = matmul(weave_ref[...], apart, 1, 0).astype(BF16)
    half = levels * rows
    sends = []
    for g in range(steps):
        here = pl.ds(g * GROUP, GROUP)
        own_rows = left_ref[g * rows : (g + 1) * rows, :]
        stack = jnp.concatenate([own_rows[:, 128 * k : 128 * k + 128] for k in range(kinds)], axis=0)
        left = jnp.concatenate([stack, stack], axis=1)
        shape = left.shape
        own = (iota(shape, 0) % rows) // comps == iota(shape, 1) // heights
        left = left * jnp.where(own, 1.0, 0.0).astype(BF16)
        both = matmul(left, leg_ref[here].reshape(GROUP * heights, degrees), 1, 0)
        limit = limits(band_ref, wave_ref, g, slots, comps, degrees)
        degree = iota((rows, degrees), 1)
        inside = degree < limit
        even = degree % 2 == 0
        for l in range(levels):
            sym = both[l * rows : (l + 1) * rows]
            anti = both[half + l * rows : half + (l + 1) * rows]
            value = jnp.where(inside, jnp.where(even, sym, anti), 0.0).astype(BF16)
            out_ref[l, here] = value.reshape(GROUP, comps, degrees)
        sends.append(pltpu.make_async_copy(out_ref.at[:, here], out_hbm.at[:, here], out_sem.at[g]))
        sends[-1].start()
    for send in sends:
        send.wait()


def analysis(sides, pick, weave, leg, band, waves, levels):
    sources, comps, sub, slots = sides.shape
    heights, degrees = leg.shape[1:]
    smem = pl.BlockSpec(memory_space=pltpu.SMEM)
    vmem = pl.BlockSpec(memory_space=pltpu.VMEM)
    hbm = pl.BlockSpec(memory_space=pltpu.HBM)
    shape = (levels, slots, comps, degrees)
    return pl.pallas_call(
        analysis_kernel,
        in_specs=[smem, smem] + [vmem] * 4,
        out_specs=hbm,
        out_shape=jax.ShapeDtypeStruct(shape, BF16),
        scratch_shapes=[
            pltpu.VMEM((slots * comps, 2 * levels * 128), BF16),
            pltpu.VMEM(shape, BF16),
            pltpu.SemaphoreType.DMA((slots // GROUP,)),
        ],
        compiler_params=pltpu.CompilerParams(vmem_limit_bytes=16 * 2**20),
        name="analysis",
    )(band, waves, sides, pick, weave, leg)


def gather_kernel(in_ref, out_ref, share_ref):
    sources, comps, sub, slots = in_ref.shape
    pick = one_hot(iota((8, comps * sub), 1) // 4, iota((8, comps * sub), 0))
    flat = [jnp.concatenate([in_ref[d, c] for d in range(sources)], axis=1) for c in range(comps)]
    flat = jnp.concatenate(flat, axis=0)
    out_ref[...] = flat
    total = matmul(pick, flat, 1, 0).astype(BF16)
    for d in range(share_ref.shape[0]):
        share_ref[d] = total


def gather_rows(blocks, groups):
    sources, comps, sub, slots = blocks.shape
    vmem = pl.BlockSpec(memory_space=pltpu.VMEM)
    return pl.pallas_call(
        gather_kernel,
        in_specs=[vmem],
        out_specs=[vmem] * 2,
        out_shape=(
            jax.ShapeDtypeStruct((comps * sub, sources * slots), BF16),
            jax.ShapeDtypeStruct((groups, comps * sub // 4, sources * slots), BF16),
        ),
        compiler_params=pltpu.CompilerParams(vmem_limit_bytes=8 * 2**20),
        name="gather_rows",
    )(blocks)


def forcing_kernel(
    index_ref, coef_ref, total_ref, four_ref, wave_ref, gain_ref, cos_ref, sin_ref,
    out_ref, *, norm
):
    me = index_ref[0]
    groups, rows, waves = total_ref.shape
    both = four_ref.shape[0]
    sub = both // 2
    wave = wave_ref[...][None, :]
    carry = jnp.zeros((rows, waves), F32)
    for g in range(groups):
        carry = carry + jnp.where(g < me, total_ref[g].astype(F32), 0.0)
    four = four_ref[...]
    row, col = iota((both, both), 0), iota((both, both), 1)
    earlier = jnp.where((row // 4 == col // 4) & (col < row), 1.0, 0.0).astype(BF16)
    copies = one_hot(iota((both, rows), 0) // 4, iota((both, rows), 1))
    above = matmul(earlier, four, 1, 0) + matmul(copies, carry.astype(BF16), 1, 0)
    level = iota((both, 1), 0) % 4
    coef = jnp.zeros((both, 1), F32)
    for l in range(4):
        coef = jnp.where(level == l, coef_ref[l], coef)
    mixed = (four.astype(F32) + coef * above).astype(BF16)
    first, second = mixed[:sub], mixed[sub:]
    with_cos, with_sin = [], []
    for b in range(NBLK):
        cos_b, sin_b = (v.astype(BF16) for v in turns(wave, b))
        with_cos.append(first * cos_b - second * sin_b)
        with_sin.append(first * sin_b + second * cos_b)
    with_cos = jnp.concatenate(with_cos, axis=0)
    with_sin = jnp.concatenate(with_sin, axis=0)
    even = matmul(with_cos, cos_ref[...], 1, 1)
    odd = matmul(with_sin, sin_ref[...], 1, 1)
    half = NBLK * sub
    ahead = gain_ref[:half, :] * (even + odd)
    behind = gain_ref[half:, :] * (even - odd)
    forcing = jnp.concatenate([ahead, behind], axis=0).astype(BF16)
    by_cos = matmul(forcing, cos_ref[...], 1, 0)
    by_sin = matmul(forcing, sin_ref[...], 1, 0)
    by_cos = by_cos[:half] + by_cos[half:]
    by_sin = by_sin[:half] - by_sin[half:]
    first = jnp.zeros((sub, waves), F32)
    second = jnp.zeros((sub, waves), F32)
    for b in range(NBLK):
        cos_b, sin_b = turns(wave, b)
        part_cos, part_sin = by_cos[b * sub : (b + 1) * sub], by_sin[b * sub : (b + 1) * sub]
        first = first + part_cos * cos_b + part_sin * sin_b
        second = second + part_sin * cos_b - part_cos * sin_b
    bands, comps, _, slots = out_ref.shape
    half = sub // 2
    for c, value in enumerate((first, second)):
        value = value * norm
        sym, anti = value[:half] + value[half:], value[:half] - value[half:]
        sides = jnp.concatenate([sym, anti], axis=0).astype(BF16)
        for d in range(bands):
            out_ref[d, c] = sides[:, slots * d : slots * (d + 1)]


def forcing_part(index, coef, totals, four, wave, gain, cos_t, sin_t, shape, norm):
    vmem = pl.BlockSpec(memory_space=pltpu.VMEM)
    smem = pl.BlockSpec(memory_space=pltpu.SMEM)
    return pl.pallas_call(
        functools.partial(forcing_kernel, norm=norm),
        in_specs=[smem] * 2 + [vmem] * 6,
        out_specs=vmem,
        out_shape=jax.ShapeDtypeStruct(shape, BF16),
        compiler_params=pltpu.CompilerParams(vmem_limit_bytes=32 * 2**20),
        cost_estimate=pl.CostEstimate(flops=900_000_000, bytes_accessed=8_000_000, transcendentals=0),
        name="forcing_part",
    )(index, coef, totals, four, wave, gain, cos_t, sin_t)


def body(adj_spec, wave_of_slot, legendre, lat_weight, traj, traj_exp, traj_order, lev_coef):
    levels, degrees = adj_spec.shape[0], adj_spec.shape[3]
    groups = lax.axis_size(("z", "core"))
    norm = 1.0 / math.sqrt(degrees)
    band = lax.axis_index("band").astype(I32)[None]
    index = lax.axis_index(("z", "core")).astype(I32)[None]
    adj_spec, table, traj, traj_exp, traj_order, lev_coef, wave_of_slot, weight = (
        pltpu.with_memory_space_constraint(v, pltpu.HBM)
        for v in (
            adj_spec, legendre, traj, traj_exp, traj_order, lev_coef, wave_of_slot, lat_weight[None, :]
        )
    )
    blocks, table, cos_t, sin_t, gain, pick, weave = synthesis(
        adj_spec, table, band, index, wave_of_slot, weight, traj_order, traj_exp, traj, norm
    )
    blocks = lax.all_to_all(blocks, "band", split_axis=0, concat_axis=0, tiled=True)
    four, shares = gather_rows(blocks, groups)
    totals = lax.all_to_all(shares, ("z", "core"), split_axis=0, concat_axis=0, tiled=True)
    sides = forcing_part(
        index, lev_coef, totals, four, wave_of_slot, gain, cos_t, sin_t, blocks.shape, norm
    )
    sides = lax.all_to_all(sides, "band", split_axis=0, concat_axis=0, tiled=True)
    return analysis(sides, pick, weave, table, band, wave_of_slot, levels)


def solution(mesh):
    chips = Mesh(mesh.devices.reshape(mesh.shape["band"], -1, 2), ("band", "z", "core"))
    lev = ("z", "core")
    return jax.shard_map(
        body,
        mesh=chips,
        in_specs=(
            P(lev, "band", None, None),
            P(),
            P("band", None, None),
            P(),
            P(lev, "band", None),
            P(lev, "band", None),
            P(lev, None),
            P(lev),
        ),
        out_specs=P(lev, "band", None, None),
        check_vma=False,
    )
```

```python
import functools
import math

import jax
import jax.numpy as jnp
from jax import lax
from jax.experimental import pallas as pl
from jax.experimental.pallas import tpu as pltpu
from jax.sharding import Mesh
from jax.sharding import PartitionSpec as P

F32, BF16, I32 = jnp.float32, jnp.bfloat16, jnp.int32
GROUP = 8
CHUNK = 10
NBLK = 4
LOW = 16


def iota(shape, dim):
    return lax.broadcasted_iota(I32, shape, dim)


def matmul(a, b, ca, cb):
    return lax.dot_general(a, b, (((ca,), (cb,)), ((), ())), preferred_element_type=F32)


def one_hot(rows, cols):
    return jnp.where(rows == cols, 1.0, 0.0).astype(BF16)


def limits(band_ref, wave_ref, at, slots, comps, degrees):
    rows = GROUP * comps
    slot = iota((rows, 1), 0) // comps
    first = band_ref[0] * slots + at * GROUP
    limit = jnp.zeros((rows, 1), I32)
    for s in range(GROUP):
        limit = jnp.where(slot == s, degrees - wave_ref[first + s], limit)
    return limit


def turns(wave, b):
    turn = (wave * b) & 3
    cos_b = jnp.where(turn == 0, 1.0, jnp.where(turn == 2, -1.0, 0.0))
    sin_b = jnp.where(turn == 1, 1.0, jnp.where(turn == 3, -1.0, 0.0))
    return cos_b, sin_b


def circle(product, lon_count):
    quarter = lon_count // 4
    count = jnp.floor(product * (1.0 / quarter) + 0.5)
    angle = (product - count * quarter) * (2.0 * math.pi / lon_count)
    turn = count.astype(I32) & 3
    square = angle * angle
    cos = 1.0 + square * (-1 / 2 + square * (1 / 24 + square * (-1 / 720 + square * (1 / 40320))))
    sin = angle * (
        1.0 + square * (-1 / 6 + square * (1 / 120 + square * (-1 / 5040 + square * (1 / 362880))))
    )
    swap = (turn & 1) == 1
    near, far = jnp.where(swap, sin, cos), jnp.where(swap, cos, sin)
    near = jnp.where((turn == 1) | (turn == 2), -near, near)
    far = jnp.where(turn >= 2, -far, far)
    return near, far


def fill_tables(wave_ref, cos_ref, sin_ref, cos_high_ref, sin_high_ref, lons):
    wave = wave_ref[...][None, :].astype(F32)
    shape = (LOW, wave.shape[1])
    cos_low, sin_low = circle(iota(shape, 0).astype(F32) * wave, lons)
    shape = cos_high_ref.shape
    cos_high_ref[...], sin_high_ref[...] = circle((iota(shape, 0) * LOW).astype(F32) * wave, lons)

    @pl.loop(0, cos_ref.shape[0] // LOW)
    def _(i):
        cos_high = cos_high_ref[pl.ds(i, 1), :]
        sin_high = sin_high_ref[pl.ds(i, 1), :]
        at = pl.ds(pl.multiple_of(i * LOW, LOW), LOW)
        cos_ref[at, :] = (cos_high * cos_low - sin_high * sin_low).astype(BF16)
        sin_ref[at, :] = (-(sin_high * cos_low + cos_high * sin_low)).astype(BF16)


def fill_gain(order_ref, exp_ref, traj_ref, gain_ref, norm):
    levels, lats, lons = traj_ref.shape
    width = lons // NBLK
    sub = levels * lats
    row, col = iota((sub, sub), 0), iota((sub, sub), 1)
    held = jnp.zeros((sub, sub), I32)
    for r in range(levels):
        held = jnp.where(col // lats == r, order_ref[0, r], held)
    lat = row // 4 % 2 * 2 + row // 8
    pick = jnp.where((held == row % 4) & (col % lats == lat), 1.0, 0.0).astype(BF16)
    power = jnp.concatenate([exp_ref[r] for r in range(levels)], axis=0).astype(F32)
    scale = matmul(pick, jnp.exp2(power).astype(BF16), 1, 0)
    stored = jnp.concatenate([traj_ref[r] for r in range(levels)], axis=0)
    ordered = matmul(pick, stored, 1, 0)
    full = gain_ref.shape[1]
    ahead = iota((sub, full), 1)
    reverse = jnp.where(iota((full, full), 0) + iota((full, full), 1) == full, 1.0, 0.0).astype(BF16)
    back = [ordered[:, (b + 1) * width - full : (b + 1) * width] for b in range(NBLK)]
    back = matmul(jnp.concatenate(back, axis=0).astype(BF16), reverse, 1, 0)
    for b in range(NBLK):
        start = b * width
        piece = ordered[:, start : start + full] * scale[:, b : b + 1]
        gain = jnp.where(ahead <= width // 2, norm * (1.0 + jnp.tanh(piece)), 0.0)
        gain_ref[b * sub : (b + 1) * sub, :] = gain
        piece = back[b * sub : (b + 1) * sub] * scale[:, b : b + 1]
        gain = norm * (1.0 + jnp.tanh(piece))
        gain = jnp.where((ahead >= 1) & (2 * ahead < width), gain, 0.0)
        at = (NBLK + (b + 1) % NBLK) * sub
        gain_ref[at : at + sub, :] = gain


def synthesis_kernel(
    band_ref, index_ref, wave_ref, held_ref, weight_ref, row_ref, exp_ref, traj_hbm, adj_hbm, leg_hbm,
    out_ref, leg_ref, cos_ref, sin_ref, gain_ref,
    adj_ref, traj_ref, acc_ref, spread_ref, order_ref, cos_high_ref, sin_high_ref,
    adj_sem, leg_sem, traj_sem, *, norm
):
    traj_fetch = pltpu.make_async_copy(traj_hbm, traj_ref, traj_sem)
    traj_fetch.start()
    levels, slots, comps, degrees = adj_ref.shape
    rows = GROUP * comps
    heights = leg_ref.shape[1]
    steps = slots // GROUP
    fetches = []
    for g in range(steps):
        here = pl.ds(g * GROUP, GROUP)
        fetches.append((
            pltpu.make_async_copy(adj_hbm.at[:, here], adj_ref.at[:, here], adj_sem.at[g]),
            pltpu.make_async_copy(leg_hbm.at[here], leg_ref.at[here], leg_sem.at[g]),
        ))
        for fetch in fetches[-1]:
            fetch.start()
    weight = jnp.concatenate([weight_ref[...]] * (128 // heights), axis=1)
    total = slots * comps
    col, source = iota((total, comps * 128), 1), iota((total, comps * 128), 0)
    slot = col % 128
    own = (source == slot * comps + col // 128) & (slot < slots)
    spread_ref[...] = jnp.where(own, 1.0, 0.0).astype(BF16)
    size = 2 * levels * heights
    dest, origin = iota((size, size), 1), iota((size, size), 0)
    band, e, hh, l = dest // 16, dest // 8 % 2, dest // 4 % 2, dest % 4
    order_ref[...] = one_hot((e * levels + l) * heights + band * 2 + hh, origin)
    shape = (2 * levels * rows, GROUP * heights)
    own = (iota(shape, 0) % rows) // comps == iota(shape, 1) // heights
    degree = iota((rows, degrees), 1)
    sign = jnp.where(degree % 2 == 0, 1.0, -1.0).astype(BF16)
    lane = iota((rows, 128), 1) // heights
    fill_tables(row_ref, cos_ref, sin_ref, cos_high_ref, sin_high_ref, traj_ref.shape[2])
    traj_fetch.wait()
    fill_gain(held_ref, exp_ref, traj_ref, gain_ref, norm)
    for first in range(0, steps, CHUNK):
        group = range(first, first + CHUNK)
        for g in group:
            for fetch in fetches[g]:
                fetch.wait()
        wide = []
        for g in group:
            here = pl.ds(g * GROUP, GROUP)
            limit = limits(band_ref, wave_ref, g, slots, comps, degrees)
            inside = jnp.where(degree < limit, 1.0, 0.0).astype(BF16)
            flipped = inside * sign
            values = [adj_ref[l, here].reshape(rows, degrees) for l in range(levels)]
            left = jnp.concatenate(
                [v * inside for v in values] + [v * flipped for v in values], axis=0
            )
            both = matmul(left, leg_ref[here].reshape(GROUP * heights, degrees), 1, 1)
            both = jnp.where(own, both, 0.0)
            both = both[:, :128] + both[:, 128:]
            both = both + pltpu.roll(both, 64, 1)
            both = (both + pltpu.roll(both, 32, 1)) * weight
            blocks = []
            for k in range(2 * levels // 4):
                mix = both[4 * k * rows : (4 * k + 1) * rows]
                for r in range(1, 4):
                    part = both[(4 * k + r) * rows : (4 * k + r + 1) * rows]
                    mix = jnp.where(lane == r, part, mix)
                blocks.append(mix.astype(BF16))
            wide.append(jnp.concatenate(blocks, axis=1))
        acc_ref[first * rows : (first + CHUNK) * rows, :] = jnp.concatenate(wide, axis=0)
    wide = matmul(acc_ref[...], order_ref[...], 1, 0).astype(BF16)
    moved = matmul(wide, spread_ref[...], 0, 0).astype(BF16)
    for d in range(size // 16):
        for c in range(comps):
            out_ref[d, c] = moved[16 * d : 16 * d + 16, 128 * c : 128 * c + slots]


def synthesis(adj, leg, band, index, waves, weight, order, exps, traj, norm):
    levels, slots, comps, degrees = adj.shape
    heights = leg.shape[1]
    lats, lons = traj.shape[1:]
    size = 2 * levels * heights
    count = waves.shape[0]
    high = -(-(lons // NBLK // 2 + 1) // LOW)
    table = jax.ShapeDtypeStruct((high * LOW, count), BF16)
    smem = pl.BlockSpec(memory_space=pltpu.SMEM)
    vmem = pl.BlockSpec(memory_space=pltpu.VMEM)
    hbm = pl.BlockSpec(memory_space=pltpu.HBM)
    return pl.pallas_call(
        functools.partial(synthesis_kernel, norm=norm),
        in_specs=[smem] * 4 + [vmem] * 3 + [hbm] * 3,
        out_specs=[vmem] * 5,
        out_shape=(
            jax.ShapeDtypeStruct((16, comps, 16, slots), BF16),
            jax.ShapeDtypeStruct(leg.shape, BF16),
            table,
            table,
            jax.ShapeDtypeStruct((2 * NBLK * levels * lats, high * LOW), F32),
        ),
        scratch_shapes=[
            pltpu.VMEM(adj.shape, BF16),
            pltpu.VMEM(traj.shape, BF16),
            pltpu.VMEM((slots * comps, size), BF16),
            pltpu.VMEM((slots * comps, comps * 128), BF16),
            pltpu.VMEM((size, size), BF16),
            pltpu.VMEM((-(-high // 8) * 8, count), F32),
            pltpu.VMEM((-(-high // 8) * 8, count), F32),
            pltpu.SemaphoreType.DMA((slots // GROUP,)),
            pltpu.SemaphoreType.DMA((slots // GROUP,)),
            pltpu.SemaphoreType.DMA,
        ],
        compiler_params=pltpu.CompilerParams(vmem_limit_bytes=40_000_000),
        name="synthesis",
    )(band, index, waves, order, weight, waves, exps, traj, adj, leg)


def analysis_kernel(band_ref, wave_ref, in_ref, leg_ref, out_hbm, left_ref, out_ref, out_sem):
    slots, heights, degrees = leg_ref.shape
    levels, _, comps, _ = out_ref.shape
    sources, _, sub, _ = in_ref.shape
    rows = GROUP * comps
    kinds = 2 * levels
    steps = slots // GROUP
    size = sources * sub
    row = iota((size, kinds * 128), 0)
    col = iota((size, kinds * 128), 1)
    row_key = (row // 8 % 2 * levels + row % 4) * heights + row // 16 * 2 + row // 4 % 2
    pick = one_hot(row_key, col // 128 * heights + col % heights)
    parts = []
    for c in range(comps):
        flat = jnp.concatenate([in_ref[d, c] for d in range(sources)], axis=0)
        parts.append(matmul(flat, pick, 0, 0).astype(BF16))
    apart = jnp.concatenate(parts, axis=0)
    total = slots * comps
    weave = one_hot(
        iota((total, total), 0) % comps * slots + iota((total, total), 0) // comps,
        iota((total, total), 1),
    )
    left_ref[...] = matmul(weave, apart, 1, 0).astype(BF16)
    half = levels * rows
    sends = []
    for g in range(steps):
        here = pl.ds(g * GROUP, GROUP)
        own_rows = left_ref[g * rows : (g + 1) * rows, :]
        stack = jnp.concatenate([own_rows[:, 128 * k : 128 * k + 128] for k in range(kinds)], axis=0)
        left = jnp.concatenate([stack, stack], axis=1)
        shape = left.shape
        own = (iota(shape, 0) % rows) // comps == iota(shape, 1) // heights
        left = left * jnp.where(own, 1.0, 0.0).astype(BF16)
        both = matmul(left, leg_ref[here].reshape(GROUP * heights, degrees), 1, 0)
        limit = limits(band_ref, wave_ref, g, slots, comps, degrees)
        degree = iota((rows, degrees), 1)
        inside = degree < limit
        even = degree % 2 == 0
        for l in range(levels):
            sym = both[l * rows : (l + 1) * rows]
            anti = both[half + l * rows : half + (l + 1) * rows]
            value = jnp.where(inside, jnp.where(even, sym, anti), 0.0).astype(BF16)
            out_ref[l, here] = value.reshape(GROUP, comps, degrees)
        sends.append(pltpu.make_async_copy(out_ref.at[:, here], out_hbm.at[:, here], out_sem.at[g]))
        sends[-1].start()
    for send in sends:
        send.wait()


def analysis(sides, leg, band, waves, levels):
    sources, comps, sub, slots = sides.shape
    heights, degrees = leg.shape[1:]
    smem = pl.BlockSpec(memory_space=pltpu.SMEM)
    vmem = pl.BlockSpec(memory_space=pltpu.VMEM)
    hbm = pl.BlockSpec(memory_space=pltpu.HBM)
    shape = (levels, slots, comps, degrees)
    return pl.pallas_call(
        analysis_kernel,
        in_specs=[smem, smem, vmem, vmem],
        out_specs=hbm,
        out_shape=jax.ShapeDtypeStruct(shape, BF16),
        scratch_shapes=[
            pltpu.VMEM((slots * comps, 2 * levels * 128), BF16),
            pltpu.VMEM(shape, BF16),
            pltpu.SemaphoreType.DMA((slots // GROUP,)),
        ],
        compiler_params=pltpu.CompilerParams(vmem_limit_bytes=16 * 2**20),
        name="analysis",
    )(band, waves, sides, leg)


def gather_kernel(in_ref, out_ref, total_ref):
    sources, comps, sub, slots = in_ref.shape
    pick = one_hot(iota((8, comps * sub), 1) // 4, iota((8, comps * sub), 0))
    flat = [jnp.concatenate([in_ref[d, c] for d in range(sources)], axis=1) for c in range(comps)]
    flat = jnp.concatenate(flat, axis=0)
    out_ref[...] = flat
    total_ref[...] = matmul(pick, flat, 1, 0)


def gather_rows(blocks):
    sources, comps, sub, slots = blocks.shape
    vmem = pl.BlockSpec(memory_space=pltpu.VMEM)
    return pl.pallas_call(
        gather_kernel,
        in_specs=[vmem],
        out_specs=[vmem] * 2,
        out_shape=(
            jax.ShapeDtypeStruct((comps * sub, sources * slots), BF16),
            jax.ShapeDtypeStruct((comps * sub // 4, sources * slots), F32),
        ),
        compiler_params=pltpu.CompilerParams(vmem_limit_bytes=8 * 2**20),
        name="gather_rows",
    )(blocks)


def share_kernel(index_ref, total_ref, below_ref, share_ref):
    chip = total_ref[...] + below_ref[...]
    rows, waves = chip.shape
    half = waves // 2
    chip = jnp.where(index_ref[0] % 2 == 0, chip[: rows // 2], chip[rows // 2 :])
    share = jnp.concatenate([chip[:, :half], chip[:, half:]], axis=0).astype(BF16)
    for d in range(share_ref.shape[0]):
        share_ref[d] = share


def share_rows(index, total, below, groups):
    rows, waves = total.shape
    vmem = pl.BlockSpec(memory_space=pltpu.VMEM)
    return pl.pallas_call(
        share_kernel,
        in_specs=[pl.BlockSpec(memory_space=pltpu.SMEM), vmem, vmem],
        out_specs=vmem,
        out_shape=jax.ShapeDtypeStruct((groups, rows, waves // 2), BF16),
        compiler_params=pltpu.CompilerParams(vmem_limit_bytes=8 * 2**20),
        name="share_rows",
    )(index, total, below)


def forcing_kernel(
    index_ref, coef_ref, total_ref, below_ref, four_ref, wave_ref, gain_ref, cos_ref, sin_ref,
    out_ref, *, norm
):
    me = index_ref[0]
    groups = total_ref.shape[0]
    rows, waves = below_ref.shape
    both = four_ref.shape[0]
    sub = both // 2
    wave = wave_ref[...][None, :]
    parts = []
    for c in range(2):
        part = jnp.zeros(total_ref.shape[1:], F32)
        for z in range(groups // 2):
            part = part + jnp.where(z < me // 2, total_ref[2 * z + c].astype(F32), 0.0)
        parts.append(jnp.concatenate([part[: rows // 2], part[rows // 2 :]], axis=1))
    carry = jnp.concatenate(parts, axis=0) + jnp.where(me % 2 == 1, below_ref[...], 0.0)
    four = four_ref[...]
    row, col = iota((both, both), 0), iota((both, both), 1)
    earlier = jnp.where((row // 4 == col // 4) & (col < row), 1.0, 0.0).astype(BF16)
    copies = one_hot(iota((both, rows), 0) // 4, iota((both, rows), 1))
    above = matmul(earlier, four, 1, 0) + matmul(copies, carry.astype(BF16), 1, 0)
    level = iota((both, 1), 0) % 4
    coef = jnp.zeros((both, 1), F32)
    for l in range(4):
        coef = jnp.where(level == l, coef_ref[l], coef)
    mixed = (four.astype(F32) + coef * above).astype(BF16)
    first, second = mixed[:sub], mixed[sub:]
    with_cos, with_sin = [], []
    for b in range(NBLK):
        cos_b, sin_b = (v.astype(BF16) for v in turns(wave, b))
        with_cos.append(first * cos_b - second * sin_b)
        with_sin.append(first * sin_b + second * cos_b)
    with_cos = jnp.concatenate(with_cos, axis=0)
    with_sin = jnp.concatenate(with_sin, axis=0)
    even = matmul(with_cos, cos_ref[...], 1, 1)
    odd = matmul(with_sin, sin_ref[...], 1, 1)
    half = NBLK * sub
    ahead = gain_ref[:half, :] * (even + odd)
    behind = gain_ref[half:, :] * (even - odd)
    forcing = jnp.concatenate([ahead, behind], axis=0).astype(BF16)
    by_cos = matmul(forcing, cos_ref[...], 1, 0)
    by_sin = matmul(forcing, sin_ref[...], 1, 0)
    by_cos = by_cos[:half] + by_cos[half:]
    by_sin = by_sin[:half] - by_sin[half:]
    first = jnp.zeros((sub, waves), F32)
    second = jnp.zeros((sub, waves), F32)
    for b in range(NBLK):
        cos_b, sin_b = turns(wave, b)
        part_cos, part_sin = by_cos[b * sub : (b + 1) * sub], by_sin[b * sub : (b + 1) * sub]
        first = first + part_cos * cos_b + part_sin * sin_b
        second = second + part_sin * cos_b - part_cos * sin_b
    bands, comps, _, slots = out_ref.shape
    half = sub // 2
    for c, value in enumerate((first, second)):
        value = value * norm
        sym, anti = value[:half] + value[half:], value[:half] - value[half:]
        sides = jnp.concatenate([sym, anti], axis=0).astype(BF16)
        for d in range(bands):
            out_ref[d, c] = sides[:, slots * d : slots * (d + 1)]


def forcing_part(index, coef, totals, below, four, wave, gain, cos_t, sin_t, shape, norm):
    vmem = pl.BlockSpec(memory_space=pltpu.VMEM)
    smem = pl.BlockSpec(memory_space=pltpu.SMEM)
    return pl.pallas_call(
        functools.partial(forcing_kernel, norm=norm),
        in_specs=[smem] * 2 + [vmem] * 7,
        out_specs=vmem,
        out_shape=jax.ShapeDtypeStruct(shape, BF16),
        compiler_params=pltpu.CompilerParams(vmem_limit_bytes=32 * 2**20),
        cost_estimate=pl.CostEstimate(flops=900_000_000, bytes_accessed=8_000_000, transcendentals=0),
        name="forcing_part",
    )(index, coef, totals, below, four, wave, gain, cos_t, sin_t)


def body(adj_spec, wave_of_slot, legendre, lat_weight, traj, traj_exp, traj_order, lev_coef):
    levels, degrees = adj_spec.shape[0], adj_spec.shape[3]
    groups = lax.axis_size(("z", "core"))
    norm = 1.0 / math.sqrt(degrees)
    band = lax.axis_index("band").astype(I32)[None]
    index = lax.axis_index(("z", "core")).astype(I32)[None]
    adj_spec, table, traj, traj_exp, traj_order, lev_coef, wave_of_slot, weight = (
        pltpu.with_memory_space_constraint(v, pltpu.HBM)
        for v in (
            adj_spec, legendre, traj, traj_exp, traj_order, lev_coef, wave_of_slot, lat_weight[None, :]
        )
    )
    blocks, table, cos_t, sin_t, gain = synthesis(
        adj_spec, table, band, index, wave_of_slot, weight, traj_order, traj_exp, traj, norm
    )
    blocks = lax.all_to_all(blocks, "band", split_axis=0, concat_axis=0, tiled=True)
    four, total = gather_rows(blocks)
    below = lax.ppermute(total, "core", [(0, 1), (1, 0)])
    shares = share_rows(index, total, below, groups)
    totals = lax.all_to_all(shares, ("z", "core"), split_axis=0, concat_axis=0, tiled=True)
    sides = forcing_part(
        index, lev_coef, totals, below, four, wave_of_slot, gain, cos_t, sin_t, blocks.shape, norm
    )
    sides = lax.all_to_all(sides, "band", split_axis=0, concat_axis=0, tiled=True)
    return analysis(sides, table, band, wave_of_slot, levels)


def solution(mesh):
    chips = Mesh(mesh.devices.reshape(mesh.shape["band"], -1, 2), ("band", "z", "core"))
    lev = ("z", "core")
    return jax.shard_map(
        body,
        mesh=chips,
        in_specs=(
            P(lev, "band", None, None),
            P(),
            P("band", None, None),
            P(),
            P(lev, "band", None),
            P(lev, "band", None),
            P(lev, None),
            P(lev),
        ),
        out_specs=P(lev, "band", None, None),
        check_vma=False,
    )
```

```python
import functools
import math

import jax
import jax.numpy as jnp
from jax import lax
from jax.experimental import pallas as pl
from jax.experimental.pallas import tpu as pltpu
from jax.sharding import Mesh
from jax.sharding import PartitionSpec as P

F32, BF16, I32 = jnp.float32, jnp.bfloat16, jnp.int32
GROUP = 8
CHUNK = 10
NBLK = 4
LOW = 16


def iota(shape, dim):
    return lax.broadcasted_iota(I32, shape, dim)


def matmul(a, b, ca, cb):
    return lax.dot_general(a, b, (((ca,), (cb,)), ((), ())), preferred_element_type=F32)


def one_hot(rows, cols):
    return jnp.where(rows == cols, 1.0, 0.0).astype(BF16)


def limits(band_ref, wave_ref, at, slots, comps, degrees):
    rows = GROUP * comps
    slot = iota((rows, 1), 0) // comps
    first = band_ref[0] * slots + at * GROUP
    limit = jnp.zeros((rows, 1), I32)
    for s in range(GROUP):
        limit = jnp.where(slot == s, degrees - wave_ref[first + s], limit)
    return limit


def turns(wave, b):
    turn = (wave * b) & 3
    cos_b = jnp.where(turn == 0, 1.0, jnp.where(turn == 2, -1.0, 0.0))
    sin_b = jnp.where(turn == 1, 1.0, jnp.where(turn == 3, -1.0, 0.0))
    return cos_b, sin_b


def circle(product, lon_count):
    quarter = lon_count // 4
    count = jnp.floor(product * (1.0 / quarter) + 0.5)
    angle = (product - count * quarter) * (2.0 * math.pi / lon_count)
    turn = count.astype(I32) & 3
    square = angle * angle
    cos = 1.0 + square * (-1 / 2 + square * (1 / 24 + square * (-1 / 720 + square * (1 / 40320))))
    sin = angle * (
        1.0 + square * (-1 / 6 + square * (1 / 120 + square * (-1 / 5040 + square * (1 / 362880))))
    )
    swap = (turn & 1) == 1
    near, far = jnp.where(swap, sin, cos), jnp.where(swap, cos, sin)
    near = jnp.where((turn == 1) | (turn == 2), -near, near)
    far = jnp.where(turn >= 2, -far, far)
    return near, far


def fill_tables(wave_ref, cos_ref, sin_ref, cos_high_ref, sin_high_ref, lons):
    wave = wave_ref[...][None, :].astype(F32)
    shape = (LOW, wave.shape[1])
    cos_low, sin_low = circle(iota(shape, 0).astype(F32) * wave, lons)
    shape = cos_high_ref.shape
    cos_high_ref[...], sin_high_ref[...] = circle((iota(shape, 0) * LOW).astype(F32) * wave, lons)

    @pl.loop(0, cos_ref.shape[0] // LOW)
    def _(i):
        cos_high = cos_high_ref[pl.ds(i, 1), :]
        sin_high = sin_high_ref[pl.ds(i, 1), :]
        at = pl.ds(pl.multiple_of(i * LOW, LOW), LOW)
        cos_ref[at, :] = (cos_high * cos_low - sin_high * sin_low).astype(BF16)
        sin_ref[at, :] = (-(sin_high * cos_low + cos_high * sin_low)).astype(BF16)


def fill_gain(order_ref, exp_ref, traj_ref, gain_ref, norm):
    levels, lats, lons = traj_ref.shape
    width = lons // NBLK
    sub = levels * lats
    row, col = iota((sub, sub), 0), iota((sub, sub), 1)
    held = jnp.zeros((sub, sub), I32)
    for r in range(levels):
        held = jnp.where(col // lats == r, order_ref[0, r], held)
    lat = row // 4 % 2 * 2 + row // 8
    pick = jnp.where((held == row % 4) & (col % lats == lat), 1.0, 0.0).astype(BF16)
    power = jnp.concatenate([exp_ref[r] for r in range(levels)], axis=0).astype(F32)
    scale = matmul(pick, jnp.exp2(power).astype(BF16), 1, 0)
    stored = jnp.concatenate([traj_ref[r] for r in range(levels)], axis=0)
    ordered = matmul(pick, stored, 1, 0)
    full = gain_ref.shape[1]
    ahead = iota((sub, full), 1)
    reverse = jnp.where(iota((full, full), 0) + iota((full, full), 1) == full, 1.0, 0.0).astype(BF16)
    back = [ordered[:, (b + 1) * width - full : (b + 1) * width] for b in range(NBLK)]
    back = matmul(jnp.concatenate(back, axis=0).astype(BF16), reverse, 1, 0)
    for b in range(NBLK):
        start = b * width
        piece = ordered[:, start : start + full] * scale[:, b : b + 1]
        gain = jnp.where(ahead <= width // 2, norm * (1.0 + jnp.tanh(piece)), 0.0)
        gain_ref[b * sub : (b + 1) * sub, :] = gain
        piece = back[b * sub : (b + 1) * sub] * scale[:, b : b + 1]
        gain = norm * (1.0 + jnp.tanh(piece))
        gain = jnp.where((ahead >= 1) & (2 * ahead < width), gain, 0.0)
        at = (NBLK + (b + 1) % NBLK) * sub
        gain_ref[at : at + sub, :] = gain


def synthesis_kernel(
    band_ref, index_ref, wave_ref, held_ref, weight_ref, row_ref, exp_ref, traj_hbm, adj_hbm, leg_hbm,
    out_ref, leg_ref, cos_ref, sin_ref, gain_ref,
    adj_ref, traj_ref, acc_ref, spread_ref, order_ref, cos_high_ref, sin_high_ref,
    adj_sem, leg_sem, traj_sem, *, norm
):
    traj_fetch = pltpu.make_async_copy(traj_hbm, traj_ref, traj_sem)
    traj_fetch.start()
    levels, slots, comps, degrees = adj_ref.shape
    rows = GROUP * comps
    heights = leg_ref.shape[1]
    steps = slots // GROUP
    fetches = []
    for g in range(steps):
        here = pl.ds(g * GROUP, GROUP)
        fetches.append((
            pltpu.make_async_copy(adj_hbm.at[:, here], adj_ref.at[:, here], adj_sem.at[g]),
            pltpu.make_async_copy(leg_hbm.at[here], leg_ref.at[here], leg_sem.at[g]),
        ))
        for fetch in fetches[-1]:
            fetch.start()
    weight = jnp.concatenate([weight_ref[...]] * (128 // heights), axis=1)
    total = slots * comps
    col, source = iota((total, comps * 128), 1), iota((total, comps * 128), 0)
    slot = col % 128
    own = (source == slot * comps + col // 128) & (slot < slots)
    spread_ref[...] = jnp.where(own, 1.0, 0.0).astype(BF16)
    size = 2 * levels * heights
    dest, origin = iota((size, size), 1), iota((size, size), 0)
    band, e, hh, l = dest // 16, dest // 8 % 2, dest // 4 % 2, dest % 4
    order_ref[...] = one_hot((e * levels + l) * heights + band * 2 + hh, origin)
    shape = (2 * levels * rows, GROUP * heights)
    own = (iota(shape, 0) % rows) // comps == iota(shape, 1) // heights
    degree = iota((rows, degrees), 1)
    sign = jnp.where(degree % 2 == 0, 1.0, -1.0).astype(BF16)
    lane = iota((rows, 128), 1) // heights
    fill_tables(row_ref, cos_ref, sin_ref, cos_high_ref, sin_high_ref, traj_ref.shape[2])
    traj_fetch.wait()
    fill_gain(held_ref, exp_ref, traj_ref, gain_ref, norm)
    for first in range(0, steps, CHUNK):
        group = range(first, first + CHUNK)
        for g in group:
            for fetch in fetches[g]:
                fetch.wait()
        wide = []
        for g in group:
            here = pl.ds(g * GROUP, GROUP)
            limit = limits(band_ref, wave_ref, g, slots, comps, degrees)
            inside = jnp.where(degree < limit, 1.0, 0.0).astype(BF16)
            flipped = inside * sign
            values = [adj_ref[l, here].reshape(rows, degrees) for l in range(levels)]
            left = jnp.concatenate(
                [v * inside for v in values] + [v * flipped for v in values], axis=0
            )
            both = matmul(left, leg_ref[here].reshape(GROUP * heights, degrees), 1, 1)
            both = jnp.where(own, both, 0.0)
            both = both[:, :128] + both[:, 128:]
            both = both + pltpu.roll(both, 64, 1)
            both = (both + pltpu.roll(both, 32, 1)) * weight
            blocks = []
            for k in range(2 * levels // 4):
                mix = both[4 * k * rows : (4 * k + 1) * rows]
                for r in range(1, 4):
                    part = both[(4 * k + r) * rows : (4 * k + r + 1) * rows]
                    mix = jnp.where(lane == r, part, mix)
                blocks.append(mix.astype(BF16))
            wide.append(jnp.concatenate(blocks, axis=1))
        acc_ref[first * rows : (first + CHUNK) * rows, :] = jnp.concatenate(wide, axis=0)
    wide = matmul(acc_ref[...], order_ref[...], 1, 0).astype(BF16)
    moved = matmul(wide, spread_ref[...], 0, 0).astype(BF16)
    for d in range(size // 16):
        for c in range(comps):
            out_ref[d, c] = moved[16 * d : 16 * d + 16, 128 * c : 128 * c + slots]


def synthesis(adj, leg, band, index, waves, weight, order, exps, traj, norm):
    levels, slots, comps, degrees = adj.shape
    heights = leg.shape[1]
    lats, lons = traj.shape[1:]
    size = 2 * levels * heights
    count = waves.shape[0]
    high = -(-(lons // NBLK // 2 + 1) // LOW)
    table = jax.ShapeDtypeStruct((high * LOW, count), BF16)
    smem = pl.BlockSpec(memory_space=pltpu.SMEM)
    vmem = pl.BlockSpec(memory_space=pltpu.VMEM)
    hbm = pl.BlockSpec(memory_space=pltpu.HBM)
    return pl.pallas_call(
        functools.partial(synthesis_kernel, norm=norm),
        in_specs=[smem] * 4 + [vmem] * 3 + [hbm] * 3,
        out_specs=[vmem] * 5,
        out_shape=(
            jax.ShapeDtypeStruct((16, comps, 16, slots), BF16),
            jax.ShapeDtypeStruct(leg.shape, BF16),
            table,
            table,
            jax.ShapeDtypeStruct((2 * NBLK * levels * lats, high * LOW), F32),
        ),
        scratch_shapes=[
            pltpu.VMEM(adj.shape, BF16),
            pltpu.VMEM(traj.shape, BF16),
            pltpu.VMEM((slots * comps, size), BF16),
            pltpu.VMEM((slots * comps, comps * 128), BF16),
            pltpu.VMEM((size, size), BF16),
            pltpu.VMEM((-(-high // 8) * 8, count), F32),
            pltpu.VMEM((-(-high // 8) * 8, count), F32),
            pltpu.SemaphoreType.DMA((slots // GROUP,)),
            pltpu.SemaphoreType.DMA((slots // GROUP,)),
            pltpu.SemaphoreType.DMA,
        ],
        compiler_params=pltpu.CompilerParams(vmem_limit_bytes=40_000_000),
        name="synthesis",
    )(band, index, waves, order, weight, waves, exps, traj, adj, leg)


def analysis_kernel(band_ref, wave_ref, in_ref, leg_ref, out_hbm, left_ref, out_ref, out_sem):
    slots, heights, degrees = leg_ref.shape
    levels, _, comps, _ = out_ref.shape
    sources, _, sub, _ = in_ref.shape
    rows = GROUP * comps
    kinds = 2 * levels
    steps = slots // GROUP
    size = sources * sub
    row = iota((size, kinds * 128), 0)
    col = iota((size, kinds * 128), 1)
    row_key = (row // 8 % 2 * levels + row % 4) * heights + row // 16 * 2 + row // 4 % 2
    pick = one_hot(row_key, col // 128 * heights + col % heights)
    parts = []
    for c in range(comps):
        flat = jnp.concatenate([in_ref[d, c] for d in range(sources)], axis=0)
        parts.append(matmul(flat, pick, 0, 0).astype(BF16))
    apart = jnp.concatenate(parts, axis=0)
    total = slots * comps
    weave = one_hot(
        iota((total, total), 0) % comps * slots + iota((total, total), 0) // comps,
        iota((total, total), 1),
    )
    left_ref[...] = matmul(weave, apart, 1, 0).astype(BF16)
    half = levels * rows
    sends = []
    for g in range(steps):
        here = pl.ds(g * GROUP, GROUP)
        own_rows = left_ref[g * rows : (g + 1) * rows, :]
        stack = jnp.concatenate([own_rows[:, 128 * k : 128 * k + 128] for k in range(kinds)], axis=0)
        left = jnp.concatenate([stack, stack], axis=1)
        shape = left.shape
        own = (iota(shape, 0) % rows) // comps == iota(shape, 1) // heights
        left = left * jnp.where(own, 1.0, 0.0).astype(BF16)
        both = matmul(left, leg_ref[here].reshape(GROUP * heights, degrees), 1, 0)
        limit = limits(band_ref, wave_ref, g, slots, comps, degrees)
        degree = iota((rows, degrees), 1)
        inside = degree < limit
        even = degree % 2 == 0
        for l in range(levels):
            sym = both[l * rows : (l + 1) * rows]
            anti = both[half + l * rows : half + (l + 1) * rows]
            value = jnp.where(inside, jnp.where(even, sym, anti), 0.0).astype(BF16)
            out_ref[l, here] = value.reshape(GROUP, comps, degrees)
        sends.append(pltpu.make_async_copy(out_ref.at[:, here], out_hbm.at[:, here], out_sem.at[g]))
        sends[-1].start()
    for send in sends:
        send.wait()


def analysis(sides, leg, band, waves, levels):
    sources, comps, sub, slots = sides.shape
    heights, degrees = leg.shape[1:]
    smem = pl.BlockSpec(memory_space=pltpu.SMEM)
    vmem = pl.BlockSpec(memory_space=pltpu.VMEM)
    hbm = pl.BlockSpec(memory_space=pltpu.HBM)
    shape = (levels, slots, comps, degrees)
    return pl.pallas_call(
        analysis_kernel,
        in_specs=[smem, smem, vmem, vmem],
        out_specs=hbm,
        out_shape=jax.ShapeDtypeStruct(shape, BF16),
        scratch_shapes=[
            pltpu.VMEM((slots * comps, 2 * levels * 128), BF16),
            pltpu.VMEM(shape, BF16),
            pltpu.SemaphoreType.DMA((slots // GROUP,)),
        ],
        compiler_params=pltpu.CompilerParams(vmem_limit_bytes=16 * 2**20),
        name="analysis",
    )(band, waves, sides, leg)


def gather_kernel(in_ref, out_ref, total_ref):
    sources, comps, sub, slots = in_ref.shape
    pick = one_hot(iota((8, comps * sub), 1) // 4, iota((8, comps * sub), 0))
    flat = [jnp.concatenate([in_ref[d, c] for d in range(sources)], axis=1) for c in range(comps)]
    flat = jnp.concatenate(flat, axis=0)
    out_ref[...] = flat
    total_ref[...] = matmul(pick, flat, 1, 0)


def gather_rows(blocks):
    sources, comps, sub, slots = blocks.shape
    vmem = pl.BlockSpec(memory_space=pltpu.VMEM)
    return pl.pallas_call(
        gather_kernel,
        in_specs=[vmem],
        out_specs=[vmem] * 2,
        out_shape=(
            jax.ShapeDtypeStruct((comps * sub, sources * slots), BF16),
            jax.ShapeDtypeStruct((comps * sub // 4, sources * slots), F32),
        ),
        compiler_params=pltpu.CompilerParams(vmem_limit_bytes=8 * 2**20),
        name="gather_rows",
    )(blocks)


def share_kernel(index_ref, total_ref, below_ref, share_ref):
    chip = total_ref[...] + below_ref[...]
    rows, waves = chip.shape
    half = waves // 2
    chip = jnp.where(index_ref[0] % 2 == 0, chip[: rows // 2], chip[rows // 2 :])
    share = jnp.concatenate([chip[:, :half], chip[:, half:]], axis=0).astype(BF16)
    for d in range(share_ref.shape[0]):
        share_ref[d] = share


def share_rows(index, total, below, groups):
    rows, waves = total.shape
    vmem = pl.BlockSpec(memory_space=pltpu.VMEM)
    return pl.pallas_call(
        share_kernel,
        in_specs=[pl.BlockSpec(memory_space=pltpu.SMEM), vmem, vmem],
        out_specs=vmem,
        out_shape=jax.ShapeDtypeStruct((groups, rows, waves // 2), BF16),
        compiler_params=pltpu.CompilerParams(vmem_limit_bytes=8 * 2**20),
        name="share_rows",
    )(index, total, below)


def prior_kernel(index_ref, total_ref, prior_ref):
    prior = jnp.zeros(prior_ref.shape, F32)
    for z in range(total_ref.shape[0]):
        prior = prior + jnp.where(z < index_ref[0] // 2, total_ref[z].astype(F32), 0.0)
    prior_ref[...] = prior


def prior_rows(index, totals):
    vmem = pl.BlockSpec(memory_space=pltpu.VMEM)
    return pl.pallas_call(
        prior_kernel,
        in_specs=[pl.BlockSpec(memory_space=pltpu.SMEM), vmem],
        out_specs=vmem,
        out_shape=jax.ShapeDtypeStruct(totals.shape[1:], F32),
        compiler_params=pltpu.CompilerParams(vmem_limit_bytes=8 * 2**20),
        name="prior_rows",
    )(index, totals)


def forcing_kernel(
    index_ref, coef_ref, mine_ref, other_ref, below_ref, four_ref, wave_ref, gain_ref, cos_ref, sin_ref,
    out_ref, *, norm
):
    me = index_ref[0]
    rows, waves = below_ref.shape
    both = four_ref.shape[0]
    sub = both // 2
    wave = wave_ref[...][None, :]
    mine, other = mine_ref[...], other_ref[...]
    upper = me % 2 == 1
    parts = (jnp.where(upper, other, mine), jnp.where(upper, mine, other))
    parts = [jnp.concatenate([v[: rows // 2], v[rows // 2 :]], axis=1) for v in parts]
    carry = jnp.concatenate(parts, axis=0) + jnp.where(me % 2 == 1, below_ref[...], 0.0)
    four = four_ref[...]
    row, col = iota((both, both), 0), iota((both, both), 1)
    earlier = jnp.where((row // 4 == col // 4) & (col < row), 1.0, 0.0).astype(BF16)
    copies = one_hot(iota((both, rows), 0) // 4, iota((both, rows), 1))
    above = matmul(earlier, four, 1, 0) + matmul(copies, carry.astype(BF16), 1, 0)
    level = iota((both, 1), 0) % 4
    coef = jnp.zeros((both, 1), F32)
    for l in range(4):
        coef = jnp.where(level == l, coef_ref[l], coef)
    mixed = (four.astype(F32) + coef * above).astype(BF16)
    first, second = mixed[:sub], mixed[sub:]
    with_cos, with_sin = [], []
    for b in range(NBLK):
        cos_b, sin_b = (v.astype(BF16) for v in turns(wave, b))
        with_cos.append(first * cos_b - second * sin_b)
        with_sin.append(first * sin_b + second * cos_b)
    with_cos = jnp.concatenate(with_cos, axis=0)
    with_sin = jnp.concatenate(with_sin, axis=0)
    even = matmul(with_cos, cos_ref[...], 1, 1)
    odd = matmul(with_sin, sin_ref[...], 1, 1)
    half = NBLK * sub
    ahead = gain_ref[:half, :] * (even + odd)
    behind = gain_ref[half:, :] * (even - odd)
    forcing = jnp.concatenate([ahead, behind], axis=0).astype(BF16)
    by_cos = matmul(forcing, cos_ref[...], 1, 0)
    by_sin = matmul(forcing, sin_ref[...], 1, 0)
    by_cos = by_cos[:half] + by_cos[half:]
    by_sin = by_sin[:half] - by_sin[half:]
    first = jnp.zeros((sub, waves), F32)
    second = jnp.zeros((sub, waves), F32)
    for b in range(NBLK):
        cos_b, sin_b = turns(wave, b)
        part_cos, part_sin = by_cos[b * sub : (b + 1) * sub], by_sin[b * sub : (b + 1) * sub]
        first = first + part_cos * cos_b + part_sin * sin_b
        second = second + part_sin * cos_b - part_cos * sin_b
    bands, comps, _, slots = out_ref.shape
    half = sub // 2
    for c, value in enumerate((first, second)):
        value = value * norm
        sym, anti = value[:half] + value[half:], value[:half] - value[half:]
        sides = jnp.concatenate([sym, anti], axis=0).astype(BF16)
        for d in range(bands):
            out_ref[d, c] = sides[:, slots * d : slots * (d + 1)]


def forcing_part(index, coef, mine, other, below, four, wave, gain, cos_t, sin_t, shape, norm):
    vmem = pl.BlockSpec(memory_space=pltpu.VMEM)
    smem = pl.BlockSpec(memory_space=pltpu.SMEM)
    return pl.pallas_call(
        functools.partial(forcing_kernel, norm=norm),
        in_specs=[smem] * 2 + [vmem] * 8,
        out_specs=vmem,
        out_shape=jax.ShapeDtypeStruct(shape, BF16),
        compiler_params=pltpu.CompilerParams(vmem_limit_bytes=32 * 2**20),
        cost_estimate=pl.CostEstimate(flops=900_000_000, bytes_accessed=8_000_000, transcendentals=0),
        name="forcing_part",
    )(index, coef, mine, other, below, four, wave, gain, cos_t, sin_t)


def body(adj_spec, wave_of_slot, legendre, lat_weight, traj, traj_exp, traj_order, lev_coef):
    levels, degrees = adj_spec.shape[0], adj_spec.shape[3]
    groups = lax.axis_size("z")
    norm = 1.0 / math.sqrt(degrees)
    band = lax.axis_index("band").astype(I32)[None]
    index = lax.axis_index(("z", "core")).astype(I32)[None]
    adj_spec, table, traj, traj_exp, traj_order, lev_coef, wave_of_slot, weight = (
        pltpu.with_memory_space_constraint(v, pltpu.HBM)
        for v in (
            adj_spec, legendre, traj, traj_exp, traj_order, lev_coef, wave_of_slot, lat_weight[None, :]
        )
    )
    blocks, table, cos_t, sin_t, gain = synthesis(
        adj_spec, table, band, index, wave_of_slot, weight, traj_order, traj_exp, traj, norm
    )
    blocks = lax.all_to_all(blocks, "band", split_axis=0, concat_axis=0, tiled=True)
    four, total = gather_rows(blocks)
    below = lax.ppermute(total, "core", [(0, 1), (1, 0)])
    shares = share_rows(index, total, below, groups)
    totals = lax.all_to_all(shares, "z", split_axis=0, concat_axis=0, tiled=True)
    mine = prior_rows(index, totals)
    other = lax.ppermute(mine, "core", [(0, 1), (1, 0)])
    sides = forcing_part(
        index, lev_coef, mine, other, below, four, wave_of_slot, gain, cos_t, sin_t, blocks.shape, norm
    )
    sides = lax.all_to_all(sides, "band", split_axis=0, concat_axis=0, tiled=True)
    return analysis(sides, table, band, wave_of_slot, levels)


def solution(mesh):
    chips = Mesh(mesh.devices.reshape(mesh.shape["band"], -1, 2), ("band", "z", "core"))
    lev = ("z", "core")
    return jax.shard_map(
        body,
        mesh=chips,
        in_specs=(
            P(lev, "band", None, None),
            P(),
            P("band", None, None),
            P(),
            P(lev, "band", None),
            P(lev, "band", None),
            P(lev, None),
            P(lev),
        ),
        out_specs=P(lev, "band", None, None),
        check_vma=False,
    )
```
